32 devices in a mesh: pages: 8 (over y, x, core), seq: 4 (over z).
Axes of the slice: x: 2, y: 2, z: 4, core: 2. Of those that a mesh axis runs over, the one named last changes fastest.
Arguments:
- tokens: bfloat16 [32, 576, 768], P('pages', 'seq'), may hold values from -6 to 6
- cotangent: bfloat16 [32, 576, 768], P('pages', 'seq'), may hold values from -6 to 6
- conv_text: float32 [3, 3, 768], replicated, may hold values from -4 to 4
- conv_patch: float32 [3, 3, 768], replicated, may hold values from -4 to 4
- proj_query: bfloat16 [768, 768], replicated, may hold values from -0.21875 to 0.21875
- bias_query: float32 [768], replicated, may hold values from -4 to 4
- proj_key: bfloat16 [768, 768], replicated, may hold values from -0.21875 to 0.21875
- proj_value: bfloat16 [768, 768], replicated, may hold values from -0.21875 to 0.21875
- bias_value: float32 [768], replicated, may hold values from -0.4375 to 0.4375
- proj_output: bfloat16 [768, 768], replicated, may hold values from -3 to 3
- bias_output: float32 [768], replicated, may hold values from -4 to 4
- rel_order: float32 [12, 33], replicated, may hold values from -6 to 6
- rel_horiz: float32 [12, 33], replicated, may hold values from -6 to 6
- rel_vert: float32 [12, 33], replicated, may hold values from -6 to 6
- norm_gain: float32 [768], replicated, may hold values from 0.5 to 1.5
- norm_shift: float32 [768], replicated, may hold values from -4 to 4
- expand_weight: bfloat16 [768, 3072], replicated, may hold values from -0.21875 to 0.21875
- expand_bias: float32 [3072], replicated, may hold values from -4 to 4
- reduce_weight: bfloat16 [3072, 768], replicated, may hold values from -0.109375 to 0.109375
- reduce_bias: float32 [768], replicated, may hold values from -4 to 4
- final_gain: float32 [768], replicated, may hold values from 0.5 to 1.5
- final_shift: float32 [768], replicated, may hold values from -4 to 4
- text_count: int32 [32], P('pages'), may hold values from 128 to 512, as said below
- box_left: int32 [32, 576], P('pages'), may hold values from 0 to 63
- box_top: int32 [32, 576], P('pages'), may hold values from 0 to 63
Outputs:
- mixed_out: bfloat16 [32, 576, 768], P('pages', 'seq')
- grad_tokens: float32 [32, 576, 768], P('pages', 'seq')
- grad_conv_text: float32 [3, 3, 768], replicated
- grad_conv_patch: float32 [3, 3, 768], replicated
- grad_query: float32 [768, 768], P('pages')
- grad_bias_query: float32 [768], replicated
- grad_key: float32 [768, 768], P('pages')
- grad_value: float32 [768, 768], P('pages')
- grad_bias_value: float32 [768], replicated
- grad_output: float32 [768, 768], P('pages')
- grad_bias_output: float32 [768], replicated
- grad_order: float32 [12, 33], replicated
- grad_horiz: float32 [12, 33], replicated
- grad_vert: float32 [12, 33], replicated
- grad_norm_gain: float32 [768], replicated
- grad_norm_shift: float32 [768], replicated
- grad_expand: float32 [768, 3072], P('pages')
- grad_expand_bias: float32 [3072], replicated
- grad_reduce: float32 [3072, 768], P('pages')
- grad_reduce_bias: float32 [768], replicated
- grad_final_gain: float32 [768], replicated
- grad_final_shift: float32 [768], replicated
The draws below stay inside these ranges and needn't reach their ends.
Inputs may be any that keep to these rules, and one draw needn't show every extreme that they name: Text rows 0 .. text_count - 1 of a page are valid, the rest of its 512 text rows are masked; some page has every text row valid and some has 128.
All inputs are finite; a program needn't handle non-finite values.
Results may differ from the reference program's by a relative error of at most 0.017.
The reference program's roundings to bfloat16 on the way count: a program that leaves them out, or rounds other values in their place, can miss the bound.
Values may be sent and summed in bfloat16 or wider, within the bound.
No kernel may reach another device: no remote copies, remote signals or barrier semaphores. Data moves between devices by JAX's collectives and lax.ppermute only.
A program may use at most 256 MiB of HBM per device.

```python
import jax
import jax.numpy as jnp
from jax import lax

D = 768
HEADS = 12
HEAD = 64
FF = 3072
TEXT = 512
GRID = 7
SPAN = 16
PG_DEV = 4
PATCHES = 49
L = 576
NB = 33
PAGES = 32


def draw_text_count(key, part):
    counts = jax.random.randint(key, (PAGES,), TEXT // 4, TEXT + 1)
    counts = counts.at[0].set(TEXT).at[1].set(TEXT // 4)
    return counts.astype(jnp.int32)


def plant(entries, own_key, least, high):
    spot = [jax.random.randint(jax.random.fold_in(own_key, axis), (), 0, length) for axis, length in enumerate(entries.shape)]
    widest = entries.shape.index(max(entries.shape))
    beside = spot[:widest] + [(spot[widest] + 1) % entries.shape[widest]] + spot[widest + 1:]
    return entries.at[tuple(spot)].set(least).at[tuple(beside)].set(high)


def block_levels(stream_key, shape, split, low, largest):
    def one(dim, blocks):
        draws = jax.random.uniform(jax.random.fold_in(jax.random.fold_in(stream_key, 6), dim), (blocks,), jnp.float32, low / len(split), largest / len(split))
        return jnp.repeat(jnp.exp(draws), shape[dim] // blocks).reshape((-1,) + (1,) * (len(shape) - dim - 1))

    loudness = one(*split[0])
    for cut in split[1:]:
        loudness = loudness * one(*cut)
    return loudness


def gaussian(own_key, extent, spread, bound, split=(), kind=jnp.bfloat16):
    factor_of = block_levels(own_key, extent, split, -0.22, 0.18) if split else 1.0
    values = jax.random.normal(own_key, extent, jnp.float32) * spread * factor_of
    return jnp.minimum(jnp.maximum(values, -bound), bound).astype(kind)


def setup_inputs(seed: int = 0) -> dict:
    splits = jax.random.split(jax.random.key(seed), 26)
    tokens = gaussian(splits[0], (PAGES, L, D), 1.0, 6.0, ((0, 8), (1, 4)))
    cotangent = gaussian(splits[1], (PAGES, L, D), 1.0, 6.0, ((0, 8), (1, 4)))
    conv_text = gaussian(splits[2], (3, 3, D), 0.3, 4.0, (), jnp.float32)
    conv_patch = gaussian(splits[3], (3, 3, D), 0.3, 4.0, (), jnp.float32)
    proj_query = gaussian(splits[4], (D, D), D ** -0.5, 0.21875)
    bias_query = gaussian(splits[5], (D,), 0.3, 4.0, (), jnp.float32)
    proj_key = gaussian(splits[6], (D, D), D ** -0.5, 0.21875)
    proj_value = gaussian(splits[7], (D, D), D ** -0.5, 0.21875)
    bias_value = gaussian(splits[8], (D,), 0.03, 0.4375, (), jnp.float32)
    proj_output = gaussian(splits[9], (D, D), 4 ** -0.5, 3.0)
    bias_output = gaussian(splits[10], (D,), 0.3, 4.0, (), jnp.float32)
    rel_order = gaussian(splits[11], (HEADS, NB), 0.5, 6.0, (), jnp.float32)
    rel_horiz = gaussian(splits[12], (HEADS, NB), 0.5, 6.0, (), jnp.float32)
    rel_vert = gaussian(splits[13], (HEADS, NB), 0.5, 6.0, (), jnp.float32)
    norm_gain = jnp.clip(1.0 + 0.1 * jax.random.normal(splits[14], (D,), jnp.float32), 0.5, 1.5)
    norm_shift = gaussian(splits[15], (D,), 0.3, 4.0, (), jnp.float32)
    expand_weight = gaussian(splits[16], (D, FF), D ** -0.5, 0.21875)
    expand_bias = gaussian(splits[17], (FF,), 0.3, 4.0, (), jnp.float32)
    reduce_weight = gaussian(splits[18], (FF, D), FF ** -0.5, 0.109375)
    reduce_bias = gaussian(splits[19], (D,), 0.3, 4.0, (), jnp.float32)
    final_gain = jnp.clip(1.0 + 0.1 * jax.random.normal(splits[20], (D,), jnp.float32), 0.5, 1.5)
    final_shift = gaussian(splits[21], (D,), 0.3, 4.0, (), jnp.float32)
    text_count = draw_text_count(jax.random.fold_in(splits[25], 71), 0)
    box_left = plant(jax.random.randint(splits[23], (PAGES, L), 0, 4 * SPAN), jax.random.fold_in(splits[23], 1), 0, (4 * SPAN) - 1).astype(jnp.int32)
    box_top = plant(jax.random.randint(splits[24], (PAGES, L), 0, 4 * SPAN), jax.random.fold_in(splits[24], 1), 0, (4 * SPAN) - 1).astype(jnp.int32)
    return dict(tokens=tokens, cotangent=cotangent, conv_text=conv_text, conv_patch=conv_patch, proj_query=proj_query, bias_query=bias_query, proj_key=proj_key, proj_value=proj_value, bias_value=bias_value, proj_output=proj_output, bias_output=bias_output, rel_order=rel_order, rel_horiz=rel_horiz, rel_vert=rel_vert, norm_gain=norm_gain, norm_shift=norm_shift, expand_weight=expand_weight, expand_bias=expand_bias, reduce_weight=reduce_weight, reduce_bias=reduce_bias, final_gain=final_gain, final_shift=final_shift, text_count=text_count, box_left=box_left, box_top=box_top)


EPS = 1e-06
SCALE = 0.125
NEG = -1e+30

@jax.custom_vjp
def low(v):
    return lax.optimization_barrier(v.astype(jnp.bfloat16)).astype(jnp.float32)

@jax.custom_vjp
def low_back(v):
    return v

def low_keep(v):
    return (low(v), None)

def low_pass(kept, grad):
    return (grad,)

def back_keep(v):
    return (v, None)

def back_low(kept, grad):
    return (low(grad),)
low.defvjp(low_keep, low_pass)
low_back.defvjp(back_keep, back_low)

def mult(left_side, right_side):
    return jnp.dot(left_side, right_side, precision=lax.Precision.HIGHEST)

def layer_norm(inputs, gain_vec, shift_vec):
    average = lax.optimization_barrier(jnp.mean(inputs, axis=-1, keepdims=True))
    centred = inputs - average
    variance = lax.optimization_barrier(jnp.mean(centred * centred, axis=-1, keepdims=True))
    return centred * lax.rsqrt(variance + EPS) * gain_vec + shift_vec

def gelu_exact(inputs):
    return jax.nn.gelu(inputs, approximate=False)

def softmax_rows(scores):
    row_max = lax.optimization_barrier(jnp.max(scores, axis=-1, keepdims=True))
    expo_terms = jnp.exp(scores - row_max)
    return expo_terms / lax.optimization_barrier(jnp.sum(expo_terms, axis=-1, keepdims=True))

def bucket_of(first_pos, second_pos):
    return jnp.clip(second_pos[None, :] - first_pos[:, None], -SPAN, SPAN) + SPAN

def page_forward(page_rows, count, left_pos, top_pos, weights):
    conv_text, conv_patch, proj_query, bias_query, proj_key, proj_value, bias_value, proj_output, bias_output, rel_order, rel_horiz, rel_vert, norm_gain, norm_shift, expand_weight, expand_bias, reduce_weight, reduce_bias, final_gain, final_shift = weights
    length = page_rows.shape[0]
    model_width = page_rows.shape[1]
    positions = jnp.arange(length, dtype=jnp.int32)
    text_keep = (positions < count).astype(jnp.float32)[:, None]
    patch_mask = (positions >= TEXT) & (positions < TEXT + PATCHES)
    key_ok = (positions < count) | patch_mask
    padded = jnp.pad(page_rows * text_keep, ((3, 3), (0, 0)))
    text_term = jnp.zeros((length, model_width), jnp.float32)
    for dilation in range(1, 4):
        for tap_index in range(3):
            offset = (tap_index - 1) * dilation
            text_term = text_term + conv_text[dilation - 1, tap_index] * padded[3 + offset:3 + offset + length]
    grid_rows = jnp.pad(page_rows[TEXT:TEXT + PATCHES].reshape(GRID, GRID, model_width), ((1, 1), (1, 1), (0, 0)))
    patch_term = jnp.zeros((GRID, GRID, model_width), jnp.float32)
    for across in range(3):
        for down_index in range(3):
            patch_term = patch_term + conv_patch[across, down_index] * grid_rows[across:across + GRID, down_index:down_index + GRID]
    patch_full = jnp.concatenate([jnp.zeros((TEXT, model_width), jnp.float32), patch_term.reshape(PATCHES, model_width), jnp.zeros((length - TEXT - PATCHES, model_width), jnp.float32)], axis=0)
    settled = page_rows + text_keep * text_term + patch_full
    entry_low = low(settled)
    query_heads = low_back(low(mult(entry_low, proj_query) + bias_query)).reshape(length, HEADS, HEAD)
    key_heads = low_back(low(mult(entry_low, proj_key))).reshape(length, HEADS, HEAD)
    value_heads = low_back(low(mult(entry_low, proj_value) + bias_value)).reshape(length, HEADS, HEAD)
    raw_scores = jnp.einsum('ihd,jhd->hij', query_heads, key_heads, precision=lax.Precision.HIGHEST) * SCALE
    rel_terms = rel_order[:, bucket_of(positions, positions)] + rel_horiz[:, bucket_of(left_pos, left_pos)] + rel_vert[:, bucket_of(top_pos, top_pos)]
    scores = low_back(jnp.where(key_ok[None, None, :], raw_scores + rel_terms, NEG))
    probs_low = low(softmax_rows(scores))
    heads_out = jnp.einsum('hij,jhd->ihd', probs_low, value_heads, precision=lax.Precision.HIGHEST)
    attended = low_back(low(heads_out.reshape(length, model_width)))
    branch = low_back(mult(attended, proj_output) + bias_output)
    first_norm = layer_norm(settled + branch, norm_gain, norm_shift)
    expanded = low_back(mult(low(first_norm), expand_weight) + expand_bias)
    activated = low(gelu_exact(expanded))
    reduced = low_back(mult(activated, reduce_weight) + reduce_bias)
    return layer_norm(first_norm + reduced, final_gain, final_shift)

def reference(tokens, cotangent, conv_text, conv_patch, proj_query, bias_query, proj_key, proj_value, bias_value, proj_output, bias_output, rel_order, rel_horiz, rel_vert, norm_gain, norm_shift, expand_weight, expand_bias, reduce_weight, reduce_bias, final_gain, final_shift, text_count, box_left, box_top):
    weights = (conv_text.astype(jnp.float32), conv_patch.astype(jnp.float32), proj_query.astype(jnp.float32), bias_query.astype(jnp.float32), proj_key.astype(jnp.float32), proj_value.astype(jnp.float32), bias_value.astype(jnp.float32), proj_output.astype(jnp.float32), bias_output.astype(jnp.float32), rel_order.astype(jnp.float32), rel_horiz.astype(jnp.float32), rel_vert.astype(jnp.float32), norm_gain.astype(jnp.float32), norm_shift.astype(jnp.float32), expand_weight.astype(jnp.float32), expand_bias.astype(jnp.float32), reduce_weight.astype(jnp.float32), reduce_bias.astype(jnp.float32), final_gain.astype(jnp.float32), final_shift.astype(jnp.float32))
    groups = tokens.shape[0] // PG_DEV
    counts = text_count.reshape(groups, PG_DEV)
    left_rows = box_left.reshape(groups, PG_DEV, L)
    top_rows = box_top.reshape(groups, PG_DEV, L)

    def group_forward(page_items, weight_set):
        rows_in, count_in, left_in, top_in = page_items
        return jax.vmap(page_forward, in_axes=(0, 0, 0, 0, None))(rows_in, count_in, left_in, top_in, weight_set)
    checked = jax.checkpoint(group_forward)

    def forward(rows_all, weight_set):
        shaped = rows_all.reshape(groups, PG_DEV, L, D)
        result = lax.map(lambda page_items: checked(page_items, weight_set), (shaped, counts, left_rows, top_rows))
        return result.reshape(rows_all.shape)
    mixed_out, pull_back = jax.vjp(forward, tokens.astype(jnp.float32), weights)
    grad_tokens, grads = pull_back(cotangent.astype(jnp.float32))
    return (mixed_out.astype(jnp.bfloat16), grad_tokens, grads[0], grads[1], grads[2], grads[3], grads[4], grads[5], grads[6], grads[7], grads[8], grads[9], grads[10], grads[11], grads[12], grads[13], grads[14], grads[15], grads[16], grads[17], grads[18], grads[19])
```

```python
import jax
import jax.numpy as jnp
from jax import lax
from jax.experimental import pallas as pl
from jax.experimental.pallas import tpu as pltpu
from jax.sharding import PartitionSpec as P

BF = jnp.bfloat16
F32 = jnp.float32
TEXT = 512
GRID = 7
SPAN = 16
EPS = 1e-06
SCALE = 0.125
NEG = -1e30
RT = 64
BOX = 64


def order_offsets():
    return (-128,-64,0,64)

def table_prep(rel_order, rel_horiz, rel_vert):
    heads, nb = rel_order.shape
    a=jnp.arange(64)[:,None]; c=jnp.arange(64)[None,:]
    b=jnp.clip(c-a,-SPAN,SPAN)+SPAN
    oh=(b.reshape(-1)[None,:]==jnp.arange(nb)[:,None]).astype(F32)
    th=jnp.dot(rel_horiz,oh,precision=lax.Precision.HIGHEST).reshape(heads,64,64)
    tv=jnp.dot(rel_vert,oh,precision=lax.Precision.HIGHEST).reshape(heads,64,64)
    z=jnp.zeros_like(th)
    def hl(x):
        hi=lax.reduce_precision(x,8,7)
        return hi, x-hi
    hh,hlo=hl(th); vh,vlo=hl(tv)
    top=jnp.concatenate([hh,z,hlo,z],2); bot=jnp.concatenate([z,vh,z,vlo],2)
    wt=jnp.concatenate([top,bot],1).astype(BF)
    i=jnp.arange(RT)[:,None]; j=jnp.arange(128)[None,:]
    ob=jnp.stack([jnp.clip(d+j-i,-SPAN,SPAN)+SPAN for d in order_offsets()])
    ohd=(ob.reshape(-1)[None,:]==jnp.arange(nb)[:,None]).astype(F32)
    od=jnp.dot(rel_order,ohd,precision=lax.Precision.HIGHEST).reshape(heads,4,RT,128)
    return wt, od

def fwd_kernel(edge_ref,q_ref,k_ref,v_ref,oh_ref,wt_ref,ord_ref,mask_ref,p_ref,o_ref,qa_ref,ka_ref,s_ref):
    g=pl.program_id(0)
    L=q_ref.shape[0]
    @pl.when(g==0)
    def _():
        ka_ref[:,128:256]=oh_ref[...]
        ka_ref[:,256:384]=oh_ref[...]
    ka_ref[:,0:128]=k_ref[...]
    lane=lax.broadcasted_iota(jnp.int32,(L,128),1)
    for e in range(2):
        keep=(lane<64) if e==0 else (lane>=64)
        qa_ref[e,:,0:128]=jnp.where(keep,q_ref[...],jnp.zeros((),BF))
        qa_ref[e,:,128:384]=jnp.dot(oh_ref[...],wt_ref[e],preferred_element_type=F32).astype(BF)
        s_ref[e]=lax.dot_general(qa_ref[e],ka_ref[...],(((1,),(1,)),((),())),preferred_element_type=F32)
    outs=[]
    nj=(L+127)//128
    for e in range(2):
        h=2*g+e
        left=edge_ref[h,0]; right=edge_ref[h,1]
        for a in range(L//RT):
            r0=a*RT
            cols=[]
            for b in range(nj):
                w=min(128,L-128*b); d=128*b-RT*a
                t=s_ref[e,r0:r0+RT,128*b:128*b+w]+mask_ref[:,128*b:128*b+w]
                if d in order_offsets():
                    t=t+ord_ref[e,order_offsets().index(d)][:,:w]
                elif d<0: t=t+left
                else: t=t+right
                cols.append(t)
            t=jnp.concatenate(cols,1)
            m=jnp.max(t,axis=1,keepdims=True)
            ex=jnp.exp(t-m)
            tot=jnp.sum(ex,axis=1,keepdims=True)
            p_ref[e,r0:r0+RT,:]=(ex*(1.0/tot)).astype(BF)
        outs.append(jnp.dot(p_ref[e],v_ref[...],preferred_element_type=F32))
    o_ref[...]=jnp.where(lane<64,outs[0],outs[1]).astype(BF)

def attn_fwd(q,k,v,oh,wt,od,edge,mask):
    L,D=q.shape; H=wt.shape[0]
    col=pl.BlockSpec((L,128),lambda g,*_:(0,g))
    full=lambda shp: pl.BlockSpec(shp,lambda g,*_:(0,)*len(shp))
    return pl.pallas_call(fwd_kernel,
        out_shape=(jax.ShapeDtypeStruct((H,L,L),BF),jax.ShapeDtypeStruct((L,D),BF)),
        grid_spec=pltpu.PrefetchScalarGridSpec(num_scalar_prefetch=1,grid=(H//2,),
            in_specs=[col,col,col,full((L,128)),pl.BlockSpec((2,128,256),lambda g,*_:(g,0,0)),
                      pl.BlockSpec((2,4,RT,128),lambda g,*_:(g,0,0,0)),full((1,L))],
            out_specs=[pl.BlockSpec((2,L,L),lambda g,*_:(g,0,0)),col],
            scratch_shapes=[pltpu.VMEM((2,L,384),BF),pltpu.VMEM((L,384),BF),pltpu.VMEM((2,L,L),F32)]),
        name="attn_fwd",
    )(edge,q,k,v,oh,wt,od,mask)

def bwd_kernel(p_ref,q_ref,k_ref,v_ref,do_ref,o_ref,oh_ref,oht_ref,
               dq_ref,dk_ref,dv_ref,hist_ref,ord_ref,va_ref,rhs_ref,ds_ref,dp_ref):
    g=pl.program_id(0)
    L=q_ref.shape[0]
    lane=lax.broadcasted_iota(jnp.int32,(L,128),1)
    @pl.when(g==0)
    def _():
        va_ref[:,128:256]=jnp.where(lane<2,1.0,0.0).astype(BF)
        rhs_ref[:,128:256]=oh_ref[...]
    va_ref[:,0:128]=v_ref[...]
    rhs_ref[:,0:128]=k_ref[...]
    nj=(L+127)//128
    do=do_ref[...]
    prod=do.astype(F32)*o_ref[...].astype(F32)
    res=[]
    for e in range(2):
        keep=(lane<64) if e==0 else (lane>=64)
        inner=-jnp.sum(jnp.where(keep,prod,0.0),axis=1,keepdims=True)
        hi=inner.astype(BF); lo=(inner-hi.astype(F32)).astype(BF)
        ext=jnp.where(lane==0,jnp.broadcast_to(hi.astype(F32),(L,128)),jnp.where(lane==1,jnp.broadcast_to(lo.astype(F32),(L,128)),0.0)).astype(BF)
        da=jnp.concatenate([jnp.where(keep,do,jnp.zeros((),BF)),ext],1)
        dp_ref[e]=lax.dot_general(da,va_ref[...],(((1,),(1,)),((),())),preferred_element_type=F32)
    for e in range(2):
        accs={}
        for a in range(L//RT):
            r0=a*RT
            pf=p_ref[e,r0:r0+RT,:].astype(F32)
            ds=pf*dp_ref[e,r0:r0+RT,:]
            ds_ref[e,r0:r0+RT,:]=ds.astype(BF)
            for b in range(nj):
                w=min(128,L-128*b); d=128*b-RT*a
                t=ds[:,128*b:128*b+w]
                if w<128: t=jnp.concatenate([t,jnp.zeros((RT,128-w),F32)],1)
                key=order_offsets().index(d) if d in order_offsets() else (4 if d<0 else 5)
                accs[key]=t if key not in accs else accs[key]+t
        for key in range(6):
            ord_ref[e,key]=accs[key]
        r=jnp.dot(ds_ref[e],rhs_ref[...],preferred_element_type=F32)
        gg=r[:,128:256]
        ghi=gg.astype(BF); glo=(gg-ghi.astype(F32)).astype(BF)
        hh=jnp.dot(oht_ref[...],jnp.concatenate([ghi,glo],1),preferred_element_type=F32)
        hist_ref[e]=hh[:,0:128]+hh[:,128:256]
        dk=lax.dot_general(ds_ref[e],q_ref[...],(((0,),(0,)),((),())),preferred_element_type=F32)
        dv=lax.dot_general(p_ref[e],do,(((0,),(0,)),((),())),preferred_element_type=F32)
        res.append((r[:,0:128],dk,dv))
    first=lane<64
    dq_ref[...]=(jnp.where(first,res[0][0],res[1][0])*0.125).astype(BF)
    dk_ref[...]=jnp.where(first,res[0][1],res[1][1]).astype(BF)
    dv_ref[...]=jnp.where(first,res[0][2],res[1][2]).astype(BF)

def attn_bwd(p,q,k,v,do,o,oh,oht):
    L,D=q.shape; H=p.shape[0]
    col=pl.BlockSpec((L,128),lambda g:(0,g))
    full=lambda shp: pl.BlockSpec(shp,lambda g:(0,)*len(shp))
    return pl.pallas_call(bwd_kernel,
        out_shape=(jax.ShapeDtypeStruct((L,D),BF),)*3+(jax.ShapeDtypeStruct((H,128,128),F32),jax.ShapeDtypeStruct((H,6,RT,128),F32)),
        grid=(H//2,),
        in_specs=[pl.BlockSpec((2,L,L),lambda g:(g,0,0)),col,col,col,col,col,full((L,128)),full((128,L))],
        out_specs=[col,col,col,pl.BlockSpec((2,128,128),lambda g:(g,0,0)),pl.BlockSpec((2,6,RT,128),lambda g:(g,0,0,0))],
        scratch_shapes=[pltpu.VMEM((L,256),BF),pltpu.VMEM((L,256),BF),pltpu.VMEM((2,L,L),BF),pltpu.VMEM((2,L,L),F32)],
        name="attn_bwd",
    )(p,q,k,v,do,o,oh,oht)


def xor_pairs(n, bit):
    return [(i, i ^ bit) for i in range(n)]


def swap(value, axis, bit):
    return lax.ppermute(value, axis, xor_pairs(lax.axis_size(axis), bit))


def page_in(blocks):
    n = lax.axis_size("seq")
    place = lax.axis_index("seq")
    got = [lax.dynamic_index_in_dim(blocks, place, 0, keepdims=True)]
    for d in range(1, n):
        part = lax.dynamic_index_in_dim(blocks, lax.rem(place + d, n), 0, keepdims=True)
        got.append(lax.ppermute(part, "seq", [(i, (i + d) % n) for i in range(n)]))
    ring = jnp.concatenate(got[::-1] * 2, axis=0)
    return lax.dynamic_slice_in_dim(ring, n - 1 - place, n, 0)


def halve(value, ids, bit):
    pos = [i for i, x in enumerate(ids) if not x & bit]
    kept = [x for x in ids if not x & bit]
    low = jnp.concatenate([value[i : i + 1] for i in pos], 0) if len(pos) > 1 else value[pos[0] : pos[0] + 1]
    pos1 = [i for i, x in enumerate(ids) if x & bit]
    high = jnp.concatenate([value[i : i + 1] for i in pos1], 0) if len(pos1) > 1 else value[pos1[0] : pos1[0] + 1]
    mine = (lax.axis_index("pages") & bit) != 0
    keep = jnp.where(mine, high, low)
    send = jnp.where(mine, low, high)
    got = swap(send, "pages", bit)
    return (keep.astype(F32) + got.astype(F32)).astype(BF), kept


def scatter_pages(value):
    n = value.shape[0]
    bits = []
    b = 1
    while b < n:
        bits.append(b)
        b *= 2
    ids = list(range(n))
    value, ids = halve(value, ids, bits[0])
    half = value.shape[2] // 2
    parts = []
    for order, piece in ((bits[1:], value[:, :, :half]), (bits[1:][::-1], value[:, :, half:])):
        left = ids
        for bit in order:
            piece, left = halve(piece, left, bit)
        parts.append(piece)
    return jnp.concatenate(parts, 2)[0]


def sum_seq(value):
    n = lax.axis_size("seq")
    place = lax.axis_index("seq")
    rows, cols = value.shape
    quarters = value.reshape(n, rows // n, cols)
    total = lax.dynamic_index_in_dim(quarters, place, 0, keepdims=False).astype(F32)
    for d in range(1, n):
        part = lax.dynamic_index_in_dim(quarters, lax.rem(place + d, n), 0, keepdims=False)
        total = total + lax.ppermute(part, "seq", [(i, (i + d) % n) for i in range(n)]).astype(F32)
    total = total.astype(BF)[None]
    got = [total] + [lax.ppermute(total, "seq", [(i, (i + d) % n) for i in range(n)]) for d in range(1, n)]
    ring = jnp.concatenate(got[::-1] * 2, axis=0)
    return lax.dynamic_slice_in_dim(ring, n - 1 - place, n, 0).reshape(rows, cols)


def sum_all(value):
    b = 1
    while b < lax.axis_size("pages"):
        value = value + swap(value, "pages", b)
        b *= 2
    b = 1
    while b < lax.axis_size("seq"):
        value = value + swap(value, "seq", b)
        b *= 2
    return value


def layer_norm(inputs, gain_vec, shift_vec):
    average = jnp.mean(inputs, axis=-1, keepdims=True)
    centred = inputs - average
    variance = jnp.mean(centred * centred, axis=-1, keepdims=True)
    return centred * lax.rsqrt(variance + EPS) * gain_vec + shift_vec


def gelu_exact(inputs):
    return jax.nn.gelu(inputs, approximate=False)


def shifted(value, offset):
    rows = value.shape[0]
    if offset == 0:
        return value
    zeros = jnp.zeros((abs(offset),) + value.shape[1:], value.dtype)
    if offset > 0:
        return jnp.concatenate([value[offset:], zeros], 0)
    return jnp.concatenate([zeros, value[: rows + offset]], 0)


def patch_conv(patch_rows, conv_patch):
    side = patch_rows.shape[0]
    grid_pad = jnp.pad(patch_rows, ((1, 1), (1, 1), (0, 0)))
    running = jnp.zeros_like(patch_rows)
    for across in range(3):
        for down_index in range(3):
            running = running + conv_patch[across, down_index] * grid_pad[across : across + side, down_index : down_index + side]
    return running


def per_device(
    tokens, cotangent, conv_text, conv_patch, proj_query, bias_query, proj_key, proj_value, bias_value,
    proj_output, bias_output, rel_order, rel_horiz, rel_vert, norm_gain, norm_shift, expand_weight,
    expand_bias, reduce_weight, reduce_bias, final_gain, final_shift, text_count, box_left, box_top,
):
    pages_here, stretch, width = tokens.shape
    n_seq = lax.axis_size("seq")
    n_pages = lax.axis_size("pages")
    place = lax.axis_index("seq")
    length = stretch * n_seq
    heads = rel_order.shape[0]
    patches = GRID * GRID
    pick = lambda a: lax.dynamic_index_in_dim(a, place, 0, keepdims=False)
    count, left, top = pick(text_count), pick(box_left), pick(box_top)
    pos = jnp.arange(length, dtype=jnp.int32)
    keep = (pos < count).astype(F32)[:, None]
    key_ok = (pos < count) | ((pos >= TEXT) & (pos < TEXT + patches))
    mask = jnp.where(key_ok, 0.0, NEG).astype(F32)[None]
    cells = jnp.arange(BOX, dtype=jnp.int32)
    oh = jnp.concatenate([left[:, None] == cells[None], top[:, None] == cells[None]], 1).astype(BF)
    oht = jnp.concatenate([left[None] == cells[:, None], top[None] == cells[:, None]], 0).astype(BF)
    edge = jnp.stack([rel_order[:, 0], rel_order[:, -1]], 1)
    wt, od = table_prep(rel_order, rel_horiz, rel_vert)

    page = page_in(tokens).reshape(length, width).astype(F32)
    d_out = page_in(cotangent).reshape(length, width).astype(F32)

    masked = page * keep
    text_term = jnp.zeros_like(page)
    for s in range(1, 4):
        for t in range(3):
            text_term = text_term + conv_text[s - 1, t] * shifted(masked, (t - 1) * s)
    patch_rows = page[TEXT : TEXT + patches].reshape(GRID, GRID, width)
    patch_term = patch_conv(patch_rows, conv_patch).reshape(patches, width)
    above = jnp.zeros((TEXT, width), F32)
    below = jnp.zeros((length - TEXT - patches, width), F32)
    settled = page + keep * text_term + jnp.concatenate([above, patch_term, below], 0)
    entry = settled.astype(BF)
    query = (jnp.dot(entry, proj_query, preferred_element_type=F32) + bias_query).astype(BF)
    key = jnp.dot(entry, proj_key, preferred_element_type=F32).astype(BF)
    value = (jnp.dot(entry, proj_value, preferred_element_type=F32) + bias_value).astype(BF)
    query = query * jnp.asarray(SCALE, BF)
    probs, attended = attn_fwd(query, key, value, oh, wt, od, edge, mask)
    branch = jnp.dot(attended, proj_output, preferred_element_type=F32) + bias_output
    first_norm, norm_pull = jax.vjp(layer_norm, settled + branch, norm_gain, norm_shift)
    first_low = first_norm.astype(BF)
    expanded = jnp.dot(first_low, expand_weight, preferred_element_type=F32) + expand_bias
    activated_float, gelu_pull = jax.vjp(gelu_exact, expanded)
    activated = activated_float.astype(BF)
    reduced = jnp.dot(activated, reduce_weight, preferred_element_type=F32) + reduce_bias
    mixed_float, final_pull = jax.vjp(layer_norm, first_norm + reduced, final_gain, final_shift)
    mixed_out = page_in(mixed_float.astype(BF).reshape(n_seq, stretch, width))
    d_second, g_final_gain, g_final_shift = final_pull(d_out)
    d_reduced = d_second.astype(BF)
    g_reduce_bias = jnp.sum(d_reduced, axis=0, dtype=F32)
    g_reduce = jnp.einsum("rf,rd->fd", activated, d_reduced, preferred_element_type=F32).astype(BF)
    d_activated = jnp.einsum("rd,fd->rf", d_reduced, reduce_weight, preferred_element_type=F32)
    d_expanded = gelu_pull(d_activated)[0].astype(BF)
    g_expand_bias = jnp.sum(d_expanded, axis=0, dtype=F32)
    g_expand = jnp.einsum("rd,rf->df", first_low, d_expanded, preferred_element_type=F32).astype(BF)
    d_first = d_second + jnp.einsum("rf,df->rd", d_expanded, expand_weight, preferred_element_type=F32)
    d_first_in, g_norm_gain, g_norm_shift = norm_pull(d_first)
    d_branch = d_first_in.astype(BF)
    g_output_bias = jnp.sum(d_branch, axis=0, dtype=F32)
    g_output = jnp.einsum("re,rd->ed", attended, d_branch, preferred_element_type=F32).astype(BF)
    d_attended = jnp.einsum("rd,ed->re", d_branch, proj_output, preferred_element_type=F32).astype(BF)

    d_query, d_key, d_value, hist, ords = attn_bwd(probs, query, key, value, d_attended, attended, oh, oht)

    g_query_bias = jnp.sum(d_query, axis=0, dtype=F32)
    g_value_bias = jnp.sum(d_value, axis=0, dtype=F32)
    g_query, g_key, g_value = (
        jnp.einsum("re,rd->ed", entry, d, preferred_element_type=F32).astype(BF) for d in (d_query, d_key, d_value)
    )
    d_entry = (
        jnp.einsum("rd,ed->re", d_query, proj_query, preferred_element_type=F32)
        + jnp.einsum("rd,ed->re", d_key, proj_key, preferred_element_type=F32)
        + jnp.einsum("rd,ed->re", d_value, proj_value, preferred_element_type=F32)
    )
    d_settled = d_first_in + d_entry
    text_grad = d_settled * keep
    d_masked = jnp.zeros_like(text_grad)
    tap_sums = []
    for s in range(1, 4):
        for t in range(3):
            offset = (t - 1) * s
            d_masked = d_masked + conv_text[s - 1, t] * shifted(text_grad, -offset)
            tap_sums.append(jnp.sum(text_grad * shifted(masked, offset), axis=0))
    g_conv_text = jnp.stack(tap_sums).reshape(9, width)
    patch_grad = d_settled[TEXT : TEXT + patches].reshape(GRID, GRID, width)
    unused_out, patch_pull = jax.vjp(patch_conv, patch_rows, conv_patch)
    d_patch_rows, g_conv_patch = patch_pull(patch_grad)
    grad_tokens = d_settled + keep * d_masked + jnp.concatenate([above, d_patch_rows.reshape(patches, width), below], 0)
    grad_tokens = page_in(grad_tokens.astype(BF).reshape(n_seq, stretch, width)).astype(F32)

    a = jnp.arange(BOX)[:, None]
    c = jnp.arange(BOX)[None]
    nb = rel_order.shape[1]
    cell_hot = (jnp.clip(c - a, -SPAN, SPAN).reshape(-1, 1) + SPAN == jnp.arange(nb)).astype(F32)
    i = jnp.arange(RT)[:, None]
    j = jnp.arange(128)[None]
    band = jnp.stack([jnp.clip(d + j - i, -SPAN, SPAN) for d in order_offsets()] + [jnp.full((RT, 128), -SPAN), jnp.full((RT, 128), SPAN)])
    band_hot = (band.reshape(-1, 1) + SPAN == jnp.arange(nb)).astype(F32)
    high = lax.Precision.HIGHEST
    g_horiz = jnp.dot(hist[:, :BOX, :BOX].reshape(heads, -1), cell_hot, precision=high)
    g_vert = jnp.dot(hist[:, BOX:, BOX:].reshape(heads, -1), cell_hot, precision=high)
    g_order = jnp.dot(ords.reshape(heads, -1), band_hot, precision=high)

    def reduced_matrix(g):
        return scatter_pages(g.reshape(n_pages, g.shape[0] // n_pages, g.shape[1]))

    o_reduce = sum_seq(reduced_matrix(g_reduce)).astype(F32)
    o_expand = sum_seq(reduced_matrix(g_expand)).astype(F32)
    four = jnp.concatenate([g.reshape(n_pages, width // n_pages, width) for g in (g_output, g_query, g_key, g_value)], 1)
    o_four = sum_seq(scatter_pages(four)).astype(F32)
    rb = width // n_pages
    o_output, o_query, o_key, o_value = (o_four[k * rb : (k + 1) * rb] for k in range(4))

    small = [
        g_conv_text, g_conv_patch.reshape(9, width), g_query_bias, g_value_bias, g_output_bias,
        g_order, g_horiz, g_vert, g_norm_gain, g_norm_shift, g_expand_bias, g_reduce_bias, g_final_gain, g_final_shift,
    ]
    sizes = [x.size for x in small]
    flat = jnp.concatenate([x.reshape(-1) for x in small])
    pad = -flat.size % 1024
    flat = sum_all(jnp.pad(flat, (0, pad)).reshape(-1, 128)).reshape(-1)
    shapes = [(3, 3, width), (3, 3, width)] + [x.shape for x in small[2:]]
    outs, at = [], 0
    for size, shape in zip(sizes, shapes):
        outs.append(flat[at : at + size].reshape(shape))
        at += size
    (s_conv_text, s_conv_patch, s_query_bias, s_value_bias, s_output_bias, s_order, s_horiz, s_vert,
     s_norm_gain, s_norm_shift, s_expand_bias, s_reduce_bias, s_final_gain, s_final_shift) = outs
    return (
        mixed_out, grad_tokens, s_conv_text, s_conv_patch, o_query, s_query_bias, o_key, o_value, s_value_bias,
        o_output, s_output_bias, s_order, s_horiz, s_vert, s_norm_gain, s_norm_shift, o_expand, s_expand_bias,
        o_reduce, s_reduce_bias, s_final_gain, s_final_shift,
    )


def solution(mesh):
    placed = (
        P("pages", "seq", None),
        P("pages", "seq", None),
        P(),
        P(),
        P(),
        P(),
        P(),
        P(),
        P(),
        P(),
        P(),
        P(),
        P(),
        P(),
        P(),
        P(),
        P(),
        P(),
        P(),
        P(),
        P(),
        P(),
        P("pages"),
        P("pages", None),
        P("pages", None),
    )
    return jax.shard_map(
        per_device,
        mesh=mesh,
        in_specs=placed,
        out_specs=(
            P("pages", "seq", None),
            P("pages", "seq", None),
            P(),
            P(),
            P("pages", None),
            P(),
            P("pages", None),
            P("pages", None),
            P(),
            P("pages", None),
            P(),
            P(),
            P(),
            P(),
            P(),
            P(),
            P("pages", None),
            P(),
            P("pages", None),
            P(),
            P(),
            P(),
        ),
        check_vma=False,
    )
```

```python
import functools
import jax
import jax.numpy as jnp
from jax import lax
from jax.experimental import pallas as pl
from jax.experimental.pallas import tpu as pltpu
from jax.sharding import PartitionSpec as P

BF = jnp.bfloat16
F32 = jnp.float32
TEXT = 512
GRID = 7
SPAN = 16
EPS = 1e-06
SCALE = 0.125
NEG = -1e30
BOX = 64
RT = 64
EDGE = 16
CELLS = 56
OFFSETS = (-128, -64, 0, 64)
TAPS = (-3, -2, -1, 0, 1, 2, 3)
ERF_P = 0.33
ERF_Q = (0.18635791540145874, 0.1829543262720108, 0.20123349130153656, 0.047190189361572266,
         0.4085558354854584, -0.35120898485183716, 0.4602709114551544, -0.1353536993265152)


def dot(a, b):
    return jnp.dot(a, b, preferred_element_type=F32)


def dot_t(a, b):
    return lax.dot_general(a, b, (((1,), (1,)), ((), ())), preferred_element_type=F32)


def t_dot(a, b):
    return lax.dot_general(a, b, (((0,), (0,)), ((), ())), preferred_element_type=F32)


def whole(shape, buffers=1):
    return pl.BlockSpec(shape, lambda *_: (0,) * len(shape), pipeline_mode=pl.Buffered(buffers))


def whole_out(shape):
    return pl.BlockSpec(shape, lambda *_: (0,) * len(shape))


def lanes(n):
    return [slice(128 * c, 128 * (c + 1)) for c in range(n // 128)]


def row_sum(x):
    return jnp.sum(x, axis=0, keepdims=True)


def shift_rows(window, offset, rows):
    if offset == 0:
        return window[8 : 8 + rows]
    return pltpu.roll(window, (-offset) % window.shape[0], 0)[8 : 8 + rows]


def gather_page(dest, row0, place, n_seq, own, others):
    stretch = own.shape[0]
    for d, block in enumerate((own,) + tuple(others)):
        source = lax.rem(place - d + n_seq, n_seq)
        dest[pl.ds(pl.multiple_of(row0 + source * stretch, 16), stretch), :] = block[...].astype(dest.dtype)


def front_kernel(info_ref, edge_ref, *refs, n_seq):
    blocks = refs[:n_seq]
    (ct_ref, cp_ref, pm_ref, turn_ref, wq_ref, bq_ref, wk_ref, wv_ref, bv_ref, oh_ref, wt_ref, ord_ref,
     set_ref, et_ref, q_ref, k_ref, v_ref, p_ref, o_ref,
     entry_ref, xs_ref, ms_ref, ka_ref, qa_ref, s_ref) = refs[n_seq:]
    g = pl.program_id(0)
    length, width = entry_ref.shape
    place, count = info_ref[0], info_ref[1]

    @pl.when(g == 0)
    def _():
        zero = jnp.zeros((EDGE, width), F32)
        xs_ref[0:EDGE, :] = zero
        xs_ref[EDGE + length :, :] = zero
        ms_ref[0:EDGE, :] = zero
        ms_ref[EDGE + length :, :] = zero
        gather_page(xs_ref, EDGE, place, n_seq, blocks[0], blocks[1:])

        def mask_chunk(i, carry):
            r0 = pl.multiple_of(i * RT, RT)
            keep = (r0 + lax.broadcasted_iota(jnp.int32, (RT, 128), 0)) < count
            for c in lanes(width):
                ms_ref[pl.ds(r0 + EDGE, RT), c] = jnp.where(keep, xs_ref[pl.ds(r0 + EDGE, RT), c], 0.0)
            return carry

        lax.fori_loop(0, length // RT, mask_chunk, 0)

        def conv_chunk(i, carry):
            r0 = pl.multiple_of(i * RT, RT)
            keep = (r0 + lax.broadcasted_iota(jnp.int32, (RT, 128), 0)) < count
            for c in lanes(width):
                window = ms_ref[pl.ds(r0 + EDGE - 8, RT + 16), c]
                term = None
                for n, d in enumerate(TAPS):
                    part = shift_rows(window, d, RT) * ct_ref[n : n + 1, c]
                    term = part if term is None else term + part
                set_ref[pl.ds(r0, RT), c] = xs_ref[pl.ds(r0 + EDGE, RT), c] + jnp.where(keep, term, 0.0)
            return carry

        lax.fori_loop(0, length // RT, conv_chunk, 0)
        for c in lanes(width):
            window = xs_ref[EDGE + TEXT - 8 : EDGE + TEXT + CELLS + 8, c]
            term = jnp.zeros((CELLS, 128), F32)
            for n in range(9):
                off = (n // 3 - 1) * GRID + n % 3 - 1
                term = term + shift_rows(window, off, CELLS) * (cp_ref[n : n + 1, c] * pm_ref[:, n : n + 1])
            set_ref[TEXT : TEXT + CELLS, c] = set_ref[TEXT : TEXT + CELLS, c] + term
        entry_ref[...] = set_ref[...].astype(BF)
        et_ref[...] = dot_t(turn_ref[...], entry_ref[...]).astype(BF)
        for c in range(width // 256):
            s = slice(256 * c, 256 * (c + 1))
            q_ref[:, s] = (dot(entry_ref[...], wq_ref[:, s]) + bq_ref[:, s]).astype(BF) * jnp.asarray(SCALE, BF)
            k_ref[:, s] = dot(entry_ref[...], wk_ref[:, s]).astype(BF)
            v_ref[:, s] = (dot(entry_ref[...], wv_ref[:, s]) + bv_ref[:, s]).astype(BF)
        ka_ref[:, 128:256] = oh_ref[...]
        ka_ref[:, 256:384] = oh_ref[...]

    pair = pl.ds(pl.multiple_of(g * 128, 128), 128)
    ka_ref[:, 0:128] = k_ref[:, pair]
    lane = lax.broadcasted_iota(jnp.int32, (length, 128), 1)
    for e in range(2):
        mine = (lane < 64) if e == 0 else (lane >= 64)
        qa_ref[e, :, 0:128] = jnp.where(mine, q_ref[:, pair], jnp.zeros((), BF))
        qa_ref[e, :, 128:384] = dot(oh_ref[...], wt_ref[e]).astype(BF)
        s_ref[e] = dot_t(qa_ref[e], ka_ref[...])
    cols = (length + 127) // 128
    at = lax.broadcasted_iota(jnp.int32, (1, length), 1)
    ok = (at < count) | ((at >= TEXT) & (at < TEXT + GRID * GRID))
    bar = jnp.where(ok, 0.0, NEG)
    outs = []
    for e in range(2):
        left, right = edge_ref[2 * g + e, 0], edge_ref[2 * g + e, 1]
        for a in range(length // RT):
            r0 = a * RT
            parts = []
            for b in range(cols):
                w = min(128, length - 128 * b)
                d = 128 * b - r0
                t = s_ref[e, r0 : r0 + RT, 128 * b : 128 * b + w]
                m = bar[:, 128 * b : 128 * b + w]
                if d in OFFSETS:
                    t = t + ord_ref[e, OFFSETS.index(d)][:, :w] + m
                else:
                    t = t + (m + (left if d < 0 else right))
                parts.append(t)
            t = jnp.concatenate(parts, 1)
            top = jnp.max(t, axis=1, keepdims=True)
            ex = jnp.exp(t - top)
            total = jnp.sum(ex, axis=1, keepdims=True)
            p_ref[e, r0 : r0 + RT, :] = (ex * (1.0 / total)).astype(BF)
        outs.append(dot(p_ref[e], v_ref[:, pair]))
    o_ref[...] = jnp.where(lane < 64, outs[0], outs[1]).astype(BF)


def front(info, edge, blocks, ct, cp, pm, turn, wq, bq, wk, wv, bv, oh, wt, od):
    n_seq = len(blocks)
    stretch, width = blocks[0].shape
    length = n_seq * stretch
    heads = wt.shape[0]
    sds = jax.ShapeDtypeStruct
    flops = 2 * length * width * width * 3 + heads * 2 * length * length * (384 + 128)
    return pl.pallas_call(
        functools.partial(front_kernel, n_seq=n_seq),
        out_shape=(sds((length, width), F32), sds((width, length), BF)) + (sds((length, width), BF),) * 3
        + (sds((heads, length, length), BF), sds((length, width), BF)),
        grid_spec=pltpu.PrefetchScalarGridSpec(
            num_scalar_prefetch=2, grid=(heads // 2,),
            in_specs=[whole((stretch, width))] * n_seq
            + [whole(ct.shape), whole(cp.shape), whole(pm.shape), whole(turn.shape), whole(wq.shape), whole(bq.shape), whole(wk.shape),
               whole(wv.shape), whole(bv.shape), whole(oh.shape),
               pl.BlockSpec((2, 128, 256), lambda g, *_: (g, 0, 0)),
               pl.BlockSpec((2, len(OFFSETS), RT, 128), lambda g, *_: (g, 0, 0, 0))],
            out_specs=[whole_out((length, width)), whole_out((width, length))] + [whole_out((length, width))] * 3
            + [pl.BlockSpec((2, length, length), lambda g, *_: (g, 0, 0)), pl.BlockSpec((length, 128), lambda g, *_: (0, g))],
            scratch_shapes=[pltpu.VMEM((length, width), BF), pltpu.VMEM((length + 2 * EDGE, width), F32), pltpu.VMEM((length + 2 * EDGE, width), F32),
                            pltpu.VMEM((length, 384), BF), pltpu.VMEM((2, length, 384), BF), pltpu.VMEM((2, length, length), F32)],
        ),
        cost_estimate=pl.CostEstimate(flops=25_000_000_000, bytes_accessed=8 << 20, transcendentals=0),
        name="front",
    )(info, edge, *blocks, ct, cp, pm, turn, wq, bq, wk, wv, bv, oh, wt, od)


def norm_stats(u):
    mean = jnp.mean(u, axis=1, keepdims=True)
    c = u - mean
    rs = lax.rsqrt(jnp.mean(c * c, axis=1, keepdims=True) + EPS)
    return c * rs, rs


def norm_back(u, xhat, rs):
    return rs * (u - jnp.mean(u, axis=1, keepdims=True) - xhat * jnp.mean(u * xhat, axis=1, keepdims=True))


def gelu_pair(x):
    t = 1.0 / (1.0 + jnp.abs(x) * (ERF_P * 0.7071067811865476))
    bell = jnp.exp(x * x * -0.5)
    q = jnp.full_like(t, 0.5 * ERF_Q[7])
    for k in range(6, -1, -1):
        q = q * t + 0.5 * ERF_Q[k]
    tail = q * t * bell
    cdf = jnp.where(x < 0, tail, 1.0 - tail)
    return x * cdf, cdf + x * (bell * 0.3989422804014327)


def middle_kernel(info_ref, *refs, n_seq, tiles, tile, block):
    cots = refs[:n_seq]
    (att_ref, set_ref, wo_ref, bo_ref, ng_ref, ns_ref, w1_ref, b1_ref, w2_ref, b2_ref, fg_ref, fs_ref, turn_ref) = refs[n_seq : n_seq + 13]
    outs = refs[n_seq + 13 :]
    mixed = outs[:n_seq]
    (xh_ref, rs_ref, fl_ref, gp_ref, ds_ref, dr_ref, gk_ref, gs_ref, sm_ref, act_ref, fn_ref, acc_ref, cot_ref, mix_ref, e_ref, g_ref) = outs[n_seq:]
    i = pl.program_id(0)
    length, width = fl_ref.shape
    place = info_ref[0]

    @pl.when(i == 0)
    def _():
        for c in range(width // 256):
            s = slice(256 * c, 256 * (c + 1))
            acc_ref[:, s] = dot(att_ref[...], wo_ref[:, s])

        def chunk(j, carry):
            r = pl.ds(pl.multiple_of(j * RT, RT), RT)
            u = set_ref[r, :] + (acc_ref[r, :] + bo_ref[...])
            xhat, rs = norm_stats(u)
            xh_ref[r, :] = xhat
            rs_ref[r, :] = jnp.broadcast_to(rs, (RT, 128))
            fn = xhat * ng_ref[...] + ns_ref[...]
            fn_ref[r, :] = fn
            fl_ref[r, :] = fn.astype(BF)
            return carry

        lax.fori_loop(0, length // RT, chunk, 0)
        gather_page(cot_ref, 0, place, n_seq, cots[0], cots[1:])

    @pl.when(i < tiles)
    def _():
        half = tile // 3
        for n in range(3):
            e_ref[n] = dot(fl_ref[...], w1_ref[:, n * half : (n + 1) * half])
        for n in range(3):
            s = slice(n * half, (n + 1) * half)
            act, gp = gelu_pair(e_ref[n] + b1_ref[:, s])
            act_ref[i, :, s] = act.astype(BF)
            gp_ref[:, s] = gp.astype(gp_ref.dtype)
        part = dot(act_ref[i], w2_ref[...])

        @pl.when(i == 0)
        def _():
            acc_ref[...] = part

        @pl.when(i > 0)
        def _():
            acc_ref[...] += part

    @pl.when(i == tiles - 1)
    def _():
        def chunk(j, sums):
            r0 = pl.multiple_of(j * RT, RT)
            r = pl.ds(r0, RT)
            second = fn_ref[r, :] + (acc_ref[r, :] + b2_ref[...])
            xhat, rs = norm_stats(second)
            mix_ref[r, :] = (xhat * fg_ref[...] + fs_ref[...]).astype(BF)
            cot = cot_ref[r, :].astype(F32)
            back = norm_back(cot * fg_ref[...], xhat, rs)
            ds_ref[r, :] = back
            low = back.astype(BF)
            dr_ref[r, :] = low
            return (sums[0] + row_sum(cot * xhat), sums[1] + row_sum(cot), sums[2] + row_sum(low.astype(F32)))

        sums = lax.fori_loop(0, length // RT, chunk, (jnp.zeros((1, width), F32),) * 3)
        for n in range(3):
            sm_ref[n : n + 1, :] = sums[n]
        stretch = length // n_seq
        for d in range(n_seq):
            dest = lax.rem(place + d, n_seq)
            mixed[d][...] = mix_ref[pl.ds(pl.multiple_of(dest * stretch, 16), stretch), :]

    @pl.when(i >= tiles)
    def _():
        grad = t_dot(act_ref[i - tiles], dr_ref[...]).astype(BF)
        if 2 * block == tile:
            g_ref[...] = grad
            core = info_ref[2]
            gk_ref[...] = g_ref[pl.ds(pl.multiple_of(core * block, block), block), :]
            gs_ref[...] = g_ref[pl.ds(pl.multiple_of((1 - core) * block, block), block), :]
        else:
            turned = dot(turn_ref[...], grad).astype(BF)
            gk_ref[...] = turned[: tile // 2]
            gs_ref[...] = turned[tile // 2 :]


def middle(info, cots, att, settled, wo, bo, ng, ns, w1, b1, w2, b2, fg, fs, turn, block):
    tile = w1.shape[0]
    n_seq = len(cots)
    stretch, width = cots[0].shape
    length = n_seq * stretch
    ff = w1.shape[1]
    tiles = ff // tile
    sds = jax.ShapeDtypeStruct
    early = lambda i: jnp.minimum(i, tiles - 1)
    late = lambda i: jnp.maximum(i - tiles, 0)
    return pl.pallas_call(
        functools.partial(middle_kernel, n_seq=n_seq, tiles=tiles, tile=tile, block=block),
        out_shape=(sds((stretch, width), BF),) * n_seq
        + (sds((length, width), F32), sds((length, 128), F32), sds((length, width), BF), sds((length, ff), BF),
           sds((length, width), F32), sds((length, width), BF), sds((ff // 2, width), BF), sds((ff // 2, width), BF), sds((8, width), F32)),
        grid_spec=pltpu.PrefetchScalarGridSpec(
            num_scalar_prefetch=1, grid=(2 * tiles,),
            in_specs=[whole((stretch, width))] * n_seq
            + [whole(att.shape), whole(settled.shape), whole(wo.shape), whole(bo.shape), whole(ng.shape), whole(ns.shape),
               pl.BlockSpec((width, tile), lambda i, *_: (0, early(i))), pl.BlockSpec((1, tile), lambda i, *_: (0, early(i))),
               pl.BlockSpec((tile, width), lambda i, *_: (early(i), 0)), whole(b2.shape), whole(fg.shape), whole(fs.shape), whole(turn.shape)],
            out_specs=[whole_out((stretch, width))] * n_seq
            + [whole_out((length, width)), whole_out((length, 128)), whole_out((length, width)),
               pl.BlockSpec((length, tile), lambda i, *_: (0, early(i))),
               whole_out((length, width)), whole_out((length, width)),
               pl.BlockSpec((tile // 2, width), lambda i, *_: (late(i), 0)), pl.BlockSpec((tile // 2, width), lambda i, *_: (late(i), 0)),
               whole_out((8, width))],
            scratch_shapes=[pltpu.VMEM((tiles, length, tile), BF), pltpu.VMEM((length, width), F32), pltpu.VMEM((length, width), F32),
                            pltpu.VMEM((length, width), BF), pltpu.VMEM((length, width), BF), pltpu.VMEM((3, length, tile // 3), F32),
                            pltpu.VMEM((tile, width), BF)],
        ),
        cost_estimate=pl.CostEstimate(flops=35_000_000_000, bytes_accessed=8 << 20, transcendentals=0),
        name="middle",
    )(info, *cots, att, settled, wo, bo, ng, ns, w1, b1, w2, b2, fg, fs, turn)


def back_kernel(*refs, tiles, last):
    if last:
        (dr_ref, in_ref, w2_ref, gp_ref, w1_ref, fl_ref, turn_ref, xh_ref, rs_ref, ng_ref, att_ref, wo_ref) = refs[:12]
        (gk_ref, gs_ref, be_ref, df_ref, da_ref, sm_ref, flt_ref, acc_ref, db_ref) = refs[-9:]
    else:
        (dr_ref, in_ref, w2_ref, gp_ref, w1_ref, fl_ref, turn_ref) = refs[:7]
        (gk_ref, gs_ref, be_ref, acc_ref, flt_ref) = refs[-5:]
    i = pl.program_id(0)
    length, width = dr_ref.shape

    @pl.when(i == 0)
    def _():
        flt_ref[...] = dot_t(turn_ref[...], fl_ref[...]).astype(BF)
        acc_ref[...] = in_ref[...]

    @pl.when(i < tiles)
    def _():
        de = dot_t(dr_ref[...], w2_ref[...]) * gp_ref[...].astype(F32)
        de = de.astype(BF)
        be_ref[...] = row_sum(de.astype(F32))
        grad = dot(flt_ref[...], de).astype(BF)
        gk_ref[...] = grad[: width // 2]
        gs_ref[...] = grad[width // 2 :]
        acc_ref[...] += dot_t(de, w1_ref[...])

    if not last:
        return

    @pl.when(i == tiles)
    def _():
        def chunk(j, sums):
            r = pl.ds(pl.multiple_of(j * RT, RT), RT)
            first = acc_ref[r, :]
            xhat = xh_ref[r, :]
            back = norm_back(first * ng_ref[...], xhat, rs_ref[r, 0:1])
            df_ref[r, :] = back
            low = back.astype(BF)
            db_ref[r, :] = low
            return (sums[0] + row_sum(first * xhat), sums[1] + row_sum(first), sums[2] + row_sum(low.astype(F32)))

        sums = lax.fori_loop(0, length // RT, chunk, (jnp.zeros((1, width), F32),) * 3)
        for n in range(3):
            sm_ref[n : n + 1, :] = sums[n]
        da_ref[...] = dot_t(db_ref[...], wo_ref[...]).astype(BF)
        grad = dot(dot_t(turn_ref[...], att_ref[...]).astype(BF), db_ref[...]).astype(BF)
        gk_ref[...] = grad[: width // 2]
        gs_ref[...] = grad[width // 2 :]


def back(first, tiles, dr, acc, w2, gp, w1, fl, turn, filled=(), norm=None):
    length, width = dr.shape
    ff = w1.shape[1]
    last = norm is not None
    sds = jax.ShapeDtypeStruct
    at = lambda i: jnp.minimum(i, tiles - 1) + first
    grad = pl.BlockSpec((width // 2, width), lambda i: (0, i + first))
    args = [dr, acc, w2, gp, w1, fl, turn] + list(norm or ())
    out_shape = [sds((width // 2, ff + width), BF), sds((width // 2, ff + width), BF), sds((1, ff), F32), sds((length, width), F32)]
    out_specs = [grad, grad, pl.BlockSpec((1, width), lambda i: (0, at(i))), whole_out((length, width))]
    scratch = [pltpu.VMEM((width, length), BF)]
    if last:
        out_shape += [sds((length, width), BF), sds((8, width), F32)]
        out_specs += [whole_out((length, width)), whole_out((8, width))]
        scratch += [pltpu.VMEM((length, width), F32), pltpu.VMEM((length, width), BF)]
    return pl.pallas_call(
        functools.partial(back_kernel, tiles=tiles, last=last),
        out_shape=tuple(out_shape),
        grid=(tiles + last,),
        in_specs=[whole(dr.shape), whole(acc.shape), pl.BlockSpec((width, width), lambda i: (at(i), 0)),
                  pl.BlockSpec((length, width), lambda i: (0, at(i))), pl.BlockSpec((width, width), lambda i: (0, at(i)))]
        + [whole(x.shape) for x in args[5:]] + [pl.BlockSpec(memory_space=pl.ANY)] * len(filled),
        out_specs=out_specs,
        scratch_shapes=scratch,
        input_output_aliases={len(args) + n: n for n in range(len(filled))},
        cost_estimate=pl.CostEstimate(flops=12_000_000_000, bytes_accessed=8 << 20, transcendentals=0),
        name="back",
    )(*args, *filled)


def diagonals(x):
    wide = jnp.concatenate([x, jnp.zeros_like(x)], 1)
    return row_sum(pltpu.roll(wide, 0, 1, stride=1, stride_axis=0))


def hi_lo(x):
    hi = x.astype(BF)
    return jnp.concatenate([hi, (x - hi.astype(F32)).astype(BF)], 1)


def heads_kernel(*refs):
    (p_ref, q_ref, k_ref, v_ref, do_ref, o_ref, oh_ref, oht_ref, et_ref, wq_ref, wk_ref, wv_ref, in_ref) = refs[:13]
    (gk_ref, gs_ref, qb_ref, diag_ref, acc_ref, va_ref, rhs_ref, dsc_ref, dp_ref, w_ref, d_ref) = refs[-11:]
    g = pl.program_id(0)
    length = q_ref.shape[0]
    lane = lax.broadcasted_iota(jnp.int32, (length, 128), 1)

    @pl.when(g == 0)
    def _():
        va_ref[:, 128:256] = jnp.where(lane < 2, 1.0, 0.0).astype(BF)
        rhs_ref[:, 128:256] = oh_ref[...]
        acc_ref[...] = in_ref[...]

    va_ref[:, 0:128] = v_ref[...]
    rhs_ref[:, 0:128] = k_ref[...]
    cols = (length + 127) // 128
    flip = (lax.broadcasted_iota(jnp.int32, (RT, RT), 0) + lax.broadcasted_iota(jnp.int32, (RT, RT), 1) == RT - 1).astype(F32).astype(BF)
    do = do_ref[...]
    prod = do.astype(F32) * o_ref[...].astype(F32)
    res = []
    for e in range(2):
        mine = (lane < 64) if e == 0 else (lane >= 64)
        inner = -jnp.sum(jnp.where(mine, prod, 0.0), axis=1, keepdims=True)
        hi = inner.astype(BF)
        lo = inner - hi.astype(F32)
        ext = jnp.where(lane == 0, hi.astype(F32), jnp.where(lane == 1, lo, 0.0)).astype(BF)
        da = jnp.concatenate([jnp.where(mine, do, jnp.zeros((), BF)), ext], 1)
        dp_ref[e] = dot_t(da, va_ref[...])
    for e in range(2):
        sums = {}
        for a in range(length // RT):
            r0 = a * RT
            ds = p_ref[e, r0 : r0 + RT, :].astype(F32) * dp_ref[e, r0 : r0 + RT, :]
            dsc_ref[e, r0 : r0 + RT, :] = ds.astype(BF)
            for b in range(cols):
                w = min(128, length - 128 * b)
                d = 128 * b - r0
                t = ds[:, 128 * b : 128 * b + w]
                if w < 128:
                    t = jnp.concatenate([t, jnp.zeros((RT, 128 - w), F32)], 1)
                key = OFFSETS.index(d) if d in OFFSETS else (4 if d < 0 else 5)
                sums[key] = sums[key] + t if key in sums else t
        for n in range(4):
            turned = dot(flip, hi_lo(sums[n]))
            diag_ref[e, n : n + 1, :] = diagonals(turned[:, 0:128] + turned[:, 128:256])
        diag_ref[e, 4:5, 0:128] = row_sum(sums[4])
        diag_ref[e, 4:5, 128:256] = row_sum(sums[5])
        r = dot(dsc_ref[e], rhs_ref[...])
        hh = dot(oht_ref[...], hi_lo(r[:, 128:256]))
        hist = hh[:, 0:128] + hh[:, 128:256]
        half = lane[:BOX] < BOX
        diag_ref[e, 5:6, :] = diagonals(jnp.where(half, hist[:BOX], 0.0))
        diag_ref[e, 6:7, :] = diagonals(jnp.where(half, 0.0, hist[BOX:]))
        diag_ref[e, 7:8, :] = jnp.zeros((1, 256), F32)
        dk = t_dot(dsc_ref[e], q_ref[...])
        dv = t_dot(p_ref[e], do)
        res.append((r[:, 0:128], dk, dv))
    first = lane < 64
    dq = (jnp.where(first, res[0][0], res[1][0]) * SCALE).astype(BF)
    dk = jnp.where(first, res[0][1], res[1][1]).astype(BF)
    dv = jnp.where(first, res[0][2], res[1][2]).astype(BF)
    d_ref[:, 0:128] = dq
    d_ref[:, 128:256] = dk
    d_ref[:, 256:384] = dv
    qb_ref[0:1, :] = row_sum(dq.astype(F32))
    qb_ref[1:2, :] = row_sum(dv.astype(F32))
    w_ref[:, 0:128] = wq_ref[...]
    w_ref[:, 128:256] = wk_ref[...]
    w_ref[:, 256:384] = wv_ref[...]
    grad = dot(et_ref[...], d_ref[...]).astype(BF)
    gk_ref[...] = grad[: grad.shape[0] // 2]
    gs_ref[...] = grad[grad.shape[0] // 2 :]
    acc_ref[...] += dot_t(d_ref[...], w_ref[...])


def heads_back(first, count, probs, q, k, v, do, o, oh, oht, et, wq, wk, wv, acc, filled=()):
    heads = probs.shape[0]
    length, width = q.shape
    steps = count // 2
    base = first // 2
    sds = jax.ShapeDtypeStruct
    col = pl.BlockSpec((length, 128), lambda g: (0, g + base))
    wcol = pl.BlockSpec((width, 128), lambda g: (0, g + base))
    flops = 2 * length * width * 64 * count * 6 + count * 2 * length * length * (256 + 256 + 128 + 128)
    return pl.pallas_call(
        heads_kernel,
        out_shape=(sds((width // 2, 3 * width), BF), sds((width // 2, 3 * width), BF), sds((8, width), F32), sds((heads, 8, 256), F32), sds((length, width), F32)),
        grid=(steps,),
        in_specs=[pl.BlockSpec((2, length, length), lambda g: (g + base, 0, 0)), col, col, col, col, col, whole(oh.shape), whole(oht.shape),
                  whole(et.shape), wcol, wcol, wcol, whole(acc.shape)] + [pl.BlockSpec(memory_space=pl.ANY)] * len(filled),
        out_specs=[pl.BlockSpec((width // 2, 384), lambda g: (0, g + base)), pl.BlockSpec((width // 2, 384), lambda g: (0, g + base)),
                   pl.BlockSpec((8, 128), lambda g: (0, g + base)), pl.BlockSpec((2, 8, 256), lambda g: (g + base, 0, 0)), whole_out((length, width))],
        input_output_aliases={13 + n: n for n in range(len(filled))},
        scratch_shapes=[pltpu.VMEM((length, 256), BF), pltpu.VMEM((length, 256), BF), pltpu.VMEM((2, length, length), BF),
                        pltpu.VMEM((2, length, length), F32), pltpu.VMEM((width, 384), BF), pltpu.VMEM((length, 384), BF)],
        cost_estimate=pl.CostEstimate(flops=20_000_000_000, bytes_accessed=8 << 20, transcendentals=0),
        name="heads_back",
    )(probs, q, k, v, do, o, oh, oht, et, wq, wk, wv, acc, *filled)


def encode_kernel(info_ref, *refs, n_seq):
    blocks = refs[:n_seq]
    in_ref, ct_ref, cp_ref, pm_ref, sm_ref, sm2_ref, be_ref, qb_ref = refs[n_seq : n_seq + 8]
    outs = refs[n_seq + 8 :]
    grads = outs[:n_seq]
    small_ref, acc_ref, gs_ref, ms_ref, gt_ref = outs[n_seq:]
    length, width = in_ref.shape
    place, count = info_ref[0], info_ref[1]
    acc_ref[...] = in_ref[...]
    small_ref[...] = jnp.zeros_like(small_ref)
    small_ref[0:3, :] = sm_ref[0:3, :]
    small_ref[3:6, :] = sm2_ref[0:3, :]
    small_ref[6:8, :] = qb_ref[0:2, :]
    tiles = be_ref.shape[1] // width
    for t in range(tiles):
        small_ref[8 + t : 9 + t, :] = be_ref[:, t * width : (t + 1) * width]
    taps, cells = 8 + tiles, 15 + tiles
    zero = jnp.zeros((EDGE, width), F32)
    gs_ref[0:EDGE, :] = zero
    gs_ref[EDGE + length :, :] = zero
    ms_ref[0:EDGE, :] = zero
    ms_ref[EDGE + length :, :] = zero
    gather_page(ms_ref, EDGE, place, n_seq, blocks[0], blocks[1:])
    for c in lanes(width):
        tok = ms_ref[EDGE + TEXT - 8 : EDGE + TEXT + CELLS + 8, c]
        own = acc_ref[TEXT : TEXT + CELLS, c]
        window = jnp.concatenate([acc_ref[TEXT - 8 : TEXT + CELLS, c], jnp.zeros((8, 128), F32)], 0)
        term = jnp.zeros((CELLS, 128), F32)
        for n in range(9):
            off = (n // 3 - 1) * GRID + n % 3 - 1
            term = term + shift_rows(window, -off, CELLS) * (cp_ref[n : n + 1, c] * pm_ref[:, 8 - n : 9 - n])
            small_ref[cells + n : cells + n + 1, c] = row_sum(own * shift_rows(tok, off, CELLS) * pm_ref[:, n : n + 1])
        gt_ref[:, c] = term

    def split_chunk(j, carry):
        r0 = pl.multiple_of(j * RT, RT)
        keep = (r0 + lax.broadcasted_iota(jnp.int32, (RT, 128), 0)) < count
        for c in lanes(width):
            dset = acc_ref[pl.ds(r0, RT), c]
            gs_ref[pl.ds(r0 + EDGE, RT), c] = jnp.where(keep, dset, 0.0)
            ms_ref[pl.ds(r0 + EDGE, RT), c] = jnp.where(keep, ms_ref[pl.ds(r0 + EDGE, RT), c], 0.0)
        return carry

    lax.fori_loop(0, length // RT, split_chunk, 0)
    for c in lanes(width):
        acc_ref[TEXT : TEXT + CELLS, c] = acc_ref[TEXT : TEXT + CELLS, c] + gt_ref[:, c]

    def conv_chunk(j, sums):
        r0 = pl.multiple_of(j * RT, RT)
        keep = (r0 + lax.broadcasted_iota(jnp.int32, (RT, 128), 0)) < count
        out = []
        for n, c in enumerate(lanes(width)):
            window = gs_ref[pl.ds(r0 + EDGE - 8, RT + 16), c]
            own = ms_ref[pl.ds(r0 + EDGE, RT), c]
            term = None
            for m, d in enumerate(TAPS):
                moved = shift_rows(window, -d, RT)
                part = moved * ct_ref[m : m + 1, c]
                term = part if term is None else term + part
                out.append(sums[n * len(TAPS) + m] + row_sum(moved * own))
            acc_ref[pl.ds(r0, RT), c] = acc_ref[pl.ds(r0, RT), c] + jnp.where(keep, term, 0.0)
        return tuple(out)

    zeros = (jnp.zeros((1, 128), F32),) * (len(TAPS) * (width // 128))
    sums = lax.fori_loop(0, length // RT, conv_chunk, zeros)
    for n, c in enumerate(lanes(width)):
        for m in range(len(TAPS)):
            small_ref[taps + m : taps + m + 1, c] = sums[n * len(TAPS) + m]
    stretch = length // n_seq
    for d in range(n_seq):
        dest = lax.rem(place + d, n_seq)
        grads[d][...] = acc_ref[pl.ds(pl.multiple_of(dest * stretch, 16), stretch), :].astype(BF)


def encode_back(info, blocks, d_settled, ct, cp, pm, sm, sm2, be, qb):
    n_seq = len(blocks)
    stretch, width = blocks[0].shape
    length = n_seq * stretch
    sds = jax.ShapeDtypeStruct
    rows = 24 + be.shape[1] // width
    rows += 8 - rows % 8
    return pl.pallas_call(
        functools.partial(encode_kernel, n_seq=n_seq),
        out_shape=(sds((stretch, width), BF),) * n_seq + (sds((rows, width), F32),),
        grid_spec=pltpu.PrefetchScalarGridSpec(
            num_scalar_prefetch=1, grid=(1,),
            in_specs=[whole((stretch, width))] * n_seq + [whole(d_settled.shape), whole(ct.shape), whole(cp.shape), whole(pm.shape), whole(sm.shape), whole(sm2.shape), whole(be.shape), whole(qb.shape)],
            out_specs=[whole_out((stretch, width))] * n_seq + [whole_out((rows, width))],
            scratch_shapes=[pltpu.VMEM((length, width), F32), pltpu.VMEM((length + 2 * EDGE, width), F32),
                            pltpu.VMEM((length + 2 * EDGE, width), F32), pltpu.VMEM((CELLS, width), F32)],
        ),
        cost_estimate=pl.CostEstimate(flops=10_000_000_000, bytes_accessed=8 << 20, transcendentals=0),
        name="encode_back",
    )(info, *blocks, d_settled, ct, cp, pm, sm, sm2, be, qb)


def turn_matrix(width, n, core):
    block, half = width // n, width // 2
    r = jnp.arange(width, dtype=jnp.int32)
    inner = jnp.where(r < half, r, r - half)
    parity = jnp.where(r < half, core, 1 - core)
    source = (2 * (inner // block) + parity) * block + inner % block
    return (source[:, None] == r[None]).astype(BF)


def restack_kernel(info_ref, *refs):
    out_ref = refs[-1]
    n = len(refs) - 1
    for d, part in enumerate(refs[:-1]):
        out_ref[lax.rem(info_ref[0] - d + n, n)] = part[...].astype(out_ref.dtype)


def restack(info, parts, dtype):
    n = len(parts)
    rows, cols = parts[0].shape
    return pl.pallas_call(
        restack_kernel, out_shape=jax.ShapeDtypeStruct((n, rows, cols), dtype),
        in_specs=[pl.BlockSpec(memory_space=pltpu.SMEM)] + [pl.BlockSpec(memory_space=pltpu.VMEM)] * n,
        out_specs=pl.BlockSpec(memory_space=pltpu.VMEM),
        cost_estimate=pl.CostEstimate(flops=1000, bytes_accessed=1000, transcendentals=0),
        name="restack",
    )(info, *parts)


def one_hot_rows(ids, size):
    return (ids.reshape(1, -1) == jnp.arange(size, dtype=jnp.int32)[:, None]).astype(F32)


def tables(rel_order, rel_horiz, rel_vert):
    heads, nb = rel_order.shape
    high = lax.Precision.HIGHEST
    a = jnp.arange(BOX, dtype=jnp.int32)
    cell = one_hot_rows(jnp.clip(a[None, :] - a[:, None], -SPAN, SPAN) + SPAN, nb)

    def split(table):
        x = jnp.dot(table, cell, precision=high).reshape(heads, BOX, BOX)
        top = lax.reduce_precision(x, 8, 7)
        return top, x - top

    (hh, hl), (vh, vl) = split(rel_horiz), split(rel_vert)
    zero = jnp.zeros_like(hh)
    wt = jnp.concatenate([jnp.concatenate([hh, zero, hl, zero], 2), jnp.concatenate([zero, vh, zero, vl], 2)], 1).astype(BF)
    i = jnp.arange(RT, dtype=jnp.int32)[:, None]
    j = jnp.arange(128, dtype=jnp.int32)[None]
    band = jnp.stack([jnp.clip(d + j - i, -SPAN, SPAN) + SPAN for d in OFFSETS])
    od = jnp.dot(rel_order, one_hot_rows(band, nb), precision=high).reshape(heads, len(OFFSETS), RT, 128)
    edge = jnp.stack([rel_order[:, 0], rel_order[:, -1]], 1)
    return wt, od, edge


def bias_grads(diag, nb):
    heads = diag.shape[0]
    high = lax.Precision.HIGHEST
    at = jnp.arange(256, dtype=jnp.int32)
    step = at - (RT - 1)
    order_bins = jnp.stack([jnp.clip(d + step, -SPAN, SPAN) for d in OFFSETS] + [jnp.where(at < 128, -SPAN, SPAN)]) + SPAN
    order = jnp.dot(diag[:, :5].reshape(heads, -1), one_hot_rows(order_bins, nb).T, precision=high)
    flat = jnp.clip(step, -SPAN, SPAN) + SPAN
    horiz = jnp.dot(diag[:, 5], one_hot_rows(flat, nb).T, precision=high)
    low = jnp.clip(step - BOX, -SPAN, SPAN) + SPAN
    vert = jnp.dot(diag[:, 6], one_hot_rows(low, nb).T, precision=high)
    return order, horiz, vert


def patch_masks():
    g = jnp.arange(CELLS, dtype=jnp.int32)
    i, j = g // GRID, g % GRID
    cols = []
    for n in range(9):
        a, b = i + n // 3 - 1, j + n % 3 - 1
        cols.append((g < GRID * GRID) & (a >= 0) & (a < GRID) & (b >= 0) & (b < GRID))
    return jnp.pad(jnp.stack(cols, 1).astype(F32), ((0, 0), (0, 128 - 9)))


def text_taps(conv_text):
    rows = []
    for d in TAPS:
        if d == 0:
            rows.append(conv_text[0, 1] + conv_text[1, 1] + conv_text[2, 1])
        else:
            rows.append(conv_text[abs(d) - 1, 2 if d > 0 else 0])
    rows.append(jnp.zeros_like(rows[0]))
    return jnp.stack(rows)


def text_tap_grads(rows):
    return jnp.stack([jnp.stack([rows[3 - s], rows[3], rows[3 + s]]) for s in (1, 2, 3)])


def xor_pairs(n, bit):
    return [(i, i ^ bit) for i in range(n)]


def swap(value, axis, bit):
    return lax.ppermute(value, axis, xor_pairs(lax.axis_size(axis), bit))


def spread(blocks, after=None):
    n = lax.axis_size("seq")
    out = [blocks[0]]
    for d in range(1, n):
        out.append(lax.ppermute(blocks[d], "seq", [(i, (i + d) % n) for i in range(n)]))
    return out


def rotated(pages):
    n = lax.axis_size("seq")
    place = lax.axis_index("seq")
    return [lax.dynamic_index_in_dim(pages, lax.rem(place + d, n), 0, keepdims=False) for d in range(n)]


def total(terms):
    out = terms[0].astype(F32)
    for t in terms[1:]:
        out = out + t.astype(F32)
    return out.astype(BF)


class Reduction:
    def __init__(self, keep, send):
        n = lax.axis_size("pages")
        self.bits = [1 << b for b in range(n.bit_length() - 1)][:0:-1]
        self.shape = [2] * len(self.bits) + [keep.shape[0] * 2 // n]
        cols = keep.shape[1]
        self.cols = cols // 2
        self.orders = (self.bits[::-1], list(self.bits))
        self.at = 0
        self.send = send
        self.terms = [(tuple(self.bits), keep.reshape(self.shape + [cols]))]
        self.own = ([], [])
        self.fresh = []

    def pick(self, term, side, closed, sent=None):
        bits, value = term
        starts = [0] * value.ndim
        sizes = list(value.shape)
        for axis, bit in enumerate(bits):
            if bit in closed:
                mine = jnp.minimum(lax.axis_index("pages") & bit, 1)
                starts[axis] = 1 - mine if bit == sent else mine
                sizes[axis] = 1
        if value.shape[-1] > self.cols:
            starts[-1] = side * self.cols
            sizes[-1] = self.cols
        out = lax.dynamic_slice(value, starts, sizes)
        return out.reshape([n for axis, n in enumerate(sizes) if axis >= len(bits) or bits[axis] not in closed])

    def parts(self, side, closed, sent=None):
        return total([self.pick(t, side, closed, sent) for t in self.terms + self.own[side]])

    def step(self):
        at, last = self.at, len(self.bits)
        self.at += 1
        n = lax.axis_size("seq")
        ring = lambda d: [(i, (i + d) % n) for i in range(n)]
        place = lax.axis_index("seq")
        if at == 0:
            got = swap(self.send, "pages", 1)
            self.fresh = [got]
        elif at <= last:
            self.settle()
            self.fresh = []
            for side in range(2):
                closed = self.orders[side][:at]
                send = self.parts(side, closed, closed[-1])
                self.fresh.append(swap(send, "pages", closed[-1]))
        elif at == last + 1:
            self.settle()
            value = jnp.concatenate([self.parts(side, self.bits) for side in range(2)], 1)
            rows, cols = value.shape
            quarters = value.reshape(n, rows // n, cols)
            piece = lambda d: lax.dynamic_index_in_dim(quarters, lax.rem(place + d, n), 0, keepdims=False)
            self.own = [(), piece(0)]
            self.fresh = [lax.ppermute(piece(d), "seq", ring(d)) for d in range(1, n)]
        else:
            self.own = total([self.own[1]] + self.fresh)
            self.fresh = [lax.ppermute(self.own, "seq", ring(d)) for d in range(1, n)]

    def settle(self):
        at, last = self.at - 1, len(self.bits)
        if at == 1:
            self.terms.append((tuple(self.bits), self.fresh[0].reshape(self.terms[0][1].shape)))
        elif at > 1:
            for side in range(2):
                closed = self.orders[side][: at - 1]
                self.own[side].append((tuple(b for b in self.bits if b not in closed), self.fresh[side]))

    def over(self):
        return self.at == len(self.bits) + 3

    def result(self, info):
        out = restack(info, [self.own] + self.fresh, F32)
        return out.reshape(-1, out.shape[-1])


def tie(value, *reductions):
    value, fresh, held = lax.optimization_barrier(
        (value, tuple(r.fresh for r in reductions), tuple(r.send for r in reductions)))
    for r, f, h in zip(reductions, fresh, held):
        r.fresh, r.send = f, h
    return value


def per_device(
    tokens, cotangent, conv_text, conv_patch, proj_query, bias_query, proj_key, proj_value, bias_value,
    proj_output, bias_output, rel_order, rel_horiz, rel_vert, norm_gain, norm_shift, expand_weight,
    expand_bias, reduce_weight, reduce_bias, final_gain, final_shift, text_count, box_left, box_top,
):
    pages_here, stretch, width = tokens.shape
    n_seq = lax.axis_size("seq")
    n_pages = lax.axis_size("pages")
    assert pages_here == n_seq and n_pages & (n_pages - 1) == 0
    place = lax.axis_index("seq")
    heads, nb = rel_order.shape
    ff = expand_weight.shape[1]
    pick = lambda a: lax.dynamic_index_in_dim(a, place, 0, keepdims=False)
    count, left, top = pick(text_count), pick(box_left), pick(box_top)
    blocks = spread(rotated(tokens))
    core = lax.axis_index("pages") & 1
    info = jnp.stack([place, count, core]).astype(jnp.int32)
    turn = turn_matrix(width, n_pages, core)
    cells = jnp.arange(BOX, dtype=jnp.int32)
    oh = jnp.concatenate([left[:, None] == cells[None], top[:, None] == cells[None]], 1).astype(BF)
    oht = jnp.concatenate([left[None] == cells[::-1, None], top[None] == cells[::-1, None]], 0).astype(BF)
    wt, od, edge = tables(rel_order, rel_horiz, rel_vert)
    pm, ct = patch_masks(), text_taps(conv_text)
    cp = jnp.pad(conv_patch.reshape(9, width), ((0, 7), (0, 0)))
    row = lambda x: x[None]

    cot_out, blocks = lax.optimization_barrier((rotated(cotangent), blocks))
    cots = spread(cot_out)
    settled, et, q, k, v, probs, att = front(
        info, edge, blocks, ct, cp, pm, turn, proj_query, row(bias_query), proj_key, proj_value, row(bias_value), oh, wt, od)
    *mixed, xh, rs, fl, gp, ds, dr, grk, grs, sm = middle(
        info, cots, att, settled, proj_output, row(bias_output), row(norm_gain), row(norm_shift), expand_weight,
        row(expand_bias), reduce_weight, row(reduce_bias), row(final_gain), row(final_shift), turn, ff // n_pages)
    c_reduce = Reduction(grk, grs)
    c_reduce.step()
    mixed = spread(mixed)
    done = back(0, 2, dr, ds, reduce_weight, gp, expand_weight, fl, turn)
    done = tie(done, c_reduce)
    c_reduce.step()
    done = back(2, ff // width - 2, dr, done[3], reduce_weight, gp, expand_weight, fl, turn, done[:3],
                (xh, rs, row(norm_gain), att, proj_output))
    done, mixed = tie((done, mixed), c_reduce)
    gek, ges, be, df, da, sm2 = done
    c_expand = Reduction(gek, ges)
    heads_of = lambda first, count, da, acc, filled=(): heads_back(
        first, count, probs, q, k, v, da, att, oh, oht, et, proj_query, proj_key, proj_value, acc, filled)
    half = heads // 2
    c_reduce.step()
    c_expand.step()
    done = heads_of(0, half, da, df)
    done, da = tie((done, da), c_reduce, c_expand)
    c_reduce.step()
    c_expand.step()
    done = heads_of(half, half, da, done[4], done[:4])
    gqk, gqs, qb, diag, acc = tie(done, c_reduce, c_expand)
    c_qkv = Reduction(gqk, gqs)
    c_reduce.step()
    c_expand.step()
    c_qkv.step()
    *gts, small = encode_back(info, blocks, acc, ct, cp, pm, sm, sm2, be, qb)
    rounds = [("pages", 1 << b) for b in range(n_pages.bit_length() - 1)] + [("seq", 1 << b) for b in range(n_seq.bit_length() - 1)]
    hop = lambda d: lax.ppermute(gts[d], "seq", [(i, (i + d) % n_seq) for i in range(n_seq)])
    work = [c_reduce, c_expand, c_qkv]
    bias = jnp.concatenate(bias_grads(diag, nb), 1)
    bias = jnp.pad(bias, ((0, 0), (0, 128 - 3 * nb))).reshape(-1, width)
    phase = 0
    while rounds or not c_qkv.over():
        gts, small, bias = tie((gts, small, bias), *work)
        if phase == 0:
            small = lax.dynamic_update_slice(small, bias, (24 + ff // width, 0))
        for r in work:
            if not r.over():
                r.step()
        for d in {1: (1,), 2: (3,), 3: (2,)}.get(phase, ()):
            gts = [hop(d) if e == d else part for e, part in enumerate(gts)]
        for axis, bit in rounds[: 1 if phase < 3 else 2]:
            small = small + swap(small, axis, bit)
        rounds = rounds[1 if phase < 3 else 2 :]
        phase += 1
    o_reduce, o_expand, o_qkv = (r.result(info) for r in work)
    mixed_out = restack(info, mixed, BF)
    grad_tokens = restack(info, gts, F32)
    g3 = o_qkv.reshape(width // n_pages, heads // 2, 3, 128)
    o_query, o_key, o_value = (g3[:, :, n].reshape(width // n_pages, width) for n in range(3))
    bias = small[24 + ff // width : 24 + ff // width + heads * 128 // width].reshape(heads, 128)

    at = 0

    def take(n):
        nonlocal at
        at += n
        return small[at - n : at]

    sm, sm2, qb, be, gct, gcp = take(3), take(3), take(2), take(ff // width), take(7), take(9)
    return (
        mixed_out, grad_tokens, text_tap_grads(gct), gcp.reshape(3, 3, width), o_query, qb[0], o_key, o_value, qb[1],
        o_expand[:, ff:], sm2[2], bias[:, :nb], bias[:, nb : 2 * nb], bias[:, 2 * nb : 3 * nb], sm2[0], sm2[1],
        o_expand[:, :ff], be.reshape(ff), o_reduce, sm[2], sm[0], sm[1],
    )


def solution(mesh):
    placed = (
        P("pages", "seq", None),
        P("pages", "seq", None),
        P(),
        P(),
        P(),
        P(),
        P(),
        P(),
        P(),
        P(),
        P(),
        P(),
        P(),
        P(),
        P(),
        P(),
        P(),
        P(),
        P(),
        P(),
        P(),
        P(),
        P("pages"),
        P("pages", None),
        P("pages", None),
    )
    return jax.shard_map(
        per_device,
        mesh=mesh,
        in_specs=placed,
        out_specs=(
            P("pages", "seq", None),
            P("pages", "seq", None),
            P(),
            P(),
            P("pages", None),
            P(),
            P("pages", None),
            P("pages", None),
            P(),
            P("pages", None),
            P(),
            P(),
            P(),
            P(),
            P(),
            P(),
            P("pages", None),
            P(),
            P("pages", None),
            P(),
            P(),
            P(),
        ),
        check_vma=False,
    )
```

```python
import functools
import jax
import jax.numpy as jnp
from jax import lax
from jax.experimental import pallas as pl
from jax.experimental.pallas import tpu as pltpu
from jax.sharding import PartitionSpec as P

BF = jnp.bfloat16
F32 = jnp.float32
TEXT = 512
GRID = 7
SPAN = 16
EPS = 1e-06
SCALE = 0.125
NEG = -1e30
BOX = 64
RT = 64
LR = 32
EDGE = 16
CELLS = 56
OFFSETS = (-128, -64, 0, 64)
TAPS = (-3, -2, -1, 0, 1, 2, 3)
ERF_P = 0.33
ERF_Q = (0.18635791540145874, 0.1829543262720108, 0.20123349130153656, 0.047190189361572266,
         0.4085558354854584, -0.35120898485183716, 0.4602709114551544, -0.1353536993265152)


def dot(a, b):
    return jnp.dot(a, b, preferred_element_type=F32)


def dot_t(a, b):
    return lax.dot_general(a, b, (((1,), (1,)), ((), ())), preferred_element_type=F32)


def t_dot(a, b):
    return lax.dot_general(a, b, (((0,), (0,)), ((), ())), preferred_element_type=F32)


def whole(shape, buffers=1):
    return pl.BlockSpec(shape, lambda *_: (0,) * len(shape), pipeline_mode=pl.Buffered(buffers))


def whole_out(shape):
    return pl.BlockSpec(shape, lambda *_: (0,) * len(shape))


def lanes(n):
    return [slice(128 * c, 128 * (c + 1)) for c in range(n // 128)]


def line(ref, part=slice(None)):
    return ref[part].reshape(1, -1)


def row_sum(x):
    return jnp.sum(x, axis=0, keepdims=True)


def fold(x):
    out = x[:8]
    for r in range(8, x.shape[0], 8):
        out = out + x[r : r + 8]
    return out


def shift_rows(window, offset, rows):
    if offset == 0:
        return window[8 : 8 + rows]
    return pltpu.roll(window, (-offset) % window.shape[0], 0)[8 : 8 + rows]


def gather_page(dest, row0, place, n_seq, own, others):
    stretch = own.shape[0]
    for d, block in enumerate((own,) + tuple(others)):
        source = lax.rem(place - d + n_seq, n_seq)
        dest[pl.ds(pl.multiple_of(row0 + source * stretch, 16), stretch), :] = block[...].astype(dest.dtype)


def turned_transpose(x_ref, turn_ref, core, block, dest, raw):
    rows = dest.shape[0]
    if block % 16:
        dest[...] = dot_t(turn_ref[...], x_ref[...]).astype(BF)
        return
    raw[...] = jnp.transpose(x_ref[...])
    half = rows // 2
    for k in range(half // block):
        for side in range(2):
            parity = core if side == 0 else 1 - core
            source = pl.multiple_of((2 * k + parity) * block, 16)
            dest[side * half + k * block : side * half + (k + 1) * block, :] = raw[pl.ds(source, block), :]


def moves(pairs, sems):
    return [pltpu.make_async_copy(source, dest, sems.at[n]) for n, (source, dest) in enumerate(pairs)]


def start(copies):
    for c in copies:
        c.start()


def wait(copies):
    for c in copies:
        c.wait()


def front_kernel(info_ref, edge_ref, *refs, n_seq, block):
    blocks = refs[:n_seq]
    (ct_ref, cp_ref, pm_ref, turn_ref, wq_any, bq_ref, wk_any, wv_any, bv_ref, oh_ref, wt_ref, ord_ref,
     set_any, et_any, q_any, k_any, v_any, p_ref, o_ref,
     entry_ref, xs_ref, ms_ref, ka_ref, qa_ref, s_ref, raw_ref,
     set_ref, et_ref, q_ref, k_ref, v_ref, wq_ref, wk_ref, wv_ref, in_sems, out_sems) = refs[n_seq:]
    g = pl.program_id(0)
    arriving = moves([(wq_any, wq_ref), (wk_any, wk_ref), (wv_any, wv_ref)], in_sems)
    leaving = moves([(set_ref, set_any), (et_ref, et_any), (q_ref, q_any), (k_ref, k_any), (v_ref, v_any)], out_sems)
    length, width = entry_ref.shape
    place, count = info_ref[0], info_ref[1]

    @pl.when(g == 0)
    def _():
        start(arriving)
        zero = jnp.zeros((EDGE, width), F32)
        xs_ref[0:EDGE, :] = zero
        xs_ref[EDGE + length :, :] = zero
        ms_ref[0:EDGE, :] = zero
        ms_ref[EDGE + length :, :] = zero
        gather_page(xs_ref, EDGE, place, n_seq, blocks[0], blocks[1:])

        def mask_chunk(i, carry):
            r0 = pl.multiple_of(i * RT, RT)
            keep = (r0 + lax.broadcasted_iota(jnp.int32, (RT, 128), 0)) < count
            for c in lanes(width):
                ms_ref[pl.ds(r0 + EDGE, RT), c] = jnp.where(keep, xs_ref[pl.ds(r0 + EDGE, RT), c], 0.0)
            return carry

        lax.fori_loop(0, length // RT, mask_chunk, 0)

        def conv_chunk(i, carry):
            r0 = pl.multiple_of(i * RT, RT)
            keep = (r0 + lax.broadcasted_iota(jnp.int32, (RT, 128), 0)) < count
            for c in lanes(width):
                window = ms_ref[pl.ds(r0 + EDGE - 8, RT + 16), c]
                term = None
                for n, d in enumerate(TAPS):
                    part = shift_rows(window, d, RT) * ct_ref[n : n + 1, c]
                    term = part if term is None else term + part
                set_ref[pl.ds(r0, RT), c] = xs_ref[pl.ds(r0 + EDGE, RT), c] + jnp.where(keep, term, 0.0)
            return carry

        lax.fori_loop(0, length // RT, conv_chunk, 0)
        for c in lanes(width):
            window = xs_ref[EDGE + TEXT - 8 : EDGE + TEXT + CELLS + 8, c]
            term = jnp.zeros((CELLS, 128), F32)
            for n in range(9):
                off = (n // 3 - 1) * GRID + n % 3 - 1
                term = term + shift_rows(window, off, CELLS) * (cp_ref[n : n + 1, c] * pm_ref[:, n : n + 1])
            set_ref[TEXT : TEXT + CELLS, c] = set_ref[TEXT : TEXT + CELLS, c] + term
        entry_ref[...] = set_ref[...].astype(BF)
        turned_transpose(entry_ref, turn_ref, info_ref[2], block, et_ref, raw_ref)
        wait(arriving)
        for c in range(width // 256):
            s = slice(256 * c, 256 * (c + 1))
            q_ref[:, s] = (dot(entry_ref[...], wq_ref[:, s]) + line(bq_ref, s)).astype(BF) * jnp.asarray(SCALE, BF)
            k_ref[:, s] = dot(entry_ref[...], wk_ref[:, s]).astype(BF)
            v_ref[:, s] = (dot(entry_ref[...], wv_ref[:, s]) + line(bv_ref, s)).astype(BF)
        ka_ref[:, 128:256] = oh_ref[...]
        ka_ref[:, 256:384] = oh_ref[...]
        start(leaving)

    @pl.when(g == pl.num_programs(0) - 1)
    def _():
        wait(leaving)

    pair = pl.ds(pl.multiple_of(g * 128, 128), 128)
    ka_ref[:, 0:128] = k_ref[:, pair]
    lane = lax.broadcasted_iota(jnp.int32, (length, 128), 1)
    for e in range(2):
        mine = (lane < 64) if e == 0 else (lane >= 64)
        qa_ref[e, :, 0:128] = jnp.where(mine, q_ref[:, pair], jnp.zeros((), BF))
        qa_ref[e, :, 128:384] = dot(oh_ref[...], wt_ref[e]).astype(BF)
        s_ref[e] = dot_t(qa_ref[e], ka_ref[...])
    cols = (length + 127) // 128
    at = lax.broadcasted_iota(jnp.int32, (1, length), 1)
    ok = (at < count) | ((at >= TEXT) & (at < TEXT + GRID * GRID))
    bar = jnp.where(ok, 0.0, NEG)
    outs = []
    for e in range(2):
        left, right = edge_ref[2 * g + e, 0], edge_ref[2 * g + e, 1]
        for a in range(length // RT):
            r0 = a * RT
            parts = []
            for b in range(cols):
                w = min(128, length - 128 * b)
                d = 128 * b - r0
                t = s_ref[e, r0 : r0 + RT, 128 * b : 128 * b + w]
                m = bar[:, 128 * b : 128 * b + w]
                if d in OFFSETS:
                    t = t + ord_ref[e, OFFSETS.index(d)][:, :w] + m
                else:
                    t = t + (m + (left if d < 0 else right))
                parts.append(t)
            t = jnp.concatenate(parts, 1)
            top = jnp.max(t, axis=1, keepdims=True)
            ex = jnp.exp(t - top)
            total = jnp.sum(ex, axis=1, keepdims=True)
            p_ref[e, r0 : r0 + RT, :] = (ex * (1.0 / total)).astype(BF)
        outs.append(dot(p_ref[e], v_ref[:, pair]))
    o_ref[...] = jnp.where(lane < 64, outs[0], outs[1]).astype(BF)


def front(info, edge, blocks, ct, cp, pm, turn, wq, bq, wk, wv, bv, oh, wt, od, block):
    n_seq = len(blocks)
    stretch, width = blocks[0].shape
    length = n_seq * stretch
    heads = wt.shape[0]
    sds = jax.ShapeDtypeStruct
    flops = 2 * length * width * width * 3 + heads * 2 * length * length * (384 + 128)
    return pl.pallas_call(
        functools.partial(front_kernel, n_seq=n_seq, block=block),
        out_shape=(sds((length, width), F32), sds((width, length), BF)) + (sds((length, width), BF),) * 3
        + (sds((heads, length, length), BF), sds((length, width), BF)),
        grid_spec=pltpu.PrefetchScalarGridSpec(
            num_scalar_prefetch=2, grid=(heads // 2,),
            in_specs=[whole((stretch, width))] * n_seq
            + [whole(ct.shape), whole(cp.shape), whole(pm.shape), whole(turn.shape), pl.BlockSpec(memory_space=pl.ANY), whole(bq.shape), pl.BlockSpec(memory_space=pl.ANY),
               pl.BlockSpec(memory_space=pl.ANY), whole(bv.shape), whole(oh.shape),
               pl.BlockSpec((2, 128, 256), lambda g, *_: (g, 0, 0)),
               pl.BlockSpec((2, len(OFFSETS), RT, 128), lambda g, *_: (g, 0, 0, 0))],
            out_specs=[pl.BlockSpec(memory_space=pl.ANY)] * 5
            + [pl.BlockSpec((2, length, length), lambda g, *_: (g, 0, 0)), pl.BlockSpec((length, 128), lambda g, *_: (0, g))],
            scratch_shapes=[pltpu.VMEM((length, width), BF), pltpu.VMEM((length + 2 * EDGE, width), F32), pltpu.VMEM((length + 2 * EDGE, width), F32),
                            pltpu.VMEM((length, 384), BF), pltpu.VMEM((2, length, 384), BF), pltpu.VMEM((2, length, length), F32), pltpu.VMEM((width, length), BF),
                            pltpu.VMEM((length, width), F32), pltpu.VMEM((width, length), BF)]
            + [pltpu.VMEM((length, width), BF)] * 3 + [pltpu.VMEM((width, width), BF)] * 3
            + [pltpu.SemaphoreType.DMA((3,)), pltpu.SemaphoreType.DMA((5,))],
        ),
        cost_estimate=pl.CostEstimate(flops=25_000_000_000, bytes_accessed=8 << 20, transcendentals=0),
        name="front",
    )(info, edge, *blocks, ct, cp, pm, turn, wq, bq, wk, wv, bv, oh, wt, od)


def norm_stats(u):
    mean = jnp.mean(u, axis=1, keepdims=True)
    c = u - mean
    rs = lax.rsqrt(jnp.mean(c * c, axis=1, keepdims=True) + EPS)
    return c * rs, rs


def norm_back(u, xhat, rs):
    return rs * (u - jnp.mean(u, axis=1, keepdims=True) - xhat * jnp.mean(u * xhat, axis=1, keepdims=True))


def gelu_pair(x):
    t = 1.0 / (1.0 + jnp.abs(x) * (ERF_P * 0.7071067811865476))
    bell = jnp.exp2(x * x * -0.7213475204444817)
    q = jnp.full_like(t, 0.5 * ERF_Q[7])
    for k in range(6, -1, -1):
        q = q * t + 0.5 * ERF_Q[k]
    tail = q * t * bell
    cdf = jnp.where(x < 0, tail, 1.0 - tail)
    return x * cdf, cdf + x * bell * 0.3989422804014327


def middle_kernel(info_ref, *refs, n_seq, tiles, tile, block):
    cots = refs[:n_seq]
    (att_ref, set_ref, wo_ref, bo_ref, ng_ref, ns_ref, w1_ref, b1_ref, w2_ref, b2_ref, fg_ref, fs_ref, turn_ref) = refs[n_seq : n_seq + 13]
    outs = refs[n_seq + 13 :]
    mixed = outs[:n_seq]
    (xh_any, rs_any, fl_any, gp_ref, ds_any, dr_any, gk_ref, gs_ref, sm_ref, act_ref, fn_ref, acc_ref, cot_ref, mix_ref, e_ref, g_ref, b1_rows,
     xh_ref, rs_ref, fl_ref, ds_ref, dr_ref, cot_sems, norm_sems, out_sems) = outs[n_seq:]
    i = pl.program_id(0)
    length, width = fl_ref.shape
    place = info_ref[0]
    stretch = length // n_seq
    block_of = lambda ref, d: ref.at[pl.ds(pl.multiple_of(lax.rem(place + d, n_seq) * stretch, 16), stretch), :]
    arriving = moves([(cots[d], block_of(cot_ref, n_seq - d)) for d in range(n_seq)], cot_sems)
    normed = moves([(xh_ref, xh_any), (rs_ref, rs_any), (fl_ref, fl_any)], norm_sems)
    leaving = moves([(ds_ref, ds_any), (dr_ref, dr_any)] + [(block_of(mix_ref, d), mixed[d]) for d in range(n_seq)], out_sems)

    @pl.when(i == 0)
    def _():
        start(arriving)
        for c in range(width // 256):
            s = slice(256 * c, 256 * (c + 1))
            acc_ref[:, s] = dot(att_ref[...], wo_ref[:, s])

        def chunk(j, carry):
            r = pl.ds(pl.multiple_of(j * LR, LR), LR)
            u = set_ref[r, :] + (acc_ref[r, :] + line(bo_ref))
            xhat, rs = norm_stats(u)
            xh_ref[r, :] = xhat
            rs_ref[r, :] = jnp.broadcast_to(rs, (LR, 128))
            fn = xhat * line(ng_ref) + line(ns_ref)
            fn_ref[r, :] = fn
            fl_ref[r, :] = fn.astype(BF)
            acc_ref[r, :] = jnp.broadcast_to(line(b2_ref), (LR, width))
            return carry

        lax.fori_loop(0, length // LR, chunk, 0, unroll=2)
        start(normed)
        for t in range(tiles):
            b1_rows[t] = line(b1_ref, slice(t * tile, (t + 1) * tile))

    @pl.when(i < tiles)
    def _():
        half = tile // 3
        for n in range(3):
            e_ref[n] = dot(fl_ref[...], w1_ref[:, n * half : (n + 1) * half])
        for n in range(3):
            s = slice(n * half, (n + 1) * half)
            act, gp = gelu_pair(e_ref[n] + b1_rows[i, :, s])
            act_ref[i, :, s] = act.astype(BF)
            gp_ref[:, s] = gp.astype(gp_ref.dtype)
        for c in range(width // 256):
            s = slice(256 * c, 256 * (c + 1))
            acc_ref[:, s] += dot(act_ref[i], w2_ref[:, s])

    @pl.when(i == tiles - 1)
    def _():
        wait(arriving)

        def chunk(j, sums):
            r0 = pl.multiple_of(j * LR, LR)
            r = pl.ds(r0, LR)
            second = fn_ref[r, :] + acc_ref[r, :]
            xhat, rs = norm_stats(second)
            mix_ref[r, :] = (xhat * line(fg_ref) + line(fs_ref)).astype(BF)
            cot = cot_ref[r, :].astype(F32)
            back = norm_back(cot * line(fg_ref), xhat, rs)
            ds_ref[r, :] = back
            low = back.astype(BF)
            dr_ref[r, :] = low
            return (sums[0] + fold(cot * xhat), sums[1] + fold(cot), sums[2] + fold(low.astype(F32)))

        sums = lax.fori_loop(0, length // LR, chunk, (jnp.zeros((8, width), F32),) * 3, unroll=2)
        for n in range(3):
            sm_ref[n : n + 1, :] = row_sum(sums[n])
        start(leaving)

    @pl.when(i == pl.num_programs(0) - 1)
    def _():
        wait(normed)
        wait(leaving)

    @pl.when(i >= tiles)
    def _():
        grad = t_dot(act_ref[i - tiles], dr_ref[...]).astype(BF)
        if 2 * block == tile:
            g_ref[...] = grad
            core = info_ref[2]
            gk_ref[...] = g_ref[pl.ds(pl.multiple_of(core * block, block), block), :]
            gs_ref[...] = g_ref[pl.ds(pl.multiple_of((1 - core) * block, block), block), :]
        else:
            turned = dot(turn_ref[...], grad).astype(BF)
            gk_ref[...] = turned[: tile // 2]
            gs_ref[...] = turned[tile // 2 :]


def middle(info, cots, att, settled, wo, bo, ng, ns, w1, b1, w2, b2, fg, fs, turn, block):
    tile = w1.shape[0]
    n_seq = len(cots)
    stretch, width = cots[0].shape
    length = n_seq * stretch
    ff = w1.shape[1]
    tiles = ff // tile
    sds = jax.ShapeDtypeStruct
    early = lambda i: jnp.minimum(i, tiles - 1)
    late = lambda i: jnp.maximum(i - tiles, 0)
    return pl.pallas_call(
        functools.partial(middle_kernel, n_seq=n_seq, tiles=tiles, tile=tile, block=block),
        out_shape=(sds((stretch, width), BF),) * n_seq
        + (sds((length, width), F32), sds((length, 128), F32), sds((length, width), BF), sds((length, ff), BF),
           sds((length, width), F32), sds((length, width), BF), sds((ff // 2, width), BF), sds((ff // 2, width), BF), sds((8, width), F32)),
        grid_spec=pltpu.PrefetchScalarGridSpec(
            num_scalar_prefetch=1, grid=(2 * tiles,),
            in_specs=[pl.BlockSpec(memory_space=pl.ANY)] * n_seq
            + [whole(att.shape), whole(settled.shape), whole(wo.shape), whole(bo.shape), whole(ng.shape), whole(ns.shape),
               pl.BlockSpec((width, tile), lambda i, *_: (0, early(i))), whole(b1.shape),
               pl.BlockSpec((tile, width), lambda i, *_: (early(i), 0)), whole(b2.shape), whole(fg.shape), whole(fs.shape), whole(turn.shape)],
            out_specs=[pl.BlockSpec(memory_space=pl.ANY)] * (n_seq + 3)
            + [pl.BlockSpec((length, tile), lambda i, *_: (0, early(i))), pl.BlockSpec(memory_space=pl.ANY), pl.BlockSpec(memory_space=pl.ANY),
               pl.BlockSpec((tile // 2, width), lambda i, *_: (late(i), 0)), pl.BlockSpec((tile // 2, width), lambda i, *_: (late(i), 0)),
               whole_out((8, width))],
            scratch_shapes=[pltpu.VMEM((tiles, length, tile), BF), pltpu.VMEM((length, width), F32), pltpu.VMEM((length, width), F32),
                            pltpu.VMEM((length, width), BF), pltpu.VMEM((length, width), BF), pltpu.VMEM((3, length, tile // 3), F32),
                            pltpu.VMEM((tile, width), BF), pltpu.VMEM((tiles, 1, tile), F32),
                            pltpu.VMEM((length, width), F32), pltpu.VMEM((length, 128), F32), pltpu.VMEM((length, width), BF),
                            pltpu.VMEM((length, width), F32), pltpu.VMEM((length, width), BF),
                            pltpu.SemaphoreType.DMA((n_seq,)), pltpu.SemaphoreType.DMA((3,)), pltpu.SemaphoreType.DMA((2 + n_seq,))],
        ),
        cost_estimate=pl.CostEstimate(flops=35_000_000_000, bytes_accessed=8 << 20, transcendentals=0),
        name="middle",
    )(info, *cots, att, settled, wo, bo, ng, ns, w1, b1, w2, b2, fg, fs, turn)


def back_kernel(info_ref, *refs, tiles, last, block):
    core = info_ref[2]
    if last:
        (dr_ref, in_ref, w2_ref, gp_ref, w1_ref, fl_ref, turn_ref, xh_any, rs_any, ng_ref, att_any, wo_any) = refs[:12]
        (gk_ref, gs_ref, be_ref, df_ref, da_ref, sm_ref, flt_ref, raw_ref, acc_ref, db_ref,
         xh_ref, rs_ref, att_ref, wo_ref, sems) = refs[-15:]
        arriving = moves([(xh_any, xh_ref), (rs_any, rs_ref), (att_any, att_ref), (wo_any, wo_ref)], sems)
    else:
        (dr_ref, in_ref, w2_ref, gp_ref, w1_ref, fl_ref, turn_ref) = refs[:7]
        (gk_ref, gs_ref, be_ref, acc_ref, flt_ref, raw_ref) = refs[-6:]
    i = pl.program_id(0)
    length, width = dr_ref.shape

    @pl.when(i == 0)
    def _():
        if last:
            start(arriving)
        turned_transpose(fl_ref, turn_ref, core, block, flt_ref, raw_ref)
        acc_ref[...] = in_ref[...]

    @pl.when(i < tiles)
    def _():
        de = dot_t(dr_ref[...], w2_ref[...]) * gp_ref[...].astype(F32)
        de = de.astype(BF)
        be_ref[...] = row_sum(de.astype(F32))
        grad = dot(flt_ref[...], de).astype(BF)
        gk_ref[...] = grad[: width // 2]
        gs_ref[...] = grad[width // 2 :]
        acc_ref[...] += dot_t(de, w1_ref[...])

    if not last:
        return

    @pl.when(i == tiles)
    def _():
        wait(arriving)

        def chunk(j, sums):
            r = pl.ds(pl.multiple_of(j * LR, LR), LR)
            first = acc_ref[r, :]
            xhat = xh_ref[r, :]
            back = norm_back(first * line(ng_ref), xhat, rs_ref[r, 0:1])
            df_ref[r, :] = back
            low = back.astype(BF)
            db_ref[r, :] = low
            return (sums[0] + fold(first * xhat), sums[1] + fold(first), sums[2] + fold(low.astype(F32)))

        sums = lax.fori_loop(0, length // LR, chunk, (jnp.zeros((8, width), F32),) * 3, unroll=2)
        for n in range(3):
            sm_ref[n : n + 1, :] = row_sum(sums[n])
        da_ref[...] = dot_t(db_ref[...], wo_ref[...]).astype(BF)
        turned_transpose(att_ref, turn_ref, core, block, flt_ref, raw_ref)
        grad = dot(flt_ref[...], db_ref[...]).astype(BF)
        gk_ref[...] = grad[: width // 2]
        gs_ref[...] = grad[width // 2 :]


def back(info, block, first, tiles, dr, acc, w2, gp, w1, fl, turn, filled=(), norm=None):
    length, width = dr.shape
    ff = w1.shape[1]
    last = norm is not None
    sds = jax.ShapeDtypeStruct
    at = lambda i: jnp.minimum(i, tiles - 1) + first
    grad = pl.BlockSpec((width // 2, width), lambda i, *_: (0, i + first))
    args = [dr, acc, w2, gp, w1, fl, turn] + list(norm or ())
    out_shape = [sds((width // 2, ff + width), BF), sds((width // 2, ff + width), BF), sds((1, ff), F32), sds((length, width), F32)]
    out_specs = [grad, grad, pl.BlockSpec((1, width), lambda i, *_: (0, at(i))), whole_out((length, width))]
    scratch = [pltpu.VMEM((width, length), BF), pltpu.VMEM((width, length), BF)]
    if last:
        out_shape += [sds((length, width), BF), sds((8, width), F32)]
        out_specs += [whole_out((length, width)), whole_out((8, width))]
        scratch += [pltpu.VMEM((length, width), F32), pltpu.VMEM((length, width), BF), pltpu.VMEM((length, width), F32),
                    pltpu.VMEM((length, 128), F32), pltpu.VMEM((length, width), BF), pltpu.VMEM((width, width), BF),
                    pltpu.SemaphoreType.DMA((4,))]
    return pl.pallas_call(
        functools.partial(back_kernel, tiles=tiles, last=last, block=block),
        out_shape=tuple(out_shape),
        grid_spec=pltpu.PrefetchScalarGridSpec(
            num_scalar_prefetch=1, grid=(tiles + last,),
            in_specs=[whole(dr.shape), whole(acc.shape), pl.BlockSpec((width, width), lambda i, *_: (at(i), 0)),
                      pl.BlockSpec((length, width), lambda i, *_: (0, at(i))), pl.BlockSpec((width, width), lambda i, *_: (0, at(i)))]
            + [pl.BlockSpec(memory_space=pl.ANY) if n in (7, 8, 10, 11) else whole(x.shape) for n, x in enumerate(args) if n >= 5]
            + [pl.BlockSpec(memory_space=pl.ANY)] * len(filled),
            out_specs=out_specs,
            scratch_shapes=scratch,
        ),
        input_output_aliases={1 + len(args) + n: n for n in range(len(filled))},
        cost_estimate=pl.CostEstimate(flops=12_000_000_000, bytes_accessed=8 << 20, transcendentals=0),
        name="back",
    )(info, *args, *filled)


def diagonals(x):
    wide = jnp.concatenate([x, jnp.zeros_like(x)], 1)
    return row_sum(pltpu.roll(wide, 0, 1, stride=1, stride_axis=0))


def hi_lo(x):
    hi = x.astype(BF)
    return jnp.concatenate([hi, (x - hi.astype(F32)).astype(BF)], 1)


def heads_kernel(*refs):
    (p_ref, q_ref, k_ref, v_ref, do_ref, o_ref, oh_ref, oht_ref, et_any, wq_ref, wk_ref, wv_ref, in_any) = refs[:13]
    (gk_ref, gs_ref, qb_ref, diag_ref, acc_ref, va_ref, rhs_ref, dsc_ref, dp_ref, w_ref, d_ref, et_ref, sems) = refs[-13:]
    arriving = moves([(et_any, et_ref), (in_any, acc_ref)], sems)
    g = pl.program_id(0)
    length = q_ref.shape[0]
    lane = lax.broadcasted_iota(jnp.int32, (length, 128), 1)

    @pl.when(g == 0)
    def _():
        va_ref[:, 128:256] = jnp.where(lane < 2, 1.0, 0.0).astype(BF)
        rhs_ref[:, 128:256] = oh_ref[...]
        start(arriving)

    va_ref[:, 0:128] = v_ref[...]
    rhs_ref[:, 0:128] = k_ref[...]
    cols = (length + 127) // 128
    flip = (lax.broadcasted_iota(jnp.int32, (RT, RT), 0) + lax.broadcasted_iota(jnp.int32, (RT, RT), 1) == RT - 1).astype(F32).astype(BF)
    do = do_ref[...]
    prod = do.astype(F32) * o_ref[...].astype(F32)
    res = []
    for e in range(2):
        mine = (lane < 64) if e == 0 else (lane >= 64)
        inner = -jnp.sum(jnp.where(mine, prod, 0.0), axis=1, keepdims=True)
        hi = inner.astype(BF)
        lo = inner - hi.astype(F32)
        ext = jnp.where(lane == 0, hi.astype(F32), jnp.where(lane == 1, lo, 0.0)).astype(BF)
        da = jnp.concatenate([jnp.where(mine, do, jnp.zeros((), BF)), ext], 1)
        dp_ref[e] = dot_t(da, va_ref[...])
    for e in range(2):
        sums = {}
        for a in range(length // RT):
            r0 = a * RT
            ds = p_ref[e, r0 : r0 + RT, :].astype(F32) * dp_ref[e, r0 : r0 + RT, :]
            dsc_ref[e, r0 : r0 + RT, :] = ds.astype(BF)
            for b in range(cols):
                w = min(128, length - 128 * b)
                d = 128 * b - r0
                t = ds[:, 128 * b : 128 * b + w]
                if w < 128:
                    t = jnp.concatenate([t, jnp.zeros((RT, 128 - w), F32)], 1)
                key = OFFSETS.index(d) if d in OFFSETS else (4 if d < 0 else 5)
                sums[key] = sums[key] + t if key in sums else t
        for n in range(4):
            turned = dot(flip, hi_lo(sums[n]))
            diag_ref[e, n : n + 1, :] = diagonals(turned[:, 0:128] + turned[:, 128:256])
        diag_ref[e, 4:5, 0:128] = row_sum(sums[4])
        diag_ref[e, 4:5, 128:256] = row_sum(sums[5])
        r = dot(dsc_ref[e], rhs_ref[...])
        hh = dot(oht_ref[...], hi_lo(r[:, 128:256]))
        hist = hh[:, 0:128] + hh[:, 128:256]
        half = lane[:BOX] < BOX
        diag_ref[e, 5:6, :] = diagonals(jnp.where(half, hist[:BOX], 0.0))
        diag_ref[e, 6:7, :] = diagonals(jnp.where(half, 0.0, hist[BOX:]))
        diag_ref[e, 7:8, :] = jnp.zeros((1, 256), F32)
        dk = t_dot(dsc_ref[e], q_ref[...])
        dv = t_dot(p_ref[e], do)
        res.append((r[:, 0:128], dk, dv))
    first = lane < 64
    dq = (jnp.where(first, res[0][0], res[1][0]) * SCALE).astype(BF)
    dk = jnp.where(first, res[0][1], res[1][1]).astype(BF)
    dv = jnp.where(first, res[0][2], res[1][2]).astype(BF)

    @pl.when(g == 0)
    def _():
        wait(arriving)

    d_ref[:, 0:128] = dq
    d_ref[:, 128:256] = dk
    d_ref[:, 256:384] = dv
    qb_ref[0:1, :] = row_sum(dq.astype(F32))
    qb_ref[1:2, :] = row_sum(dv.astype(F32))
    w_ref[:, 0:128] = wq_ref[...]
    w_ref[:, 128:256] = wk_ref[...]
    w_ref[:, 256:384] = wv_ref[...]
    grad = dot(et_ref[...], d_ref[...]).astype(BF)
    gk_ref[...] = grad[: grad.shape[0] // 2]
    gs_ref[...] = grad[grad.shape[0] // 2 :]
    acc_ref[...] += dot_t(d_ref[...], w_ref[...])


def heads_back(first, count, probs, q, k, v, do, o, oh, oht, et, wq, wk, wv, acc, filled=()):
    heads = probs.shape[0]
    length, width = q.shape
    steps = count // 2
    base = first // 2
    sds = jax.ShapeDtypeStruct
    col = pl.BlockSpec((length, 128), lambda g: (0, g + base))
    wcol = pl.BlockSpec((width, 128), lambda g: (0, g + base))
    flops = 2 * length * width * 64 * count * 6 + count * 2 * length * length * (256 + 256 + 128 + 128)
    return pl.pallas_call(
        heads_kernel,
        out_shape=(sds((width // 2, 3 * width), BF), sds((width // 2, 3 * width), BF), sds((8, width), F32), sds((heads, 8, 256), F32), sds((length, width), F32)),
        grid=(steps,),
        in_specs=[pl.BlockSpec((2, length, length), lambda g: (g + base, 0, 0)), col, col, col, col, col, whole(oh.shape), whole(oht.shape),
                  pl.BlockSpec(memory_space=pl.ANY), wcol, wcol, wcol] + [pl.BlockSpec(memory_space=pl.ANY)] * (1 + len(filled)),
        out_specs=[pl.BlockSpec((width // 2, 384), lambda g: (0, g + base)), pl.BlockSpec((width // 2, 384), lambda g: (0, g + base)),
                   pl.BlockSpec((8, 128), lambda g: (0, g + base)), pl.BlockSpec((2, 8, 256), lambda g: (g + base, 0, 0)), whole_out((length, width))],
        input_output_aliases={13 + n: n for n in range(len(filled))},
        scratch_shapes=[pltpu.VMEM((length, 256), BF), pltpu.VMEM((length, 256), BF), pltpu.VMEM((2, length, length), BF),
                        pltpu.VMEM((2, length, length), F32), pltpu.VMEM((width, 384), BF), pltpu.VMEM((length, 384), BF),
                        pltpu.VMEM((width, length), BF), pltpu.SemaphoreType.DMA((2,))],
        cost_estimate=pl.CostEstimate(flops=20_000_000_000, bytes_accessed=8 << 20, transcendentals=0),
        name="heads_back",
    )(probs, q, k, v, do, o, oh, oht, et, wq, wk, wv, acc, *filled)


def encode_kernel(info_ref, *refs, n_seq):
    blocks = refs[:n_seq]
    in_ref, ct_ref, cp_ref, pm_ref, sm_ref, sm2_ref, be_ref, qb_ref = refs[n_seq : n_seq + 8]
    outs = refs[n_seq + 8 :]
    grads = outs[:n_seq]
    small_ref, acc_ref, gs_ref, ms_ref, gt_ref = outs[n_seq:]
    length, width = in_ref.shape
    place, count = info_ref[0], info_ref[1]
    acc_ref[...] = in_ref[...]
    small_ref[...] = jnp.zeros_like(small_ref)
    small_ref[0:3, :] = sm_ref[0:3, :]
    small_ref[3:6, :] = sm2_ref[0:3, :]
    small_ref[6:8, :] = qb_ref[0:2, :]
    tiles = be_ref.shape[1] // width
    for t in range(tiles):
        small_ref[8 + t : 9 + t, :] = be_ref[:, t * width : (t + 1) * width]
    taps, cells = 8 + tiles, 15 + tiles
    zero = jnp.zeros((EDGE, width), F32)
    gs_ref[0:EDGE, :] = zero
    gs_ref[EDGE + length :, :] = zero
    ms_ref[0:EDGE, :] = zero
    ms_ref[EDGE + length :, :] = zero
    gather_page(ms_ref, EDGE, place, n_seq, blocks[0], blocks[1:])
    for c in lanes(width):
        tok = ms_ref[EDGE + TEXT - 8 : EDGE + TEXT + CELLS + 8, c]
        own = acc_ref[TEXT : TEXT + CELLS, c]
        window = jnp.concatenate([acc_ref[TEXT - 8 : TEXT + CELLS, c], jnp.zeros((8, 128), F32)], 0)
        term = jnp.zeros((CELLS, 128), F32)
        for n in range(9):
            off = (n // 3 - 1) * GRID + n % 3 - 1
            term = term + shift_rows(window, -off, CELLS) * (cp_ref[n : n + 1, c] * pm_ref[:, 8 - n : 9 - n])
            small_ref[cells + n : cells + n + 1, c] = row_sum(own * shift_rows(tok, off, CELLS) * pm_ref[:, n : n + 1])
        gt_ref[:, c] = term

    def split_chunk(j, carry):
        r0 = pl.multiple_of(j * RT, RT)
        keep = (r0 + lax.broadcasted_iota(jnp.int32, (RT, 128), 0)) < count
        for c in lanes(width):
            dset = acc_ref[pl.ds(r0, RT), c]
            gs_ref[pl.ds(r0 + EDGE, RT), c] = jnp.where(keep, dset, 0.0)
            ms_ref[pl.ds(r0 + EDGE, RT), c] = jnp.where(keep, ms_ref[pl.ds(r0 + EDGE, RT), c], 0.0)
        return carry

    lax.fori_loop(0, length // RT, split_chunk, 0)
    for c in lanes(width):
        acc_ref[TEXT : TEXT + CELLS, c] = acc_ref[TEXT : TEXT + CELLS, c] + gt_ref[:, c]

    def conv_chunk(j, sums):
        r0 = pl.multiple_of(j * RT, RT)
        keep = (r0 + lax.broadcasted_iota(jnp.int32, (RT, 128), 0)) < count
        out = []
        for n, c in enumerate(lanes(width)):
            window = gs_ref[pl.ds(r0 + EDGE - 8, RT + 16), c]
            own = ms_ref[pl.ds(r0 + EDGE, RT), c]
            term = None
            for m, d in enumerate(TAPS):
                moved = shift_rows(window, -d, RT)
                part = moved * ct_ref[m : m + 1, c]
                term = part if term is None else term + part
                out.append(sums[n * len(TAPS) + m] + row_sum(moved * own))
            acc_ref[pl.ds(r0, RT), c] = acc_ref[pl.ds(r0, RT), c] + jnp.where(keep, term, 0.0)
        return tuple(out)

    zeros = (jnp.zeros((1, 128), F32),) * (len(TAPS) * (width // 128))
    sums = lax.fori_loop(0, length // RT, conv_chunk, zeros)
    for n, c in enumerate(lanes(width)):
        for m in range(len(TAPS)):
            small_ref[taps + m : taps + m + 1, c] = sums[n * len(TAPS) + m]
    stretch = length // n_seq
    for d in range(n_seq):
        dest = lax.rem(place + d, n_seq)
        grads[d][...] = acc_ref[pl.ds(pl.multiple_of(dest * stretch, 16), stretch), :].astype(BF)


def encode_back(info, blocks, d_settled, ct, cp, pm, sm, sm2, be, qb):
    n_seq = len(blocks)
    stretch, width = blocks[0].shape
    length = n_seq * stretch
    sds = jax.ShapeDtypeStruct
    rows = 24 + be.shape[1] // width
    rows += 8 - rows % 8
    return pl.pallas_call(
        functools.partial(encode_kernel, n_seq=n_seq),
        out_shape=(sds((stretch, width), BF),) * n_seq + (sds((rows, width), F32),),
        grid_spec=pltpu.PrefetchScalarGridSpec(
            num_scalar_prefetch=1, grid=(1,),
            in_specs=[whole((stretch, width))] * n_seq + [whole(d_settled.shape), whole(ct.shape), whole(cp.shape), whole(pm.shape), whole(sm.shape), whole(sm2.shape), whole(be.shape), whole(qb.shape)],
            out_specs=[whole_out((stretch, width))] * n_seq + [whole_out((rows, width))],
            scratch_shapes=[pltpu.VMEM((length, width), F32), pltpu.VMEM((length + 2 * EDGE, width), F32),
                            pltpu.VMEM((length + 2 * EDGE, width), F32), pltpu.VMEM((CELLS, width), F32)],
        ),
        cost_estimate=pl.CostEstimate(flops=10_000_000_000, bytes_accessed=8 << 20, transcendentals=0),
        name="encode_back",
    )(info, *blocks, d_settled, ct, cp, pm, sm, sm2, be, qb)


def turn_matrix(width, n, core):
    block, half = width // n, width // 2
    r = jnp.arange(width, dtype=jnp.int32)
    inner = jnp.where(r < half, r, r - half)
    parity = jnp.where(r < half, core, 1 - core)
    source = (2 * (inner // block) + parity) * block + inner % block
    return (source[:, None] == r[None]).astype(BF)


def restack_kernel(info_ref, *refs, n, layout):
    parts, outs = refs[:n], refs[n:]
    for d, part in enumerate(parts):
        source = lax.rem(info_ref[0] - d + n, n)
        for out, pieces in zip(outs, layout):
            at = 0
            for start, width in pieces:
                out[source, :, at : at + width] = part[:, start : start + width].astype(out.dtype)
                at += width


def restack(info, parts, dtype, layout=None):
    n = len(parts)
    rows, cols = parts[0].shape
    layout = layout or [[(0, cols)]]
    outs = pl.pallas_call(
        functools.partial(restack_kernel, n=n, layout=layout),
        out_shape=[jax.ShapeDtypeStruct((n, rows, sum(w for _, w in pieces)), dtype) for pieces in layout],
        in_specs=[pl.BlockSpec(memory_space=pltpu.SMEM)] + [pl.BlockSpec(memory_space=pltpu.VMEM)] * n,
        out_specs=[pl.BlockSpec(memory_space=pltpu.VMEM)] * len(layout),
        cost_estimate=pl.CostEstimate(flops=1000, bytes_accessed=1000, transcendentals=0),
        name="restack",
    )(info, *parts)
    return outs


def unpack_kernel(small_ref, *outs, heads, tiles):
    gct, gcp, qb, vb, ob, order, horiz, vert, ng, ns, be, rb, fg, fs = outs
    for row, out in ((0, fg), (1, fs), (2, rb), (3, ng), (4, ns), (5, ob), (6, qb), (7, vb)):
        out[...] = small_ref[row, :]
    width = small_ref.shape[1]
    for t in range(tiles):
        be[t * width : (t + 1) * width] = small_ref[8 + t, :]
    taps, cells, bias = 8 + tiles, 15 + tiles, 24 + tiles
    for s in range(3):
        for t in range(3):
            gct[s, t, :] = small_ref[taps + 3 + (t - 1) * (s + 1), :]
            gcp[s, t, :] = small_ref[cells + 3 * s + t, :]
    nb = order.shape[1]
    per = width // 128
    for h in range(heads):
        row, at = bias + h // per, 128 * (h % per)
        for n, out in enumerate((order, horiz, vert)):
            out[h, :] = small_ref[row, at + n * nb : at + (n + 1) * nb]


def unpack(small, heads, nb, ff):
    width = small.shape[1]
    sds = lambda *shape: jax.ShapeDtypeStruct(shape, F32)
    vec = sds(width)
    return pl.pallas_call(
        functools.partial(unpack_kernel, heads=heads, tiles=ff // width),
        out_shape=(sds(3, 3, width), sds(3, 3, width), vec, vec, vec, sds(heads, nb), sds(heads, nb), sds(heads, nb),
                   vec, vec, sds(ff), vec, vec, vec),
        cost_estimate=pl.CostEstimate(flops=1000, bytes_accessed=1000, transcendentals=0),
        name="unpack",
    )(small)


def one_hot_rows(ids, size):
    return (ids.reshape(1, -1) == jnp.arange(size, dtype=jnp.int32)[:, None]).astype(F32)


def tables(rel_order, rel_horiz, rel_vert):
    heads, nb = rel_order.shape
    high = lax.Precision.HIGHEST
    a = jnp.arange(BOX, dtype=jnp.int32)
    cell = one_hot_rows(jnp.clip(a[None, :] - a[:, None], -SPAN, SPAN) + SPAN, nb)

    def split(table):
        x = jnp.dot(table, cell, precision=high).reshape(heads, BOX, BOX)
        top = lax.reduce_precision(x, 8, 7)
        return top, x - top

    (hh, hl), (vh, vl) = split(rel_horiz), split(rel_vert)
    zero = jnp.zeros_like(hh)
    wt = jnp.concatenate([jnp.concatenate([hh, zero, hl, zero], 2), jnp.concatenate([zero, vh, zero, vl], 2)], 1).astype(BF)
    i = jnp.arange(RT, dtype=jnp.int32)[:, None]
    j = jnp.arange(128, dtype=jnp.int32)[None]
    band = jnp.stack([jnp.clip(d + j - i, -SPAN, SPAN) + SPAN for d in OFFSETS])
    od = jnp.dot(rel_order, one_hot_rows(band, nb), precision=high).reshape(heads, len(OFFSETS), RT, 128)
    edge = jnp.stack([rel_order[:, 0], rel_order[:, -1]], 1)
    return wt, od, edge


def bias_grads(diag, nb):
    heads = diag.shape[0]
    high = lax.Precision.HIGHEST
    at = jnp.arange(256, dtype=jnp.int32)
    step = at - (RT - 1)
    order_bins = jnp.stack([jnp.clip(d + step, -SPAN, SPAN) for d in OFFSETS] + [jnp.where(at < 128, -SPAN, SPAN)]) + SPAN
    order = jnp.dot(diag[:, :5].reshape(heads, -1), one_hot_rows(order_bins, nb).T, precision=high)
    flat = jnp.clip(step, -SPAN, SPAN) + SPAN
    horiz = jnp.dot(diag[:, 5], one_hot_rows(flat, nb).T, precision=high)
    low = jnp.clip(step - BOX, -SPAN, SPAN) + SPAN
    vert = jnp.dot(diag[:, 6], one_hot_rows(low, nb).T, precision=high)
    return order, horiz, vert


def patch_masks():
    g = jnp.arange(CELLS, dtype=jnp.int32)
    i, j = g // GRID, g % GRID
    cols = []
    for n in range(9):
        a, b = i + n // 3 - 1, j + n % 3 - 1
        cols.append((g < GRID * GRID) & (a >= 0) & (a < GRID) & (b >= 0) & (b < GRID))
    return jnp.pad(jnp.stack(cols, 1).astype(F32), ((0, 0), (0, 128 - 9)))


def text_taps(conv_text):
    rows = []
    for d in TAPS:
        if d == 0:
            rows.append(conv_text[0, 1] + conv_text[1, 1] + conv_text[2, 1])
        else:
            rows.append(conv_text[abs(d) - 1, 2 if d > 0 else 0])
    rows.append(jnp.zeros_like(rows[0]))
    return jnp.stack(rows)


def xor_pairs(n, bit):
    return [(i, i ^ bit) for i in range(n)]


def swap(value, axis, bit):
    return lax.ppermute(value, axis, xor_pairs(lax.axis_size(axis), bit))


def spread(blocks, after=None):
    n = lax.axis_size("seq")
    out = [blocks[0]]
    for d in range(1, n):
        out.append(lax.ppermute(blocks[d], "seq", [(i, (i + d) % n) for i in range(n)]))
    return out


def rotated(pages):
    n = lax.axis_size("seq")
    place = lax.axis_index("seq")
    return [lax.dynamic_index_in_dim(pages, lax.rem(place + d, n), 0, keepdims=False) for d in range(n)]


def total(terms):
    out = terms[0].astype(F32)
    for t in terms[1:]:
        out = out + t.astype(F32)
    return out.astype(BF)


class Reduction:
    def __init__(self, keep, send, line=False):
        self.line = line and lax.axis_size("seq") == 4
        n = lax.axis_size("pages")
        self.n = n
        self.page = lax.axis_index("pages")
        self.first = (self.page & 1) == 0
        self.bits = [1 << b for b in range(1, n.bit_length() - 1)]
        self.shape = (n // 2, keep.shape[0] * 2 // n, keep.shape[1])
        self.terms = [keep.reshape(self.shape)]
        self.send, self.at, self.name = send, 0, None

    def blocks(self, depth, other):
        up, down = self.bits[:depth], self.bits[::-1][:depth]
        out = []
        for k in range((self.n // 2) >> depth):
            pair = []
            for closed in (up, down):
                free = [b for b in self.bits if b not in closed]
                index = sum((((k >> i) & 1) * b) for i, b in enumerate(free))
                mine = sum(closed)
                flip = closed[-1] if other and closed else 0
                pair.append((index + ((self.page ^ flip) & mine)) // 2)
            out.append(jnp.where(self.first, *pair))
        return out

    def pick(self, depth, other):
        rows = []
        for k, block in enumerate(self.blocks(depth, other)):
            parts = []
            for t, term in enumerate(self.terms):
                have = max(t - 1, 0)
                if have == 0:
                    place = block
                else:
                    known = self.blocks(have, False)
                    place = sum(jnp.where(known[i] == block, i, 0) for i in range(len(known)))
                parts.append(lax.dynamic_index_in_dim(term, place, 0, keepdims=False))
            rows.append(total(parts))
        return jnp.stack(rows) if len(rows) > 1 else rows[0][None]

    def step(self):
        assert not self.over()
        at, last = self.at, len(self.bits)
        self.at += 1
        n = lax.axis_size("seq")
        ring = lambda d: [(i, (i + d) % n) for i in range(n)]
        place = lax.axis_index("seq")
        if at == 0:
            self.fresh = [swap(self.send, "pages", 1)]
        elif at <= last:
            self.terms.append(self.fresh[0].reshape((-1,) + self.shape[1:]))
            pairs = [(i, i ^ (self.bits[-at] if i & 1 else self.bits[at - 1])) for i in range(self.n)]
            self.fresh = [lax.ppermute(self.pick(at, True), "pages", pairs)]
        elif at == last + 1:
            self.terms.append(self.fresh[0].reshape((-1,) + self.shape[1:]))
            value = self.pick(last, False)[0]
            rows, cols = value.shape
            if self.line:
                self.own = value
                self.fresh = [lax.ppermute(value, "seq", [(0, 1), (3, 2)])]
                return
            quarters = value.reshape(n, rows // n, cols)
            piece = lambda d: lax.dynamic_index_in_dim(quarters, lax.rem(place + d, n), 0, keepdims=False)
            self.own = piece(0)
            self.fresh = [lax.ppermute(piece(d), "seq", ring(d)) for d in range(1, n)]
        else:
            self.own = total([self.own] + self.fresh)
            if self.line:
                self.fresh = [lax.ppermute(self.own, "seq", [(1, 2), (2, 1)] if at == last + 2 else [(1, 0), (2, 3)])]
                return
            self.fresh = [lax.ppermute(self.own, "seq", ring(d)) for d in range(1, n)]

    def over(self):
        return self.at == len(self.bits) + (4 if self.line else 3)

    def result(self, info, layout=None):
        if self.line:
            place = lax.axis_index("seq")
            return [jnp.where((place == 0) | (place == 3), self.fresh[0], self.own).astype(F32)]
        outs = restack(info, [self.own] + self.fresh, F32, layout)
        return [out.reshape(-1, out.shape[-1]) for out in outs]


def tie(value, *reductions):
    value, fresh, held = lax.optimization_barrier(
        (value, tuple(r.fresh for r in reductions), tuple(r.send for r in reductions)))
    for r, f, h in zip(reductions, fresh, held):
        r.fresh, r.send = f, h
    return value


def per_device(
    tokens, cotangent, conv_text, conv_patch, proj_query, bias_query, proj_key, proj_value, bias_value,
    proj_output, bias_output, rel_order, rel_horiz, rel_vert, norm_gain, norm_shift, expand_weight,
    expand_bias, reduce_weight, reduce_bias, final_gain, final_shift, text_count, box_left, box_top,
):
    pages_here, stretch, width = tokens.shape
    n_seq = lax.axis_size("seq")
    n_pages = lax.axis_size("pages")
    assert pages_here == n_seq and n_pages & (n_pages - 1) == 0
    place = lax.axis_index("seq")
    heads, nb = rel_order.shape
    ff = expand_weight.shape[1]
    pick = lambda a: lax.dynamic_index_in_dim(a, place, 0, keepdims=False)
    count, left, top = pick(text_count), pick(box_left), pick(box_top)
    blocks = spread(rotated(tokens))
    core = lax.axis_index("pages") & 1
    info = jnp.stack([place, count, core]).astype(jnp.int32)
    turn = turn_matrix(width, n_pages, core) if width // n_pages % 16 else jnp.zeros((8, 128), BF)
    cells = jnp.arange(BOX, dtype=jnp.int32)
    oh = jnp.concatenate([left[:, None] == cells[None], top[:, None] == cells[None]], 1).astype(BF)
    oht = jnp.concatenate([left[None] == cells[::-1, None], top[None] == cells[::-1, None]], 0).astype(BF)
    wt, od, edge = tables(rel_order, rel_horiz, rel_vert)
    pm, ct = patch_masks(), text_taps(conv_text)
    cp = jnp.pad(conv_patch.reshape(9, width), ((0, 7), (0, 0)))

    cot_out, blocks = lax.optimization_barrier((rotated(cotangent), blocks))
    cots = spread(cot_out)
    settled, et, q, k, v, probs, att = front(
        info, edge, blocks, ct, cp, pm, turn, proj_query, bias_query, proj_key, proj_value, bias_value, oh, wt, od, width // n_pages)
    *mixed, xh, rs, fl, gp, ds, dr, grk, grs, sm = middle(
        info, cots, att, settled, proj_output, bias_output, norm_gain, norm_shift, expand_weight,
        expand_bias, reduce_weight, reduce_bias, final_gain, final_shift, turn, ff // n_pages)
    c_reduce = Reduction(grk, grs)
    c_reduce.step()
    mixed = spread(mixed)
    done = back(info, width // n_pages, 0, 2, dr, ds, reduce_weight, gp, expand_weight, fl, turn)
    done = tie(done, c_reduce)
    c_reduce.step()
    done = back(info, width // n_pages, 2, ff // width - 2, dr, done[3], reduce_weight, gp, expand_weight, fl, turn, done[:3],
                (xh, rs, norm_gain, att, proj_output))
    done, mixed = tie((done, mixed), c_reduce)
    gek, ges, be, df, da, sm2 = done
    c_expand = Reduction(gek, ges)
    heads_of = lambda first, count, da, acc, filled=(): heads_back(
        first, count, probs, q, k, v, da, att, oh, oht, et, proj_query, proj_key, proj_value, acc, filled)
    cuts = (0, heads // 2, heads)
    c_reduce.step()
    c_expand.step()
    done = heads_of(0, cuts[1], da, df)
    done, da = tie((done, da), c_reduce, c_expand)
    for first, last in zip(cuts[1:-1], cuts[2:]):
        c_reduce.step()
        c_expand.step()
        done = heads_of(first, last - first, da, done[4], done[:4])
        done, da = tie((done, da), c_reduce, c_expand)
    gqk, gqs, qb, diag, acc = done
    c_qkv = Reduction(gqk, gqs)
    for r in (c_reduce, c_expand, c_qkv):
        if not r.over():
            r.step()
    *gts, small = encode_back(info, blocks, acc, ct, cp, pm, sm, sm2, be, qb)
    rounds = [("pages", 1 << b) for b in range(n_pages.bit_length() - 1)] + [("seq", 1 << b) for b in range(n_seq.bit_length() - 1)]
    hop = lambda d: lax.ppermute(gts[d], "seq", [(i, (i + d) % n_seq) for i in range(n_seq)])
    work = [c_reduce, c_expand, c_qkv]
    for r, name in zip(work, ("reduce", "expand", "qkv")):
        r.name = name
    bias = jnp.concatenate(bias_grads(diag, nb), 1)
    bias = jnp.pad(bias, ((0, 0), (0, 128 - 3 * nb))).reshape(-1, width)
    hops = {0: (1,), 1: (3,), 2: (2,)}
    turns = [rounds[1:2], rounds[2:3], rounds[:1] + rounds[3:4], rounds[4:]] if len(rounds) == 5 else [rounds]
    layouts = {
        "reduce": None,
        "expand": [[(0, ff)], [(ff, width)]],
        "qkv": [[(384 * p + 128 * n, 128) for p in range(heads // 2)] for n in range(3)],
    }
    ready = {}
    phase = 0
    while turns or not c_qkv.over():
        gts, small, bias, ready = tie((gts, small, bias, ready), *work)
        if phase == 0:
            small = lax.dynamic_update_slice(small, bias, (24 + ff // width, 0))
            ready["mixed"] = restack(info, mixed, BF)
        for r in work:
            if not r.over():
                r.step()
            elif r.own is not None and r is not c_qkv:
                ready[r.name] = r.result(info, layouts[r.name])
                r.own, r.fresh = None, []
        for d in hops.get(phase, ()):
            gts = [hop(d) if e == d else part for e, part in enumerate(gts)]
        for axis, bit in turns.pop(0) if turns else ():
            small = small + swap(small, axis, bit)
        phase += 1
    (mixed_out,) = ready["mixed"]
    (o_reduce,), (o_expand, o_output) = (
        ready[r.name] if r.name in ready else r.result(info, layouts[r.name]) for r in (c_reduce, c_expand))
    o_query, o_key, o_value = c_qkv.result(info, layouts["qkv"])
    (grad_tokens,) = restack(info, gts, F32)

    (g_conv_text, g_conv_patch, g_qb, g_vb, g_ob, g_order, g_horiz, g_vert, g_ng, g_ns, g_be, g_rb, g_fg, g_fs) = unpack(
        small, heads, nb, ff)
    return (
        mixed_out, grad_tokens, g_conv_text, g_conv_patch, o_query, g_qb, o_key, o_value, g_vb,
        o_output, g_ob, g_order, g_horiz, g_vert, g_ng, g_ns, o_expand, g_be, o_reduce, g_rb, g_fg, g_fs,
    )


def solution(mesh):
    placed = (
        P("pages", "seq", None),
        P("pages", "seq", None),
        P(),
        P(),
        P(),
        P(),
        P(),
        P(),
        P(),
        P(),
        P(),
        P(),
        P(),
        P(),
        P(),
        P(),
        P(),
        P(),
        P(),
        P(),
        P(),
        P(),
        P("pages"),
        P("pages", None),
        P("pages", None),
    )
    return jax.shard_map(
        per_device,
        mesh=mesh,
        in_specs=placed,
        out_specs=(
            P("pages", "seq", None),
            P("pages", "seq", None),
            P(),
            P(),
            P("pages", None),
            P(),
            P("pages", None),
            P("pages", None),
            P(),
            P("pages", None),
            P(),
            P(),
            P(),
            P(),
            P(),
            P(),
            P("pages", None),
            P(),
            P("pages", None),
            P(),
            P(),
            P(),
        ),
        check_vma=False,
    )
```

```python
import functools
import jax
import jax.numpy as jnp
from jax import lax
from jax.experimental import pallas as pl
from jax.experimental.pallas import tpu as pltpu
from jax.sharding import PartitionSpec as P

BF = jnp.bfloat16
F32 = jnp.float32
TEXT = 512
GRID = 7
SPAN = 16
EPS = 1e-06
SCALE = 0.125
NEG = -1e30
BOX = 64
RT = 64
LR = 32
EDGE = 16
CELLS = 56
OFFSETS = (-128, -64, 0, 64)
TAPS = (-3, -2, -1, 0, 1, 2, 3)
ERF_P = 0.33
ERF_Q = (0.18635791540145874, 0.1829543262720108, 0.20123349130153656, 0.047190189361572266,
         0.4085558354854584, -0.35120898485183716, 0.4602709114551544, -0.1353536993265152)


def dot(a, b):
    return jnp.dot(a, b, preferred_element_type=F32)


def dot_t(a, b):
    return lax.dot_general(a, b, (((1,), (1,)), ((), ())), preferred_element_type=F32)


def t_dot(a, b):
    return lax.dot_general(a, b, (((0,), (0,)), ((), ())), preferred_element_type=F32)


def whole(shape, buffers=1):
    return pl.BlockSpec(shape, lambda *_: (0,) * len(shape), pipeline_mode=pl.Buffered(buffers))


def whole_out(shape):
    return pl.BlockSpec(shape, lambda *_: (0,) * len(shape))


def lanes(n):
    return [slice(128 * c, 128 * (c + 1)) for c in range(n // 128)]


def line(ref, part=slice(None)):
    return ref[part].reshape(1, -1)


def row_sum(x):
    return jnp.sum(x, axis=0, keepdims=True)


def fold(x):
    out = x[:8]
    for r in range(8, x.shape[0], 8):
        out = out + x[r : r + 8]
    return out


def shift_rows(window, offset, rows):
    if offset == 0:
        return window[8 : 8 + rows]
    return pltpu.roll(window, (-offset) % window.shape[0], 0)[8 : 8 + rows]


def gather_page(dest, row0, place, n_seq, own, others):
    stretch = own.shape[0]
    for d, block in enumerate((own,) + tuple(others)):
        source = lax.rem(place - d + n_seq, n_seq)
        dest[pl.ds(pl.multiple_of(row0 + source * stretch, 16), stretch), :] = block[...].astype(dest.dtype)


def turned_transpose(x_ref, turn_ref, core, block, dest, raw):
    rows = dest.shape[0]
    if block % 16:
        dest[...] = dot_t(turn_ref[...], x_ref[...]).astype(BF)
        return
    raw[...] = jnp.transpose(x_ref[...])
    half = rows // 2
    for k in range(half // block):
        for side in range(2):
            parity = core if side == 0 else 1 - core
            source = pl.multiple_of((2 * k + parity) * block, 16)
            dest[side * half + k * block : side * half + (k + 1) * block, :] = raw[pl.ds(source, block), :]


def moves(pairs, sems):
    return [pltpu.make_async_copy(source, dest, sems.at[n]) for n, (source, dest) in enumerate(pairs)]


def start(copies):
    for c in copies:
        c.start()


def wait(copies):
    for c in copies:
        c.wait()


def front_kernel(info_ref, edge_ref, *refs, n_seq, block):
    blocks = refs[:n_seq]
    (ct_ref, cp_ref, pm_ref, turn_ref, wq_any, bq_ref, wk_any, wv_any, bv_ref, oh_ref, wt_ref, ord_ref,
     set_any, et_any, q_any, k_any, v_any, p_ref, o_ref,
     entry_ref, xs_ref, ms_ref, ka_ref, qa_ref, s_ref, raw_ref,
     set_ref, et_ref, q_ref, k_ref, v_ref, wq_ref, wk_ref, wv_ref, in_sems, out_sems) = refs[n_seq:]
    g = pl.program_id(0)
    arriving = moves([(wq_any, wq_ref), (wk_any, wk_ref), (wv_any, wv_ref)], in_sems)
    leaving = moves([(set_ref, set_any), (et_ref, et_any), (q_ref, q_any), (k_ref, k_any), (v_ref, v_any)], out_sems)
    length, width = entry_ref.shape
    place, count = info_ref[0], info_ref[1]

    @pl.when(g == 0)
    def _():
        start(arriving)
        zero = jnp.zeros((EDGE, width), F32)
        xs_ref[0:EDGE, :] = zero
        xs_ref[EDGE + length :, :] = zero
        ms_ref[0:EDGE, :] = zero
        ms_ref[EDGE + length :, :] = zero
        gather_page(xs_ref, EDGE, place, n_seq, blocks[0], blocks[1:])

        def mask_chunk(i, carry):
            r0 = pl.multiple_of(i * RT, RT)
            keep = (r0 + lax.broadcasted_iota(jnp.int32, (RT, 128), 0)) < count
            for c in lanes(width):
                ms_ref[pl.ds(r0 + EDGE, RT), c] = jnp.where(keep, xs_ref[pl.ds(r0 + EDGE, RT), c], 0.0)
            return carry

        lax.fori_loop(0, length // RT, mask_chunk, 0)

        def conv_chunk(i, carry):
            r0 = pl.multiple_of(i * RT, RT)
            keep = (r0 + lax.broadcasted_iota(jnp.int32, (RT, 128), 0)) < count
            for c in lanes(width):
                window = ms_ref[pl.ds(r0 + EDGE - 8, RT + 16), c]
                term = None
                for n, d in enumerate(TAPS):
                    part = shift_rows(window, d, RT) * ct_ref[n : n + 1, c]
                    term = part if term is None else term + part
                set_ref[pl.ds(r0, RT), c] = xs_ref[pl.ds(r0 + EDGE, RT), c] + jnp.where(keep, term, 0.0)
            return carry

        lax.fori_loop(0, length // RT, conv_chunk, 0)
        for c in lanes(width):
            window = xs_ref[EDGE + TEXT - 8 : EDGE + TEXT + CELLS + 8, c]
            term = jnp.zeros((CELLS, 128), F32)
            for n in range(9):
                off = (n // 3 - 1) * GRID + n % 3 - 1
                term = term + shift_rows(window, off, CELLS) * (cp_ref[n : n + 1, c] * pm_ref[:, n : n + 1])
            set_ref[TEXT : TEXT + CELLS, c] = set_ref[TEXT : TEXT + CELLS, c] + term
        entry_ref[...] = set_ref[...].astype(BF)
        turned_transpose(entry_ref, turn_ref, info_ref[2], block, et_ref, raw_ref)
        wait(arriving)
        for c in range(width // 256):
            s = slice(256 * c, 256 * (c + 1))
            q_ref[:, s] = (dot(entry_ref[...], wq_ref[:, s]) + line(bq_ref, s)).astype(BF) * jnp.asarray(SCALE, BF)
            k_ref[:, s] = dot(entry_ref[...], wk_ref[:, s]).astype(BF)
            v_ref[:, s] = (dot(entry_ref[...], wv_ref[:, s]) + line(bv_ref, s)).astype(BF)
        ka_ref[:, 128:256] = oh_ref[...]
        ka_ref[:, 256:384] = oh_ref[...]
        start(leaving)

    @pl.when(g == pl.num_programs(0) - 1)
    def _():
        wait(leaving)

    pair = pl.ds(pl.multiple_of(g * 128, 128), 128)
    ka_ref[:, 0:128] = k_ref[:, pair]
    lane = lax.broadcasted_iota(jnp.int32, (length, 128), 1)
    for e in range(2):
        mine = (lane < 64) if e == 0 else (lane >= 64)
        qa_ref[e, :, 0:128] = jnp.where(mine, q_ref[:, pair], jnp.zeros((), BF))
        qa_ref[e, :, 128:384] = dot(oh_ref[...], wt_ref[e]).astype(BF)
        s_ref[e] = dot_t(qa_ref[e], ka_ref[...])
    cols = (length + 127) // 128
    at = lax.broadcasted_iota(jnp.int32, (1, length), 1)
    ok = (at < count) | ((at >= TEXT) & (at < TEXT + GRID * GRID))
    bar = jnp.where(ok, 0.0, NEG)
    outs = []
    for e in range(2):
        left, right = edge_ref[2 * g + e, 0], edge_ref[2 * g + e, 1]
        for a in range(length // RT):
            r0 = a * RT
            parts = []
            for b in range(cols):
                w = min(128, length - 128 * b)
                d = 128 * b - r0
                t = s_ref[e, r0 : r0 + RT, 128 * b : 128 * b + w]
                m = bar[:, 128 * b : 128 * b + w]
                if d in OFFSETS:
                    t = t + ord_ref[e, OFFSETS.index(d)][:, :w] + m
                else:
                    t = t + (m + (left if d < 0 else right))
                parts.append(t)
            t = jnp.concatenate(parts, 1)
            top = jnp.max(t, axis=1, keepdims=True)
            ex = jnp.exp(t - top)
            total = jnp.sum(ex, axis=1, keepdims=True)
            p_ref[e, r0 : r0 + RT, :] = (ex * (1.0 / total)).astype(BF)
        outs.append(dot(p_ref[e], v_ref[:, pair]))
    o_ref[...] = jnp.where(lane < 64, outs[0], outs[1]).astype(BF)


def front(info, edge, blocks, ct, cp, pm, turn, wq, bq, wk, wv, bv, oh, wt, od, block):
    n_seq = len(blocks)
    stretch, width = blocks[0].shape
    length = n_seq * stretch
    heads = wt.shape[0]
    sds = jax.ShapeDtypeStruct
    flops = 2 * length * width * width * 3 + heads * 2 * length * length * (384 + 128)
    return pl.pallas_call(
        functools.partial(front_kernel, n_seq=n_seq, block=block),
        out_shape=(sds((length, width), F32), sds((width, length), BF)) + (sds((length, width), BF),) * 3
        + (sds((heads, length, length), BF), sds((length, width), BF)),
        grid_spec=pltpu.PrefetchScalarGridSpec(
            num_scalar_prefetch=2, grid=(heads // 2,),
            in_specs=[whole((stretch, width))] * n_seq
            + [whole(ct.shape), whole(cp.shape), whole(pm.shape), whole(turn.shape), pl.BlockSpec(memory_space=pl.ANY), whole(bq.shape), pl.BlockSpec(memory_space=pl.ANY),
               pl.BlockSpec(memory_space=pl.ANY), whole(bv.shape), whole(oh.shape),
               pl.BlockSpec((2, 128, 256), lambda g, *_: (g, 0, 0)),
               pl.BlockSpec((2, len(OFFSETS), RT, 128), lambda g, *_: (g, 0, 0, 0))],
            out_specs=[pl.BlockSpec(memory_space=pl.ANY)] * 5
            + [pl.BlockSpec((2, length, length), lambda g, *_: (g, 0, 0)), pl.BlockSpec((length, 128), lambda g, *_: (0, g))],
            scratch_shapes=[pltpu.VMEM((length, width), BF), pltpu.VMEM((length + 2 * EDGE, width), F32), pltpu.VMEM((length + 2 * EDGE, width), F32),
                            pltpu.VMEM((length, 384), BF), pltpu.VMEM((2, length, 384), BF), pltpu.VMEM((2, length, length), F32), pltpu.VMEM((width, length), BF),
                            pltpu.VMEM((length, width), F32), pltpu.VMEM((width, length), BF)]
            + [pltpu.VMEM((length, width), BF)] * 3 + [pltpu.VMEM((width, width), BF)] * 3
            + [pltpu.SemaphoreType.DMA((3,)), pltpu.SemaphoreType.DMA((5,))],
        ),
        cost_estimate=pl.CostEstimate(flops=25_000_000_000, bytes_accessed=8 << 20, transcendentals=0),
        name="front",
    )(info, edge, *blocks, ct, cp, pm, turn, wq, bq, wk, wv, bv, oh, wt, od)


def norm_stats(u):
    mean = jnp.mean(u, axis=1, keepdims=True)
    c = u - mean
    rs = lax.rsqrt(jnp.mean(c * c, axis=1, keepdims=True) + EPS)
    return c * rs, rs


def norm_back(u, xhat, rs):
    return rs * (u - jnp.mean(u, axis=1, keepdims=True) - xhat * jnp.mean(u * xhat, axis=1, keepdims=True))


def gelu_pair(x):
    t = 1.0 / (1.0 + jnp.abs(x) * (ERF_P * 0.7071067811865476))
    bell = jnp.exp2(x * x * -0.7213475204444817)
    q = jnp.full_like(t, 0.5 * ERF_Q[7])
    for k in range(6, -1, -1):
        q = q * t + 0.5 * ERF_Q[k]
    tail = q * t * bell
    cdf = jnp.where(x < 0, tail, 1.0 - tail)
    return x * cdf, cdf + x * bell * 0.3989422804014327


def middle_kernel(info_ref, *refs, n_seq, tiles, tile, block):
    cots = refs[:n_seq]
    (att_ref, set_ref, wo_ref, bo_ref, ng_ref, ns_ref, w1_ref, b1_ref, w2_ref, b2_ref, fg_ref, fs_ref, turn_ref) = refs[n_seq : n_seq + 13]
    outs = refs[n_seq + 13 :]
    mixed = outs[:n_seq]
    (xh_any, rs_any, fl_any, gp_ref, ds_any, dr_any, gk_ref, gs_ref, sm_ref, act_ref, fn_ref, acc_ref, cot_ref, mix_ref, e_ref, g_ref, b1_rows,
     xh_ref, rs_ref, fl_ref, ds_ref, dr_ref, cot_sems, norm_sems, out_sems) = outs[n_seq:]
    i = pl.program_id(0)
    length, width = fl_ref.shape
    place = info_ref[0]
    stretch = length // n_seq
    block_of = lambda ref, d: ref.at[pl.ds(pl.multiple_of(lax.rem(place + d, n_seq) * stretch, 16), stretch), :]
    arriving = moves([(cots[d], block_of(cot_ref, n_seq - d)) for d in range(n_seq)], cot_sems)
    normed = moves([(xh_ref, xh_any), (rs_ref, rs_any), (fl_ref, fl_any)], norm_sems)
    leaving = moves([(ds_ref, ds_any), (dr_ref, dr_any)] + [(block_of(mix_ref, d), mixed[d]) for d in range(n_seq)], out_sems)

    @pl.when(i == 0)
    def _():
        start(arriving)
        for c in range(width // 256):
            s = slice(256 * c, 256 * (c + 1))
            acc_ref[:, s] = dot(att_ref[...], wo_ref[:, s])

        def chunk(j, carry):
            r = pl.ds(pl.multiple_of(j * LR, LR), LR)
            u = set_ref[r, :] + (acc_ref[r, :] + line(bo_ref))
            xhat, rs = norm_stats(u)
            xh_ref[r, :] = xhat
            rs_ref[r, :] = jnp.broadcast_to(rs, (LR, 128))
            fn = xhat * line(ng_ref) + line(ns_ref)
            fn_ref[r, :] = fn
            fl_ref[r, :] = fn.astype(BF)
            acc_ref[r, :] = jnp.broadcast_to(line(b2_ref), (LR, width))
            return carry

        lax.fori_loop(0, length // LR, chunk, 0, unroll=6)
        start(normed)
        for t in range(tiles):
            b1_rows[t] = line(b1_ref, slice(t * tile, (t + 1) * tile))

    @pl.when(i < tiles)
    def _():
        half = tile // 3
        for n in range(3):
            e_ref[n] = dot(fl_ref[...], w1_ref[:, n * half : (n + 1) * half])
        for n in range(3):
            s = slice(n * half, (n + 1) * half)
            act, gp = gelu_pair(e_ref[n] + b1_rows[i, :, s])
            act_ref[i, :, s] = act.astype(BF)
            gp_ref[:, s] = gp.astype(gp_ref.dtype)
        for c in range(width // 256):
            s = slice(256 * c, 256 * (c + 1))
            acc_ref[:, s] += dot(act_ref[i], w2_ref[:, s])

    @pl.when(i == tiles - 1)
    def _():
        wait(arriving)

        def chunk(j, sums):
            r0 = pl.multiple_of(j * LR, LR)
            r = pl.ds(r0, LR)
            second = fn_ref[r, :] + acc_ref[r, :]
            xhat, rs = norm_stats(second)
            mix_ref[r, :] = (xhat * line(fg_ref) + line(fs_ref)).astype(BF)
            cot = cot_ref[r, :].astype(F32)
            back = norm_back(cot * line(fg_ref), xhat, rs)
            ds_ref[r, :] = back
            low = back.astype(BF)
            dr_ref[r, :] = low
            return (sums[0] + fold(cot * xhat), sums[1] + fold(cot), sums[2] + fold(low.astype(F32)))

        sums = lax.fori_loop(0, length // LR, chunk, (jnp.zeros((8, width), F32),) * 3, unroll=6)
        for n in range(3):
            sm_ref[n : n + 1, :] = row_sum(sums[n])
        start(leaving)

    @pl.when(i == pl.num_programs(0) - 1)
    def _():
        wait(normed)
        wait(leaving)

    @pl.when(i >= tiles)
    def _():
        grad = t_dot(act_ref[i - tiles], dr_ref[...]).astype(BF)
        if 2 * block == tile:
            g_ref[...] = grad
            core = info_ref[2]
            gk_ref[...] = g_ref[pl.ds(pl.multiple_of(core * block, block), block), :]
            gs_ref[...] = g_ref[pl.ds(pl.multiple_of((1 - core) * block, block), block), :]
        else:
            turned = dot(turn_ref[...], grad).astype(BF)
            gk_ref[...] = turned[: tile // 2]
            gs_ref[...] = turned[tile // 2 :]


def middle(info, cots, att, settled, wo, bo, ng, ns, w1, b1, w2, b2, fg, fs, turn, block):
    tile = w1.shape[0]
    n_seq = len(cots)
    stretch, width = cots[0].shape
    length = n_seq * stretch
    ff = w1.shape[1]
    tiles = ff // tile
    sds = jax.ShapeDtypeStruct
    early = lambda i: jnp.minimum(i, tiles - 1)
    late = lambda i: jnp.maximum(i - tiles, 0)
    return pl.pallas_call(
        functools.partial(middle_kernel, n_seq=n_seq, tiles=tiles, tile=tile, block=block),
        out_shape=(sds((stretch, width), BF),) * n_seq
        + (sds((length, width), F32), sds((length, 128), F32), sds((length, width), BF), sds((length, ff), BF),
           sds((length, width), F32), sds((length, width), BF), sds((ff // 2, width), BF), sds((ff // 2, width), BF), sds((8, width), F32)),
        grid_spec=pltpu.PrefetchScalarGridSpec(
            num_scalar_prefetch=1, grid=(2 * tiles,),
            in_specs=[pl.BlockSpec(memory_space=pl.ANY)] * n_seq
            + [whole(att.shape), whole(settled.shape), whole(wo.shape), whole(bo.shape), whole(ng.shape), whole(ns.shape),
               pl.BlockSpec((width, tile), lambda i, *_: (0, early(i))), whole(b1.shape),
               pl.BlockSpec((tile, width), lambda i, *_: (early(i), 0)), whole(b2.shape), whole(fg.shape), whole(fs.shape), whole(turn.shape)],
            out_specs=[pl.BlockSpec(memory_space=pl.ANY)] * (n_seq + 3)
            + [pl.BlockSpec((length, tile), lambda i, *_: (0, early(i))), pl.BlockSpec(memory_space=pl.ANY), pl.BlockSpec(memory_space=pl.ANY),
               pl.BlockSpec((tile // 2, width), lambda i, *_: (late(i), 0)), pl.BlockSpec((tile // 2, width), lambda i, *_: (late(i), 0)),
               whole_out((8, width))],
            scratch_shapes=[pltpu.VMEM((tiles, length, tile), BF), pltpu.VMEM((length, width), F32), pltpu.VMEM((length, width), F32),
                            pltpu.VMEM((length, width), BF), pltpu.VMEM((length, width), BF), pltpu.VMEM((3, length, tile // 3), F32),
                            pltpu.VMEM((tile, width), BF), pltpu.VMEM((tiles, 1, tile), F32),
                            pltpu.VMEM((length, width), F32), pltpu.VMEM((length, 128), F32), pltpu.VMEM((length, width), BF),
                            pltpu.VMEM((length, width), F32), pltpu.VMEM((length, width), BF),
                            pltpu.SemaphoreType.DMA((n_seq,)), pltpu.SemaphoreType.DMA((3,)), pltpu.SemaphoreType.DMA((2 + n_seq,))],
        ),
        cost_estimate=pl.CostEstimate(flops=35_000_000_000, bytes_accessed=8 << 20, transcendentals=0),
        name="middle",
    )(info, *cots, att, settled, wo, bo, ng, ns, w1, b1, w2, b2, fg, fs, turn)


def back_kernel(info_ref, *refs, tiles, last, block):
    core = info_ref[2]
    if last:
        (dr_ref, in_ref, w2_ref, gp_ref, w1_ref, fl_ref, turn_ref, xh_any, rs_any, ng_ref, att_any, wo_any) = refs[:12]
        (gk_ref, gs_ref, be_ref, df_ref, da_ref, sm_ref, flt_ref, raw_ref, acc_ref, db_ref,
         xh_ref, rs_ref, att_ref, wo_ref, sems) = refs[-15:]
        arriving = moves([(xh_any, xh_ref), (rs_any, rs_ref), (att_any, att_ref), (wo_any, wo_ref)], sems)
    else:
        (dr_ref, in_ref, w2_ref, gp_ref, w1_ref, fl_ref, turn_ref) = refs[:7]
        (gk_ref, gs_ref, be_ref, acc_ref, flt_ref, raw_ref) = refs[-6:]
    i = pl.program_id(0)
    length, width = dr_ref.shape

    @pl.when(i == 0)
    def _():
        if last:
            start(arriving)
        turned_transpose(fl_ref, turn_ref, core, block, flt_ref, raw_ref)
        acc_ref[...] = in_ref[...]

    @pl.when(i < tiles)
    def _():
        de = dot_t(dr_ref[...], w2_ref[...]) * gp_ref[...].astype(F32)
        de = de.astype(BF)
        be_ref[...] = row_sum(de.astype(F32))
        grad = dot(flt_ref[...], de).astype(BF)
        gk_ref[...] = grad[: width // 2]
        gs_ref[...] = grad[width // 2 :]
        acc_ref[...] += dot_t(de, w1_ref[...])

    if not last:
        return

    @pl.when(i == tiles)
    def _():
        wait(arriving)

        def chunk(j, sums):
            r = pl.ds(pl.multiple_of(j * LR, LR), LR)
            first = acc_ref[r, :]
            xhat = xh_ref[r, :]
            back = norm_back(first * line(ng_ref), xhat, rs_ref[r, 0:1])
            df_ref[r, :] = back
            low = back.astype(BF)
            db_ref[r, :] = low
            return (sums[0] + fold(first * xhat), sums[1] + fold(first), sums[2] + fold(low.astype(F32)))

        sums = lax.fori_loop(0, length // LR, chunk, (jnp.zeros((8, width), F32),) * 3, unroll=6)
        for n in range(3):
            sm_ref[n : n + 1, :] = row_sum(sums[n])
        da_ref[...] = dot_t(db_ref[...], wo_ref[...]).astype(BF)
        turned_transpose(att_ref, turn_ref, core, block, flt_ref, raw_ref)
        grad = dot(flt_ref[...], db_ref[...]).astype(BF)
        gk_ref[...] = grad[: width // 2]
        gs_ref[...] = grad[width // 2 :]


def back(info, block, first, tiles, dr, acc, w2, gp, w1, fl, turn, filled=(), norm=None):
    length, width = dr.shape
    ff = w1.shape[1]
    last = norm is not None
    sds = jax.ShapeDtypeStruct
    at = lambda i: jnp.minimum(i, tiles - 1) + first
    grad = pl.BlockSpec((width // 2, width), lambda i, *_: (0, i + first))
    args = [dr, acc, w2, gp, w1, fl, turn] + list(norm or ())
    out_shape = [sds((width // 2, ff + width), BF), sds((width // 2, ff + width), BF), sds((1, ff), F32), sds((length, width), F32)]
    out_specs = [grad, grad, pl.BlockSpec((1, width), lambda i, *_: (0, at(i))), whole_out((length, width))]
    scratch = [pltpu.VMEM((width, length), BF), pltpu.VMEM((width, length), BF)]
    if last:
        out_shape += [sds((length, width), BF), sds((8, width), F32)]
        out_specs += [whole_out((length, width)), whole_out((8, width))]
        scratch += [pltpu.VMEM((length, width), F32), pltpu.VMEM((length, width), BF), pltpu.VMEM((length, width), F32),
                    pltpu.VMEM((length, 128), F32), pltpu.VMEM((length, width), BF), pltpu.VMEM((width, width), BF),
                    pltpu.SemaphoreType.DMA((4,))]
    return pl.pallas_call(
        functools.partial(back_kernel, tiles=tiles, last=last, block=block),
        out_shape=tuple(out_shape),
        grid_spec=pltpu.PrefetchScalarGridSpec(
            num_scalar_prefetch=1, grid=(tiles + last,),
            in_specs=[whole(dr.shape), whole(acc.shape), pl.BlockSpec((width, width), lambda i, *_: (at(i), 0)),
                      pl.BlockSpec((length, width), lambda i, *_: (0, at(i))), pl.BlockSpec((width, width), lambda i, *_: (0, at(i)))]
            + [pl.BlockSpec(memory_space=pl.ANY) if n in (7, 8, 10, 11) else whole(x.shape) for n, x in enumerate(args) if n >= 5]
            + [pl.BlockSpec(memory_space=pl.ANY)] * len(filled),
            out_specs=out_specs,
            scratch_shapes=scratch,
        ),
        input_output_aliases={1 + len(args) + n: n for n in range(len(filled))},
        cost_estimate=pl.CostEstimate(flops=12_000_000_000, bytes_accessed=8 << 20, transcendentals=0),
        name="back",
    )(info, *args, *filled)


def diagonals(x):
    wide = jnp.concatenate([x, jnp.zeros_like(x)], 1)
    return row_sum(pltpu.roll(wide, 0, 1, stride=1, stride_axis=0))


def hi_lo(x):
    hi = x.astype(BF)
    return jnp.concatenate([hi, (x - hi.astype(F32)).astype(BF)], 1)


def heads_kernel(*refs):
    (p_ref, q_ref, k_ref, v_ref, do_ref, o_ref, oh_ref, oht_ref, et_any, wq_ref, wk_ref, wv_ref, in_any) = refs[:13]
    (gk_ref, gs_ref, qb_ref, diag_ref, acc_ref, va_ref, rhs_ref, dsc_ref, dp_ref, w_ref, d_ref, et_ref, sems) = refs[-13:]
    arriving = moves([(et_any, et_ref), (in_any, acc_ref)], sems)
    g = pl.program_id(0)
    length = q_ref.shape[0]
    lane = lax.broadcasted_iota(jnp.int32, (length, 128), 1)

    @pl.when(g == 0)
    def _():
        va_ref[:, 128:256] = jnp.where(lane < 2, 1.0, 0.0).astype(BF)
        rhs_ref[:, 128:256] = oh_ref[...]
        start(arriving)

    va_ref[:, 0:128] = v_ref[...]
    rhs_ref[:, 0:128] = k_ref[...]
    cols = (length + 127) // 128
    flip = (lax.broadcasted_iota(jnp.int32, (RT, RT), 0) + lax.broadcasted_iota(jnp.int32, (RT, RT), 1) == RT - 1).astype(F32).astype(BF)
    do = do_ref[...]
    prod = do.astype(F32) * o_ref[...].astype(F32)
    res = []
    for e in range(2):
        mine = (lane < 64) if e == 0 else (lane >= 64)
        inner = -jnp.sum(jnp.where(mine, prod, 0.0), axis=1, keepdims=True)
        hi = inner.astype(BF)
        lo = inner - hi.astype(F32)
        ext = jnp.where(lane == 0, hi.astype(F32), jnp.where(lane == 1, lo, 0.0)).astype(BF)
        da = jnp.concatenate([jnp.where(mine, do, jnp.zeros((), BF)), ext], 1)
        dp_ref[e] = dot_t(da, va_ref[...])
    for e in range(2):
        sums = {}
        for a in range(length // RT):
            r0 = a * RT
            ds = p_ref[e, r0 : r0 + RT, :].astype(F32) * dp_ref[e, r0 : r0 + RT, :]
            dsc_ref[e, r0 : r0 + RT, :] = ds.astype(BF)
            for b in range(cols):
                w = min(128, length - 128 * b)
                d = 128 * b - r0
                t = ds[:, 128 * b : 128 * b + w]
                if w < 128:
                    t = jnp.concatenate([t, jnp.zeros((RT, 128 - w), F32)], 1)
                key = OFFSETS.index(d) if d in OFFSETS else (4 if d < 0 else 5)
                sums[key] = sums[key] + t if key in sums else t
        for n in range(4):
            turned = dot(flip, hi_lo(sums[n]))
            diag_ref[e, n : n + 1, :] = diagonals(turned[:, 0:128] + turned[:, 128:256])
        diag_ref[e, 4:5, 0:128] = row_sum(sums[4])
        diag_ref[e, 4:5, 128:256] = row_sum(sums[5])
        r = dot(dsc_ref[e], rhs_ref[...])
        hh = dot(oht_ref[...], hi_lo(r[:, 128:256]))
        hist = hh[:, 0:128] + hh[:, 128:256]
        half = lane[:BOX] < BOX
        diag_ref[e, 5:6, :] = diagonals(jnp.where(half, hist[:BOX], 0.0))
        diag_ref[e, 6:7, :] = diagonals(jnp.where(half, 0.0, hist[BOX:]))
        diag_ref[e, 7:8, :] = jnp.zeros((1, 256), F32)
        dk = t_dot(dsc_ref[e], q_ref[...])
        dv = t_dot(p_ref[e], do)
        res.append((r[:, 0:128], dk, dv))
    first = lane < 64
    dq = (jnp.where(first, res[0][0], res[1][0]) * SCALE).astype(BF)
    dk = jnp.where(first, res[0][1], res[1][1]).astype(BF)
    dv = jnp.where(first, res[0][2], res[1][2]).astype(BF)

    @pl.when(g == 0)
    def _():
        wait(arriving)

    d_ref[:, 0:128] = dq
    d_ref[:, 128:256] = dk
    d_ref[:, 256:384] = dv
    qb_ref[0:1, :] = row_sum(dq.astype(F32))
    qb_ref[1:2, :] = row_sum(dv.astype(F32))
    w_ref[:, 0:128] = wq_ref[...]
    w_ref[:, 128:256] = wk_ref[...]
    w_ref[:, 256:384] = wv_ref[...]
    grad = dot(et_ref[...], d_ref[...]).astype(BF)
    gk_ref[...] = grad[: grad.shape[0] // 2]
    gs_ref[...] = grad[grad.shape[0] // 2 :]
    acc_ref[...] += dot_t(d_ref[...], w_ref[...])


def heads_back(first, count, probs, q, k, v, do, o, oh, oht, et, wq, wk, wv, acc, filled=()):
    heads = probs.shape[0]
    length, width = q.shape
    steps = count // 2
    base = first // 2
    sds = jax.ShapeDtypeStruct
    col = pl.BlockSpec((length, 128), lambda g: (0, g + base))
    wcol = pl.BlockSpec((width, 128), lambda g: (0, g + base))
    flops = 2 * length * width * 64 * count * 6 + count * 2 * length * length * (256 + 256 + 128 + 128)
    return pl.pallas_call(
        heads_kernel,
        out_shape=(sds((width // 2, 3 * width), BF), sds((width // 2, 3 * width), BF), sds((8, width), F32), sds((heads, 8, 256), F32), sds((length, width), F32)),
        grid=(steps,),
        in_specs=[pl.BlockSpec((2, length, length), lambda g: (g + base, 0, 0)), col, col, col, col, col, whole(oh.shape), whole(oht.shape),
                  pl.BlockSpec(memory_space=pl.ANY), wcol, wcol, wcol] + [pl.BlockSpec(memory_space=pl.ANY)] * (1 + len(filled)),
        out_specs=[pl.BlockSpec((width // 2, 384), lambda g: (0, g + base)), pl.BlockSpec((width // 2, 384), lambda g: (0, g + base)),
                   pl.BlockSpec((8, 128), lambda g: (0, g + base)), pl.BlockSpec((2, 8, 256), lambda g: (g + base, 0, 0)), whole_out((length, width))],
        input_output_aliases={13 + n: n for n in range(len(filled))},
        scratch_shapes=[pltpu.VMEM((length, 256), BF), pltpu.VMEM((length, 256), BF), pltpu.VMEM((2, length, length), BF),
                        pltpu.VMEM((2, length, length), F32), pltpu.VMEM((width, 384), BF), pltpu.VMEM((length, 384), BF),
                        pltpu.VMEM((width, length), BF), pltpu.SemaphoreType.DMA((2,))],
        cost_estimate=pl.CostEstimate(flops=20_000_000_000, bytes_accessed=8 << 20, transcendentals=0),
        name="heads_back",
    )(probs, q, k, v, do, o, oh, oht, et, wq, wk, wv, acc, *filled)


def encode_kernel(info_ref, *refs, n_seq):
    blocks = refs[:n_seq]
    in_ref, ct_ref, cp_ref, pm_ref, sm_ref, sm2_ref, be_ref, qb_ref = refs[n_seq : n_seq + 8]
    outs = refs[n_seq + 8 :]
    grads = outs[:n_seq]
    small_ref, acc_ref, gs_ref, ms_ref, gt_ref = outs[n_seq:]
    length, width = in_ref.shape
    place, count = info_ref[0], info_ref[1]
    acc_ref[...] = in_ref[...]
    small_ref[...] = jnp.zeros_like(small_ref)
    small_ref[0:3, :] = sm_ref[0:3, :]
    small_ref[3:6, :] = sm2_ref[0:3, :]
    small_ref[6:8, :] = qb_ref[0:2, :]
    tiles = be_ref.shape[1] // width
    for t in range(tiles):
        small_ref[8 + t : 9 + t, :] = be_ref[:, t * width : (t + 1) * width]
    taps, cells = 8 + tiles, 15 + tiles
    zero = jnp.zeros((EDGE, width), F32)
    gs_ref[0:EDGE, :] = zero
    gs_ref[EDGE + length :, :] = zero
    ms_ref[0:EDGE, :] = zero
    ms_ref[EDGE + length :, :] = zero
    gather_page(ms_ref, EDGE, place, n_seq, blocks[0], blocks[1:])
    for c in lanes(width):
        tok = ms_ref[EDGE + TEXT - 8 : EDGE + TEXT + CELLS + 8, c]
        own = acc_ref[TEXT : TEXT + CELLS, c]
        window = jnp.concatenate([acc_ref[TEXT - 8 : TEXT + CELLS, c], jnp.zeros((8, 128), F32)], 0)
        term = jnp.zeros((CELLS, 128), F32)
        for n in range(9):
            off = (n // 3 - 1) * GRID + n % 3 - 1
            term = term + shift_rows(window, -off, CELLS) * (cp_ref[n : n + 1, c] * pm_ref[:, 8 - n : 9 - n])
            small_ref[cells + n : cells + n + 1, c] = row_sum(own * shift_rows(tok, off, CELLS) * pm_ref[:, n : n + 1])
        gt_ref[:, c] = term

    def split_chunk(j, carry):
        r0 = pl.multiple_of(j * RT, RT)
        keep = (r0 + lax.broadcasted_iota(jnp.int32, (RT, 128), 0)) < count
        for c in lanes(width):
            dset = acc_ref[pl.ds(r0, RT), c]
            gs_ref[pl.ds(r0 + EDGE, RT), c] = jnp.where(keep, dset, 0.0)
            ms_ref[pl.ds(r0 + EDGE, RT), c] = jnp.where(keep, ms_ref[pl.ds(r0 + EDGE, RT), c], 0.0)
        return carry

    lax.fori_loop(0, length // RT, split_chunk, 0)
    for c in lanes(width):
        acc_ref[TEXT : TEXT + CELLS, c] = acc_ref[TEXT : TEXT + CELLS, c] + gt_ref[:, c]

    def conv_chunk(j, sums):
        r0 = pl.multiple_of(j * RT, RT)
        keep = (r0 + lax.broadcasted_iota(jnp.int32, (RT, 128), 0)) < count
        out = []
        for n, c in enumerate(lanes(width)):
            window = gs_ref[pl.ds(r0 + EDGE - 8, RT + 16), c]
            own = ms_ref[pl.ds(r0 + EDGE, RT), c]
            term = None
            for m, d in enumerate(TAPS):
                moved = shift_rows(window, -d, RT)
                part = moved * ct_ref[m : m + 1, c]
                term = part if term is None else term + part
                out.append(sums[n * len(TAPS) + m] + row_sum(moved * own))
            acc_ref[pl.ds(r0, RT), c] = acc_ref[pl.ds(r0, RT), c] + jnp.where(keep, term, 0.0)
        return tuple(out)

    zeros = (jnp.zeros((1, 128), F32),) * (len(TAPS) * (width // 128))
    sums = lax.fori_loop(0, length // RT, conv_chunk, zeros)
    for n, c in enumerate(lanes(width)):
        for m in range(len(TAPS)):
            small_ref[taps + m : taps + m + 1, c] = sums[n * len(TAPS) + m]
    stretch = length // n_seq
    for d in range(n_seq):
        dest = lax.rem(place + d, n_seq)
        grads[d][...] = acc_ref[pl.ds(pl.multiple_of(dest * stretch, 16), stretch), :].astype(BF)


def encode_back(info, blocks, d_settled, ct, cp, pm, sm, sm2, be, qb):
    n_seq = len(blocks)
    stretch, width = blocks[0].shape
    length = n_seq * stretch
    sds = jax.ShapeDtypeStruct
    rows = 24 + be.shape[1] // width
    rows += 8 - rows % 8
    return pl.pallas_call(
        functools.partial(encode_kernel, n_seq=n_seq),
        out_shape=(sds((stretch, width), BF),) * n_seq + (sds((rows, width), F32),),
        grid_spec=pltpu.PrefetchScalarGridSpec(
            num_scalar_prefetch=1, grid=(1,),
            in_specs=[whole((stretch, width))] * n_seq + [whole(d_settled.shape), whole(ct.shape), whole(cp.shape), whole(pm.shape), whole(sm.shape), whole(sm2.shape), whole(be.shape), whole(qb.shape)],
            out_specs=[whole_out((stretch, width))] * n_seq + [whole_out((rows, width))],
            scratch_shapes=[pltpu.VMEM((length, width), F32), pltpu.VMEM((length + 2 * EDGE, width), F32),
                            pltpu.VMEM((length + 2 * EDGE, width), F32), pltpu.VMEM((CELLS, width), F32)],
        ),
        cost_estimate=pl.CostEstimate(flops=10_000_000_000, bytes_accessed=8 << 20, transcendentals=0),
        name="encode_back",
    )(info, *blocks, d_settled, ct, cp, pm, sm, sm2, be, qb)


def turn_matrix(width, n, core):
    block, half = width // n, width // 2
    r = jnp.arange(width, dtype=jnp.int32)
    inner = jnp.where(r < half, r, r - half)
    parity = jnp.where(r < half, core, 1 - core)
    source = (2 * (inner // block) + parity) * block + inner % block
    return (source[:, None] == r[None]).astype(BF)


def restack_kernel(info_ref, *refs, n, layout):
    parts, outs = refs[:n], refs[n:]
    for d, part in enumerate(parts):
        source = lax.rem(info_ref[0] - d + n, n)
        for out, pieces in zip(outs, layout):
            at = 0
            for start, width in pieces:
                out[source, :, at : at + width] = part[:, start : start + width].astype(out.dtype)
                at += width


def restack(info, parts, dtype, layout=None):
    n = len(parts)
    rows, cols = parts[0].shape
    layout = layout or [[(0, cols)]]
    outs = pl.pallas_call(
        functools.partial(restack_kernel, n=n, layout=layout),
        out_shape=[jax.ShapeDtypeStruct((n, rows, sum(w for _, w in pieces)), dtype) for pieces in layout],
        in_specs=[pl.BlockSpec(memory_space=pltpu.SMEM)] + [pl.BlockSpec(memory_space=pltpu.VMEM)] * n,
        out_specs=[pl.BlockSpec(memory_space=pltpu.VMEM)] * len(layout),
        cost_estimate=pl.CostEstimate(flops=1000, bytes_accessed=1000, transcendentals=0),
        name="restack",
    )(info, *parts)
    return outs


def unpack_kernel(small_ref, *outs, heads, tiles):
    gct, gcp, qb, vb, ob, order, horiz, vert, ng, ns, be, rb, fg, fs = outs
    for row, out in ((0, fg), (1, fs), (2, rb), (3, ng), (4, ns), (5, ob), (6, qb), (7, vb)):
        out[...] = small_ref[row, :]
    width = small_ref.shape[1]
    for t in range(tiles):
        be[t * width : (t + 1) * width] = small_ref[8 + t, :]
    taps, cells, bias = 8 + tiles, 15 + tiles, 24 + tiles
    for s in range(3):
        for t in range(3):
            gct[s, t, :] = small_ref[taps + 3 + (t - 1) * (s + 1), :]
            gcp[s, t, :] = small_ref[cells + 3 * s + t, :]
    nb = order.shape[1]
    per = width // 128
    for h in range(heads):
        row, at = bias + h // per, 128 * (h % per)
        for n, out in enumerate((order, horiz, vert)):
            out[h, :] = small_ref[row, at + n * nb : at + (n + 1) * nb]


def unpack(small, heads, nb, ff):
    width = small.shape[1]
    sds = lambda *shape: jax.ShapeDtypeStruct(shape, F32)
    vec = sds(width)
    return pl.pallas_call(
        functools.partial(unpack_kernel, heads=heads, tiles=ff // width),
        out_shape=(sds(3, 3, width), sds(3, 3, width), vec, vec, vec, sds(heads, nb), sds(heads, nb), sds(heads, nb),
                   vec, vec, sds(ff), vec, vec, vec),
        cost_estimate=pl.CostEstimate(flops=1000, bytes_accessed=1000, transcendentals=0),
        name="unpack",
    )(small)


def one_hot_rows(ids, size):
    return (ids.reshape(1, -1) == jnp.arange(size, dtype=jnp.int32)[:, None]).astype(F32)


def tables(rel_order, rel_horiz, rel_vert):
    heads, nb = rel_order.shape
    high = lax.Precision.HIGHEST
    a = jnp.arange(BOX, dtype=jnp.int32)
    cell = one_hot_rows(jnp.clip(a[None, :] - a[:, None], -SPAN, SPAN) + SPAN, nb)

    def split(table):
        x = jnp.dot(table, cell, precision=high).reshape(heads, BOX, BOX)
        top = lax.reduce_precision(x, 8, 7)
        return top, x - top

    (hh, hl), (vh, vl) = split(rel_horiz), split(rel_vert)
    zero = jnp.zeros_like(hh)
    wt = jnp.concatenate([jnp.concatenate([hh, zero, hl, zero], 2), jnp.concatenate([zero, vh, zero, vl], 2)], 1).astype(BF)
    i = jnp.arange(RT, dtype=jnp.int32)[:, None]
    j = jnp.arange(128, dtype=jnp.int32)[None]
    band = jnp.stack([jnp.clip(d + j - i, -SPAN, SPAN) + SPAN for d in OFFSETS])
    od = jnp.dot(rel_order, one_hot_rows(band, nb), precision=high).reshape(heads, len(OFFSETS), RT, 128)
    edge = jnp.stack([rel_order[:, 0], rel_order[:, -1]], 1)
    return wt, od, edge


def bias_grads(diag, nb):
    heads = diag.shape[0]
    high = lax.Precision.HIGHEST
    at = jnp.arange(256, dtype=jnp.int32)
    step = at - (RT - 1)
    order_bins = jnp.stack([jnp.clip(d + step, -SPAN, SPAN) for d in OFFSETS] + [jnp.where(at < 128, -SPAN, SPAN)]) + SPAN
    order = jnp.dot(diag[:, :5].reshape(heads, -1), one_hot_rows(order_bins, nb).T, precision=high)
    flat = jnp.clip(step, -SPAN, SPAN) + SPAN
    horiz = jnp.dot(diag[:, 5], one_hot_rows(flat, nb).T, precision=high)
    low = jnp.clip(step - BOX, -SPAN, SPAN) + SPAN
    vert = jnp.dot(diag[:, 6], one_hot_rows(low, nb).T, precision=high)
    return order, horiz, vert


def patch_masks():
    g = jnp.arange(CELLS, dtype=jnp.int32)
    i, j = g // GRID, g % GRID
    cols = []
    for n in range(9):
        a, b = i + n // 3 - 1, j + n % 3 - 1
        cols.append((g < GRID * GRID) & (a >= 0) & (a < GRID) & (b >= 0) & (b < GRID))
    return jnp.pad(jnp.stack(cols, 1).astype(F32), ((0, 0), (0, 128 - 9)))


def text_taps(conv_text):
    rows = []
    for d in TAPS:
        if d == 0:
            rows.append(conv_text[0, 1] + conv_text[1, 1] + conv_text[2, 1])
        else:
            rows.append(conv_text[abs(d) - 1, 2 if d > 0 else 0])
    rows.append(jnp.zeros_like(rows[0]))
    return jnp.stack(rows)


def xor_pairs(n, bit):
    return [(i, i ^ bit) for i in range(n)]


def swap(value, axis, bit):
    return lax.ppermute(value, axis, xor_pairs(lax.axis_size(axis), bit))


def spread(blocks, after=None):
    n = lax.axis_size("seq")
    out = [blocks[0]]
    for d in range(1, n):
        out.append(lax.ppermute(blocks[d], "seq", [(i, (i + d) % n) for i in range(n)]))
    return out


def rotated(pages):
    n = lax.axis_size("seq")
    place = lax.axis_index("seq")
    return [lax.dynamic_index_in_dim(pages, lax.rem(place + d, n), 0, keepdims=False) for d in range(n)]


def total(terms):
    out = terms[0].astype(F32)
    for t in terms[1:]:
        out = out + t.astype(F32)
    return out.astype(BF)


class Reduction:
    def __init__(self, keep, send, line=False):
        self.line = line and lax.axis_size("seq") == 4
        n = lax.axis_size("pages")
        self.n = n
        self.page = lax.axis_index("pages")
        self.first = (self.page & 1) == 0
        self.bits = [1 << b for b in range(1, n.bit_length() - 1)]
        self.shape = (n // 2, keep.shape[0] * 2 // n, keep.shape[1])
        self.terms = [keep.reshape(self.shape)]
        self.send, self.at, self.name = send, 0, None

    def blocks(self, depth, other):
        up, down = self.bits[:depth], self.bits[::-1][:depth]
        out = []
        for k in range((self.n // 2) >> depth):
            pair = []
            for closed in (up, down):
                free = [b for b in self.bits if b not in closed]
                index = sum((((k >> i) & 1) * b) for i, b in enumerate(free))
                mine = sum(closed)
                flip = closed[-1] if other and closed else 0
                pair.append((index + ((self.page ^ flip) & mine)) // 2)
            out.append(jnp.where(self.first, *pair))
        return out

    def pick(self, depth, other):
        rows = []
        for k, block in enumerate(self.blocks(depth, other)):
            parts = []
            for t, term in enumerate(self.terms):
                have = max(t - 1, 0)
                if have == 0:
                    place = block
                else:
                    known = self.blocks(have, False)
                    place = sum(jnp.where(known[i] == block, i, 0) for i in range(len(known)))
                parts.append(lax.dynamic_index_in_dim(term, place, 0, keepdims=False))
            rows.append(total(parts))
        return jnp.stack(rows) if len(rows) > 1 else rows[0][None]

    def step(self):
        assert not self.over()
        at, last = self.at, len(self.bits)
        self.at += 1
        n = lax.axis_size("seq")
        ring = lambda d: [(i, (i + d) % n) for i in range(n)]
        place = lax.axis_index("seq")
        if at == 0:
            self.fresh = [swap(self.send, "pages", 1)]
        elif at <= last:
            self.terms.append(self.fresh[0].reshape((-1,) + self.shape[1:]))
            pairs = [(i, i ^ (self.bits[-at] if i & 1 else self.bits[at - 1])) for i in range(self.n)]
            self.fresh = [lax.ppermute(self.pick(at, True), "pages", pairs)]
        elif at == last + 1:
            self.terms.append(self.fresh[0].reshape((-1,) + self.shape[1:]))
            value = self.pick(last, False)[0]
            rows, cols = value.shape
            if self.line:
                self.own = value
                self.fresh = [lax.ppermute(value, "seq", [(0, 1), (3, 2)])]
                return
            quarters = value.reshape(n, rows // n, cols)
            piece = lambda d: lax.dynamic_index_in_dim(quarters, lax.rem(place + d, n), 0, keepdims=False)
            self.own = piece(0)
            self.fresh = [lax.ppermute(piece(d), "seq", ring(d)) for d in range(1, n)]
        else:
            self.own = total([self.own] + self.fresh)
            if self.line:
                self.fresh = [lax.ppermute(self.own, "seq", [(1, 2), (2, 1)] if at == last + 2 else [(1, 0), (2, 3)])]
                return
            self.fresh = [lax.ppermute(self.own, "seq", ring(d)) for d in range(1, n)]

    def over(self):
        return self.at == len(self.bits) + (4 if self.line else 3)

    def result(self, info, layout=None):
        if self.line:
            place = lax.axis_index("seq")
            return [jnp.where((place == 0) | (place == 3), self.fresh[0], self.own).astype(F32)]
        outs = restack(info, [self.own] + self.fresh, F32, layout)
        return [out.reshape(-1, out.shape[-1]) for out in outs]


def tie(value, *reductions):
    value, fresh, held = lax.optimization_barrier(
        (value, tuple(r.fresh for r in reductions), tuple(r.send for r in reductions)))
    for r, f, h in zip(reductions, fresh, held):
        r.fresh, r.send = f, h
    return value


def per_device(
    tokens, cotangent, conv_text, conv_patch, proj_query, bias_query, proj_key, proj_value, bias_value,
    proj_output, bias_output, rel_order, rel_horiz, rel_vert, norm_gain, norm_shift, expand_weight,
    expand_bias, reduce_weight, reduce_bias, final_gain, final_shift, text_count, box_left, box_top,
):
    pages_here, stretch, width = tokens.shape
    n_seq = lax.axis_size("seq")
    n_pages = lax.axis_size("pages")
    assert pages_here == n_seq and n_pages & (n_pages - 1) == 0
    place = lax.axis_index("seq")
    heads, nb = rel_order.shape
    ff = expand_weight.shape[1]
    pick = lambda a: lax.dynamic_index_in_dim(a, place, 0, keepdims=False)
    count, left, top = pick(text_count), pick(box_left), pick(box_top)
    blocks = spread(rotated(tokens))
    core = lax.axis_index("pages") & 1
    info = jnp.stack([place, count, core]).astype(jnp.int32)
    turn = turn_matrix(width, n_pages, core) if width // n_pages % 16 else jnp.zeros((8, 128), BF)
    cells = jnp.arange(BOX, dtype=jnp.int32)
    oh = jnp.concatenate([left[:, None] == cells[None], top[:, None] == cells[None]], 1).astype(BF)
    oht = jnp.concatenate([left[None] == cells[::-1, None], top[None] == cells[::-1, None]], 0).astype(BF)
    wt, od, edge = tables(rel_order, rel_horiz, rel_vert)
    pm, ct = patch_masks(), text_taps(conv_text)
    cp = jnp.pad(conv_patch.reshape(9, width), ((0, 7), (0, 0)))

    cot_out, blocks = lax.optimization_barrier((rotated(cotangent), blocks))
    cots = spread(cot_out)
    settled, et, q, k, v, probs, att = front(
        info, edge, blocks, ct, cp, pm, turn, proj_query, bias_query, proj_key, proj_value, bias_value, oh, wt, od, width // n_pages)
    *mixed, xh, rs, fl, gp, ds, dr, grk, grs, sm = middle(
        info, cots, att, settled, proj_output, bias_output, norm_gain, norm_shift, expand_weight,
        expand_bias, reduce_weight, reduce_bias, final_gain, final_shift, turn, ff // n_pages)
    c_reduce = Reduction(grk, grs)
    c_reduce.step()
    mixed = spread(mixed)
    done = back(info, width // n_pages, 0, 2, dr, ds, reduce_weight, gp, expand_weight, fl, turn)
    done = tie(done, c_reduce)
    c_reduce.step()
    done = back(info, width // n_pages, 2, ff // width - 2, dr, done[3], reduce_weight, gp, expand_weight, fl, turn, done[:3],
                (xh, rs, norm_gain, att, proj_output))
    done, mixed = tie((done, mixed), c_reduce)
    gek, ges, be, df, da, sm2 = done
    c_expand = Reduction(gek, ges)
    heads_of = lambda first, count, da, acc, filled=(): heads_back(
        first, count, probs, q, k, v, da, att, oh, oht, et, proj_query, proj_key, proj_value, acc, filled)
    cuts = (0, heads // 2, heads)
    c_reduce.step()
    c_expand.step()
    done = heads_of(0, cuts[1], da, df)
    done, da = tie((done, da), c_reduce, c_expand)
    for first, last in zip(cuts[1:-1], cuts[2:]):
        c_reduce.step()
        c_expand.step()
        done = heads_of(first, last - first, da, done[4], done[:4])
        done, da = tie((done, da), c_reduce, c_expand)
    gqk, gqs, qb, diag, acc = done
    c_qkv = Reduction(gqk, gqs)
    for r in (c_reduce, c_expand, c_qkv):
        if not r.over():
            r.step()
    *gts, small = encode_back(info, blocks, acc, ct, cp, pm, sm, sm2, be, qb)
    rounds = [("pages", 1 << b) for b in range(n_pages.bit_length() - 1)] + [("seq", 1 << b) for b in range(n_seq.bit_length() - 1)]
    hop = lambda d: lax.ppermute(gts[d], "seq", [(i, (i + d) % n_seq) for i in range(n_seq)])
    work = [c_reduce, c_expand, c_qkv]
    for r, name in zip(work, ("reduce", "expand", "qkv")):
        r.name = name
    bias = jnp.concatenate(bias_grads(diag, nb), 1)
    bias = jnp.pad(bias, ((0, 0), (0, 128 - 3 * nb))).reshape(-1, width)
    hops = {0: (1,), 1: (3,), 2: (2,)}
    turns = [rounds[1:3], rounds[:1] + rounds[3:4], rounds[4:]] if len(rounds) == 5 else [rounds]
    layouts = {
        "reduce": None,
        "expand": [[(0, ff)], [(ff, width)]],
        "qkv": [[(384 * p + 128 * n, 128) for p in range(heads // 2)] for n in range(3)],
    }
    ready = {}
    phase = 0
    while turns or not c_qkv.over():
        gts, small, bias, ready = tie((gts, small, bias, ready), *work)
        if phase == 0:
            small = lax.dynamic_update_slice(small, bias, (24 + ff // width, 0))
            ready["mixed"] = restack(info, mixed, BF)
        for r in work:
            if not r.over():
                r.step()
            elif r.own is not None and r is not c_qkv:
                ready[r.name] = r.result(info, layouts[r.name])
                r.own, r.fresh = None, []
        for d in hops.get(phase, ()):
            gts = [hop(d) if e == d else part for e, part in enumerate(gts)]
        for axis, bit in turns.pop(0) if turns else ():
            small = small + swap(small, axis, bit)
        phase += 1
    (mixed_out,) = ready["mixed"]
    (o_reduce,), (o_expand, o_output) = (
        ready[r.name] if r.name in ready else r.result(info, layouts[r.name]) for r in (c_reduce, c_expand))
    (grad_tokens,) = restack(info, gts, F32)
    smalls = unpack(small, heads, nb, ff)
    (grad_tokens, smalls, o_reduce, o_expand, o_output), c_qkv.fresh = lax.optimization_barrier(
        ((grad_tokens, smalls, o_reduce, o_expand, o_output), c_qkv.fresh))
    o_query, o_key, o_value = c_qkv.result(info, layouts["qkv"])

    (g_conv_text, g_conv_patch, g_qb, g_vb, g_ob, g_order, g_horiz, g_vert, g_ng, g_ns, g_be, g_rb, g_fg, g_fs) = smalls
    return (
        mixed_out, grad_tokens, g_conv_text, g_conv_patch, o_query, g_qb, o_key, o_value, g_vb,
        o_output, g_ob, g_order, g_horiz, g_vert, g_ng, g_ns, o_expand, g_be, o_reduce, g_rb, g_fg, g_fs,
    )


def solution(mesh):
    placed = (
        P("pages", "seq", None),
        P("pages", "seq", None),
        P(),
        P(),
        P(),
        P(),
        P(),
        P(),
        P(),
        P(),
        P(),
        P(),
        P(),
        P(),
        P(),
        P(),
        P(),
        P(),
        P(),
        P(),
        P(),
        P(),
        P("pages"),
        P("pages", None),
        P("pages", None),
    )
    return jax.shard_map(
        per_device,
        mesh=mesh,
        in_specs=placed,
        out_specs=(
            P("pages", "seq", None),
            P("pages", "seq", None),
            P(),
            P(),
            P("pages", None),
            P(),
            P("pages", None),
            P("pages", None),
            P(),
            P("pages", None),
            P(),
            P(),
            P(),
            P(),
            P(),
            P(),
            P("pages", None),
            P(),
            P("pages", None),
            P(),
            P(),
            P(),
        ),
        check_vma=False,
    )
```

```python
import functools
import jax
import jax.numpy as jnp
from jax import lax
from jax.experimental import pallas as pl
from jax.experimental.pallas import tpu as pltpu
from jax.sharding import PartitionSpec as P

BF = jnp.bfloat16
F32 = jnp.float32
TEXT = 512
GRID = 7
SPAN = 16
EPS = 1e-06
SCALE = 0.125
NEG = -1e30
BOX = 64
RT = 64
LR = 32
EDGE = 16
CELLS = 56
OFFSETS = (-128, -64, 0, 64)
TAPS = (-3, -2, -1, 0, 1, 2, 3)
ERF_P = 0.33
ERF_Q = (0.18635791540145874, 0.1829543262720108, 0.20123349130153656, 0.047190189361572266,
         0.4085558354854584, -0.35120898485183716, 0.4602709114551544, -0.1353536993265152)


def dot(a, b):
    return jnp.dot(a, b, preferred_element_type=F32)


def dot_t(a, b):
    return lax.dot_general(a, b, (((1,), (1,)), ((), ())), preferred_element_type=F32)


def t_dot(a, b):
    return lax.dot_general(a, b, (((0,), (0,)), ((), ())), preferred_element_type=F32)


def whole(shape, buffers=1):
    return pl.BlockSpec(shape, lambda *_: (0,) * len(shape), pipeline_mode=pl.Buffered(buffers))


def whole_out(shape):
    return pl.BlockSpec(shape, lambda *_: (0,) * len(shape))


def lanes(n):
    return [slice(128 * c, 128 * (c + 1)) for c in range(n // 128)]


def line(ref, part=slice(None)):
    return ref[part].reshape(1, -1)


def row_sum(x):
    return jnp.sum(x, axis=0, keepdims=True)


def fold(x):
    out = x[:8]
    for r in range(8, x.shape[0], 8):
        out = out + x[r : r + 8]
    return out


def shift_rows(window, offset, rows):
    if offset == 0:
        return window[8 : 8 + rows]
    return pltpu.roll(window, (-offset) % window.shape[0], 0)[8 : 8 + rows]


def gather_page(dest, row0, place, n_seq, own, others):
    stretch = own.shape[0]
    for d, block in enumerate((own,) + tuple(others)):
        source = lax.rem(place - d + n_seq, n_seq)
        dest[pl.ds(pl.multiple_of(row0 + source * stretch, 16), stretch), :] = block[...].astype(dest.dtype)


def turned_transpose(x_ref, turn_ref, core, block, dest, raw):
    rows = dest.shape[0]
    if block % 16:
        dest[...] = dot_t(turn_ref[...], x_ref[...]).astype(BF)
        return
    raw[...] = jnp.transpose(x_ref[...])
    half = rows // 2
    for k in range(half // block):
        for side in range(2):
            parity = core if side == 0 else 1 - core
            source = pl.multiple_of((2 * k + parity) * block, 16)
            dest[side * half + k * block : side * half + (k + 1) * block, :] = raw[pl.ds(source, block), :]


def moves(pairs, sems):
    return [pltpu.make_async_copy(source, dest, sems.at[n]) for n, (source, dest) in enumerate(pairs)]


def start(copies):
    for c in copies:
        c.start()


def wait(copies):
    for c in copies:
        c.wait()


def front_kernel(info_ref, edge_ref, *refs, n_seq, block):
    blocks = refs[:n_seq]
    (ct_ref, cp_ref, pm_ref, turn_ref, wq_any, bq_ref, wk_any, wv_any, bv_ref, oh_ref, wt_ref, ord_ref,
     set_any, et_any, q_any, k_any, v_any, p_ref, o_ref,
     entry_ref, xs_ref, ms_ref, ka_ref, qa_ref, s_ref, raw_ref,
     set_ref, et_ref, q_ref, k_ref, v_ref, wq_ref, wk_ref, wv_ref, in_sems, out_sems) = refs[n_seq:]
    g = pl.program_id(0)
    arriving = moves([(wq_any, wq_ref), (wk_any, wk_ref), (wv_any, wv_ref)], in_sems)
    leaving = moves([(set_ref, set_any), (et_ref, et_any), (q_ref, q_any), (k_ref, k_any), (v_ref, v_any)], out_sems)
    length, width = entry_ref.shape
    place, count = info_ref[0], info_ref[1]

    @pl.when(g == 0)
    def _():
        start(arriving)
        zero = jnp.zeros((EDGE, width), F32)
        xs_ref[0:EDGE, :] = zero
        xs_ref[EDGE + length :, :] = zero
        ms_ref[0:EDGE, :] = zero
        ms_ref[EDGE + length :, :] = zero
        gather_page(xs_ref, EDGE, place, n_seq, blocks[0], blocks[1:])

        def mask_chunk(i, carry):
            r0 = pl.multiple_of(i * RT, RT)
            keep = (r0 + lax.broadcasted_iota(jnp.int32, (RT, 128), 0)) < count
            for c in lanes(width):
                ms_ref[pl.ds(r0 + EDGE, RT), c] = jnp.where(keep, xs_ref[pl.ds(r0 + EDGE, RT), c], 0.0)
            return carry

        lax.fori_loop(0, length // RT, mask_chunk, 0)

        def conv_chunk(i, carry):
            r0 = pl.multiple_of(i * RT, RT)
            keep = (r0 + lax.broadcasted_iota(jnp.int32, (RT, 128), 0)) < count
            for c in lanes(width):
                window = ms_ref[pl.ds(r0 + EDGE - 8, RT + 16), c]
                term = None
                for n, d in enumerate(TAPS):
                    part = shift_rows(window, d, RT) * ct_ref[n : n + 1, c]
                    term = part if term is None else term + part
                set_ref[pl.ds(r0, RT), c] = xs_ref[pl.ds(r0 + EDGE, RT), c] + jnp.where(keep, term, 0.0)
            return carry

        lax.fori_loop(0, length // RT, conv_chunk, 0)
        for c in lanes(width):
            window = xs_ref[EDGE + TEXT - 8 : EDGE + TEXT + CELLS + 8, c]
            term = jnp.zeros((CELLS, 128), F32)
            for n in range(9):
                off = (n // 3 - 1) * GRID + n % 3 - 1
                term = term + shift_rows(window, off, CELLS) * (cp_ref[n : n + 1, c] * pm_ref[:, n : n + 1])
            set_ref[TEXT : TEXT + CELLS, c] = set_ref[TEXT : TEXT + CELLS, c] + term
        entry_ref[...] = set_ref[...].astype(BF)
        turned_transpose(entry_ref, turn_ref, info_ref[2], block, et_ref, raw_ref)
        wait(arriving)
        for c in range(width // 256):
            s = slice(256 * c, 256 * (c + 1))
            q_ref[:, s] = (dot(entry_ref[...], wq_ref[:, s]) + line(bq_ref, s)).astype(BF) * jnp.asarray(SCALE, BF)
            k_ref[:, s] = dot(entry_ref[...], wk_ref[:, s]).astype(BF)
            v_ref[:, s] = (dot(entry_ref[...], wv_ref[:, s]) + line(bv_ref, s)).astype(BF)
        ka_ref[:, 128:256] = oh_ref[...]
        ka_ref[:, 256:384] = oh_ref[...]
        start(leaving)

    @pl.when(g == pl.num_programs(0) - 1)
    def _():
        wait(leaving)

    pair = pl.ds(pl.multiple_of(g * 128, 128), 128)
    ka_ref[:, 0:128] = k_ref[:, pair]
    lane = lax.broadcasted_iota(jnp.int32, (length, 128), 1)
    for e in range(2):
        mine = (lane < 64) if e == 0 else (lane >= 64)
        qa_ref[e, :, 0:128] = jnp.where(mine, q_ref[:, pair], jnp.zeros((), BF))
        qa_ref[e, :, 128:384] = dot(oh_ref[...], wt_ref[e]).astype(BF)
        s_ref[e] = dot_t(qa_ref[e], ka_ref[...])
    cols = (length + 127) // 128
    at = lax.broadcasted_iota(jnp.int32, (1, length), 1)
    ok = (at < count) | ((at >= TEXT) & (at < TEXT + GRID * GRID))
    bar = jnp.where(ok, 0.0, NEG)
    outs = []
    for e in range(2):
        left, right = edge_ref[2 * g + e, 0], edge_ref[2 * g + e, 1]
        for a in range(length // RT):
            r0 = a * RT
            parts = []
            for b in range(cols):
                w = min(128, length - 128 * b)
                d = 128 * b - r0
                t = s_ref[e, r0 : r0 + RT, 128 * b : 128 * b + w]
                m = bar[:, 128 * b : 128 * b + w]
                if d in OFFSETS:
                    t = t + ord_ref[e, OFFSETS.index(d)][:, :w] + m
                else:
                    t = t + (m + (left if d < 0 else right))
                parts.append(t)
            t = jnp.concatenate(parts, 1)
            top = jnp.max(t, axis=1, keepdims=True)
            ex = jnp.exp(t - top)
            total = jnp.sum(ex, axis=1, keepdims=True)
            p_ref[e, r0 : r0 + RT, :] = (ex * (1.0 / total)).astype(BF)
        outs.append(dot(p_ref[e], v_ref[:, pair]))
    o_ref[...] = jnp.where(lane < 64, outs[0], outs[1]).astype(BF)


def front(info, edge, blocks, ct, cp, pm, turn, wq, bq, wk, wv, bv, oh, wt, od, block):
    n_seq = len(blocks)
    stretch, width = blocks[0].shape
    length = n_seq * stretch
    heads = wt.shape[0]
    sds = jax.ShapeDtypeStruct
    flops = 2 * length * width * width * 3 + heads * 2 * length * length * (384 + 128)
    return pl.pallas_call(
        functools.partial(front_kernel, n_seq=n_seq, block=block),
        out_shape=(sds((length, width), F32), sds((width, length), BF)) + (sds((length, width), BF),) * 3
        + (sds((heads, length, length), BF), sds((length, width), BF)),
        grid_spec=pltpu.PrefetchScalarGridSpec(
            num_scalar_prefetch=2, grid=(heads // 2,),
            in_specs=[whole((stretch, width))] * n_seq
            + [whole(ct.shape), whole(cp.shape), whole(pm.shape), whole(turn.shape), pl.BlockSpec(memory_space=pl.ANY), whole(bq.shape), pl.BlockSpec(memory_space=pl.ANY),
               pl.BlockSpec(memory_space=pl.ANY), whole(bv.shape), whole(oh.shape),
               pl.BlockSpec((2, 128, 256), lambda g, *_: (g, 0, 0)),
               pl.BlockSpec((2, len(OFFSETS), RT, 128), lambda g, *_: (g, 0, 0, 0))],
            out_specs=[pl.BlockSpec(memory_space=pl.ANY)] * 5
            + [pl.BlockSpec((2, length, length), lambda g, *_: (g, 0, 0)), pl.BlockSpec((length, 128), lambda g, *_: (0, g))],
            scratch_shapes=[pltpu.VMEM((length, width), BF), pltpu.VMEM((length + 2 * EDGE, width), F32), pltpu.VMEM((length + 2 * EDGE, width), F32),
                            pltpu.VMEM((length, 384), BF), pltpu.VMEM((2, length, 384), BF), pltpu.VMEM((2, length, length), F32), pltpu.VMEM((width, length), BF),
                            pltpu.VMEM((length, width), F32), pltpu.VMEM((width, length), BF)]
            + [pltpu.VMEM((length, width), BF)] * 3 + [pltpu.VMEM((width, width), BF)] * 3
            + [pltpu.SemaphoreType.DMA((3,)), pltpu.SemaphoreType.DMA((5,))],
        ),
        cost_estimate=pl.CostEstimate(flops=25_000_000_000, bytes_accessed=8 << 20, transcendentals=0),
        name="front",
    )(info, edge, *blocks, ct, cp, pm, turn, wq, bq, wk, wv, bv, oh, wt, od)


def norm_stats(u):
    mean = jnp.mean(u, axis=1, keepdims=True)
    c = u - mean
    rs = lax.rsqrt(jnp.mean(c * c, axis=1, keepdims=True) + EPS)
    return c * rs, rs


def norm_back(u, xhat, rs):
    return rs * (u - jnp.mean(u, axis=1, keepdims=True) - xhat * jnp.mean(u * xhat, axis=1, keepdims=True))


def gelu_pair(x):
    t = 1.0 / (1.0 + jnp.abs(x) * (ERF_P * 0.7071067811865476))
    bell = jnp.exp2(x * x * -0.7213475204444817)
    q = jnp.full_like(t, 0.5 * ERF_Q[7])
    for k in range(6, -1, -1):
        q = q * t + 0.5 * ERF_Q[k]
    tail = q * t * bell
    cdf = jnp.where(x < 0, tail, 1.0 - tail)
    return x * cdf, cdf + x * bell * 0.3989422804014327


def middle_kernel(info_ref, *refs, n_seq, tiles, tile, block):
    cots = refs[:n_seq]
    (att_ref, set_ref, wo_ref, bo_ref, ng_ref, ns_ref, w1_ref, b1_ref, w2_ref, b2_ref, fg_ref, fs_ref, turn_ref) = refs[n_seq : n_seq + 13]
    outs = refs[n_seq + 13 :]
    mixed = outs[:n_seq]
    (xh_any, rs_any, fl_any, gp_ref, ds_any, dr_any, gk_ref, gs_ref, sm_ref, act_ref, fn_ref, acc_ref, cot_ref, mix_ref, e_ref, g_ref, b1_rows,
     xh_ref, rs_ref, fl_ref, ds_ref, dr_ref, cot_sems, norm_sems, out_sems) = outs[n_seq:]
    i = pl.program_id(0)
    length, width = fl_ref.shape
    place = info_ref[0]
    stretch = length // n_seq
    block_of = lambda ref, d: ref.at[pl.ds(pl.multiple_of(lax.rem(place + d, n_seq) * stretch, 16), stretch), :]
    arriving = moves([(cots[d], block_of(cot_ref, n_seq - d)) for d in range(n_seq)], cot_sems)
    normed = moves([(xh_ref, xh_any), (rs_ref, rs_any), (fl_ref, fl_any)], norm_sems)
    leaving = moves([(ds_ref, ds_any), (dr_ref, dr_any)] + [(block_of(mix_ref, d), mixed[d]) for d in range(n_seq)], out_sems)

    @pl.when(i == 0)
    def _():
        start(arriving)
        for c in range(width // 256):
            s = slice(256 * c, 256 * (c + 1))
            acc_ref[:, s] = dot(att_ref[...], wo_ref[:, s])

        def chunk(j, carry):
            r = pl.ds(pl.multiple_of(j * LR, LR), LR)
            u = set_ref[r, :] + (acc_ref[r, :] + line(bo_ref))
            xhat, rs = norm_stats(u)
            xh_ref[r, :] = xhat
            rs_ref[r, :] = jnp.broadcast_to(rs, (LR, 128))
            fn = xhat * line(ng_ref) + line(ns_ref)
            fn_ref[r, :] = fn
            fl_ref[r, :] = fn.astype(BF)
            acc_ref[r, :] = jnp.broadcast_to(line(b2_ref), (LR, width))
            return carry

        lax.fori_loop(0, length // LR, chunk, 0, unroll=6)
        start(normed)
        for t in range(tiles):
            b1_rows[t] = line(b1_ref, slice(t * tile, (t + 1) * tile))

    @pl.when(i < tiles)
    def _():
        half = tile // 3
        for n in range(3):
            e_ref[n] = dot(fl_ref[...], w1_ref[:, n * half : (n + 1) * half])
        for n in range(3):
            s = slice(n * half, (n + 1) * half)
            act, gp = gelu_pair(e_ref[n] + b1_rows[i, :, s])
            act_ref[i, :, s] = act.astype(BF)
            gp_ref[:, s] = gp.astype(gp_ref.dtype)
        for c in range(width // 256):
            s = slice(256 * c, 256 * (c + 1))
            acc_ref[:, s] += dot(act_ref[i], w2_ref[:, s])

    @pl.when(i == tiles - 1)
    def _():
        wait(arriving)

        def chunk(j, sums):
            r0 = pl.multiple_of(j * LR, LR)
            r = pl.ds(r0, LR)
            second = fn_ref[r, :] + acc_ref[r, :]
            xhat, rs = norm_stats(second)
            mix_ref[r, :] = (xhat * line(fg_ref) + line(fs_ref)).astype(BF)
            cot = cot_ref[r, :].astype(F32)
            back = norm_back(cot * line(fg_ref), xhat, rs)
            ds_ref[r, :] = back
            low = back.astype(BF)
            dr_ref[r, :] = low
            return (sums[0] + fold(cot * xhat), sums[1] + fold(cot), sums[2] + fold(low.astype(F32)))

        sums = lax.fori_loop(0, length // LR, chunk, (jnp.zeros((8, width), F32),) * 3, unroll=6)
        for n in range(3):
            sm_ref[n : n + 1, :] = row_sum(sums[n])
        start(leaving)

    @pl.when(i == pl.num_programs(0) - 1)
    def _():
        wait(normed)
        wait(leaving)

    @pl.when(i >= tiles)
    def _():
        grad = t_dot(act_ref[i - tiles], dr_ref[...]).astype(BF)
        if 2 * block == tile:
            g_ref[...] = grad
            core = info_ref[2]
            gk_ref[...] = g_ref[pl.ds(pl.multiple_of(core * block, block), block), :]
            gs_ref[...] = g_ref[pl.ds(pl.multiple_of((1 - core) * block, block), block), :]
        else:
            turned = dot(turn_ref[...], grad).astype(BF)
            gk_ref[...] = turned[: tile // 2]
            gs_ref[...] = turned[tile // 2 :]


def middle(info, cots, att, settled, wo, bo, ng, ns, w1, b1, w2, b2, fg, fs, turn, block):
    tile = w1.shape[0]
    n_seq = len(cots)
    stretch, width = cots[0].shape
    length = n_seq * stretch
    ff = w1.shape[1]
    tiles = ff // tile
    sds = jax.ShapeDtypeStruct
    early = lambda i: jnp.minimum(i, tiles - 1)
    late = lambda i: jnp.maximum(i - tiles, 0)
    return pl.pallas_call(
        functools.partial(middle_kernel, n_seq=n_seq, tiles=tiles, tile=tile, block=block),
        out_shape=(sds((stretch, width), BF),) * n_seq
        + (sds((length, width), F32), sds((length, 128), F32), sds((length, width), BF), sds((length, ff), BF),
           sds((length, width), F32), sds((length, width), BF), sds((ff // 2, width), BF), sds((ff // 2, width), BF), sds((8, width), F32)),
        grid_spec=pltpu.PrefetchScalarGridSpec(
            num_scalar_prefetch=1, grid=(2 * tiles,),
            in_specs=[pl.BlockSpec(memory_space=pl.ANY)] * n_seq
            + [whole(att.shape), whole(settled.shape), whole(wo.shape), whole(bo.shape), whole(ng.shape), whole(ns.shape),
               pl.BlockSpec((width, tile), lambda i, *_: (0, early(i))), whole(b1.shape),
               pl.BlockSpec((tile, width), lambda i, *_: (early(i), 0)), whole(b2.shape), whole(fg.shape), whole(fs.shape), whole(turn.shape)],
            out_specs=[pl.BlockSpec(memory_space=pl.ANY)] * (n_seq + 3)
            + [pl.BlockSpec((length, tile), lambda i, *_: (0, early(i))), pl.BlockSpec(memory_space=pl.ANY), pl.BlockSpec(memory_space=pl.ANY),
               pl.BlockSpec((tile // 2, width), lambda i, *_: (late(i), 0)), pl.BlockSpec((tile // 2, width), lambda i, *_: (late(i), 0)),
               whole_out((8, width))],
            scratch_shapes=[pltpu.VMEM((tiles, length, tile), BF), pltpu.VMEM((length, width), F32), pltpu.VMEM((length, width), F32),
                            pltpu.VMEM((length, width), BF), pltpu.VMEM((length, width), BF), pltpu.VMEM((3, length, tile // 3), F32),
                            pltpu.VMEM((tile, width), BF), pltpu.VMEM((tiles, 1, tile), F32),
                            pltpu.VMEM((length, width), F32), pltpu.VMEM((length, 128), F32), pltpu.VMEM((length, width), BF),
                            pltpu.VMEM((length, width), F32), pltpu.VMEM((length, width), BF),
                            pltpu.SemaphoreType.DMA((n_seq,)), pltpu.SemaphoreType.DMA((3,)), pltpu.SemaphoreType.DMA((2 + n_seq,))],
        ),
        cost_estimate=pl.CostEstimate(flops=35_000_000_000, bytes_accessed=8 << 20, transcendentals=0),
        name="middle",
    )(info, *cots, att, settled, wo, bo, ng, ns, w1, b1, w2, b2, fg, fs, turn)


def back_kernel(info_ref, *refs, tiles, last, block):
    core = info_ref[2]
    if last:
        (dr_ref, in_ref, w2_ref, gp_ref, w1_ref, fl_ref, turn_ref, xh_any, rs_any, ng_ref, att_any, wo_any) = refs[:12]
        (gk_ref, gs_ref, be_ref, df_ref, da_ref, sm_ref, flt_ref, raw_ref, acc_ref, db_ref,
         xh_ref, rs_ref, att_ref, wo_ref, sems) = refs[-15:]
        arriving = moves([(xh_any, xh_ref), (rs_any, rs_ref), (att_any, att_ref), (wo_any, wo_ref)], sems)
    else:
        (dr_ref, in_ref, w2_ref, gp_ref, w1_ref, fl_ref, turn_ref) = refs[:7]
        (gk_ref, gs_ref, be_ref, acc_ref, flt_ref, raw_ref) = refs[-6:]
    i = pl.program_id(0)
    length, width = dr_ref.shape

    @pl.when(i == 0)
    def _():
        if last:
            start(arriving)
        turned_transpose(fl_ref, turn_ref, core, block, flt_ref, raw_ref)
        acc_ref[...] = in_ref[...]

    @pl.when(i < tiles)
    def _():
        de = dot_t(dr_ref[...], w2_ref[...]) * gp_ref[...].astype(F32)
        de = de.astype(BF)
        be_ref[...] = row_sum(de.astype(F32))
        grad = dot(flt_ref[...], de).astype(BF)
        gk_ref[...] = grad[: width // 2]
        gs_ref[...] = grad[width // 2 :]
        acc_ref[...] += dot_t(de, w1_ref[...])

    if not last:
        return

    @pl.when(i == tiles)
    def _():
        wait(arriving)

        def chunk(j, sums):
            r = pl.ds(pl.multiple_of(j * LR, LR), LR)
            first = acc_ref[r, :]
            xhat = xh_ref[r, :]
            back = norm_back(first * line(ng_ref), xhat, rs_ref[r, 0:1])
            df_ref[r, :] = back
            low = back.astype(BF)
            db_ref[r, :] = low
            return (sums[0] + fold(first * xhat), sums[1] + fold(first), sums[2] + fold(low.astype(F32)))

        sums = lax.fori_loop(0, length // LR, chunk, (jnp.zeros((8, width), F32),) * 3, unroll=6)
        for n in range(3):
            sm_ref[n : n + 1, :] = row_sum(sums[n])
        da_ref[...] = dot_t(db_ref[...], wo_ref[...]).astype(BF)
        turned_transpose(att_ref, turn_ref, core, block, flt_ref, raw_ref)
        grad = dot(flt_ref[...], db_ref[...]).astype(BF)
        gk_ref[...] = grad[: width // 2]
        gs_ref[...] = grad[width // 2 :]


def back(info, block, first, tiles, dr, acc, w2, gp, w1, fl, turn, filled=(), norm=None):
    length, width = dr.shape
    ff = w1.shape[1]
    last = norm is not None
    sds = jax.ShapeDtypeStruct
    at = lambda i: jnp.minimum(i, tiles - 1) + first
    grad = pl.BlockSpec((width // 2, width), lambda i, *_: (0, i + first))
    args = [dr, acc, w2, gp, w1, fl, turn] + list(norm or ())
    out_shape = [sds((width // 2, ff + width), BF), sds((width // 2, ff + width), BF), sds((1, ff), F32), sds((length, width), F32)]
    out_specs = [grad, grad, pl.BlockSpec((1, width), lambda i, *_: (0, at(i))), whole_out((length, width))]
    scratch = [pltpu.VMEM((width, length), BF), pltpu.VMEM((width, length), BF)]
    if last:
        out_shape += [sds((length, width), BF), sds((8, width), F32)]
        out_specs += [whole_out((length, width)), whole_out((8, width))]
        scratch += [pltpu.VMEM((length, width), F32), pltpu.VMEM((length, width), BF), pltpu.VMEM((length, width), F32),
                    pltpu.VMEM((length, 128), F32), pltpu.VMEM((length, width), BF), pltpu.VMEM((width, width), BF),
                    pltpu.SemaphoreType.DMA((4,))]
    return pl.pallas_call(
        functools.partial(back_kernel, tiles=tiles, last=last, block=block),
        out_shape=tuple(out_shape),
        grid_spec=pltpu.PrefetchScalarGridSpec(
            num_scalar_prefetch=1, grid=(tiles + last,),
            in_specs=[whole(dr.shape), whole(acc.shape), pl.BlockSpec((width, width), lambda i, *_: (at(i), 0)),
                      pl.BlockSpec((length, width), lambda i, *_: (0, at(i))), pl.BlockSpec((width, width), lambda i, *_: (0, at(i)))]
            + [pl.BlockSpec(memory_space=pl.ANY) if n in (7, 8, 10, 11) else whole(x.shape) for n, x in enumerate(args) if n >= 5]
            + [pl.BlockSpec(memory_space=pl.ANY)] * len(filled),
            out_specs=out_specs,
            scratch_shapes=scratch,
        ),
        input_output_aliases={1 + len(args) + n: n for n in range(len(filled))},
        cost_estimate=pl.CostEstimate(flops=12_000_000_000, bytes_accessed=8 << 20, transcendentals=0),
        name="back",
    )(info, *args, *filled)


def diagonals(x):
    wide = jnp.concatenate([x, jnp.zeros_like(x)], 1)
    return row_sum(pltpu.roll(wide, 0, 1, stride=1, stride_axis=0))


def hi_lo(x):
    hi = x.astype(BF)
    return jnp.concatenate([hi, (x - hi.astype(F32)).astype(BF)], 1)


def heads_kernel(*refs):
    (p_ref, q_ref, k_ref, v_ref, do_ref, o_ref, oh_ref, oht_ref, et_any, wq_ref, wk_ref, wv_ref, in_any) = refs[:13]
    (gk_ref, gs_ref, qb_ref, diag_ref, acc_ref, va_ref, rhs_ref, dsc_ref, dp_ref, w_ref, d_ref, et_ref, sems) = refs[-13:]
    arriving = moves([(et_any, et_ref), (in_any, acc_ref)], sems)
    g = pl.program_id(0)
    length = q_ref.shape[0]
    lane = lax.broadcasted_iota(jnp.int32, (length, 128), 1)

    @pl.when(g == 0)
    def _():
        va_ref[:, 128:256] = jnp.where(lane < 2, 1.0, 0.0).astype(BF)
        rhs_ref[:, 128:256] = oh_ref[...]
        start(arriving)

    va_ref[:, 0:128] = v_ref[...]
    rhs_ref[:, 0:128] = k_ref[...]
    cols = (length + 127) // 128
    flip = (lax.broadcasted_iota(jnp.int32, (RT, RT), 0) + lax.broadcasted_iota(jnp.int32, (RT, RT), 1) == RT - 1).astype(F32).astype(BF)
    do = do_ref[...]
    prod = do.astype(F32) * o_ref[...].astype(F32)
    res = []
    for e in range(2):
        mine = (lane < 64) if e == 0 else (lane >= 64)
        inner = -jnp.sum(jnp.where(mine, prod, 0.0), axis=1, keepdims=True)
        hi = inner.astype(BF)
        lo = inner - hi.astype(F32)
        ext = jnp.where(lane == 0, hi.astype(F32), jnp.where(lane == 1, lo, 0.0)).astype(BF)
        da = jnp.concatenate([jnp.where(mine, do, jnp.zeros((), BF)), ext], 1)
        dp_ref[e] = dot_t(da, va_ref[...])
    for e in range(2):
        sums = {}
        for a in range(length // RT):
            r0 = a * RT
            ds = p_ref[e, r0 : r0 + RT, :].astype(F32) * dp_ref[e, r0 : r0 + RT, :]
            dsc_ref[e, r0 : r0 + RT, :] = ds.astype(BF)
            for b in range(cols):
                w = min(128, length - 128 * b)
                d = 128 * b - r0
                t = ds[:, 128 * b : 128 * b + w]
                if w < 128:
                    t = jnp.concatenate([t, jnp.zeros((RT, 128 - w), F32)], 1)
                key = OFFSETS.index(d) if d in OFFSETS else (4 if d < 0 else 5)
                sums[key] = sums[key] + t if key in sums else t
        for n in range(4):
            turned = dot(flip, hi_lo(sums[n]))
            diag_ref[e, n : n + 1, :] = diagonals(turned[:, 0:128] + turned[:, 128:256])
        diag_ref[e, 4:5, 0:128] = row_sum(sums[4])
        diag_ref[e, 4:5, 128:256] = row_sum(sums[5])
        r = dot(dsc_ref[e], rhs_ref[...])
        hh = dot(oht_ref[...], hi_lo(r[:, 128:256]))
        hist = hh[:, 0:128] + hh[:, 128:256]
        half = lane[:BOX] < BOX
        diag_ref[e, 5:6, :] = diagonals(jnp.where(half, hist[:BOX], 0.0))
        diag_ref[e, 6:7, :] = diagonals(jnp.where(half, 0.0, hist[BOX:]))
        diag_ref[e, 7:8, :] = jnp.zeros((1, 256), F32)
        dk = t_dot(dsc_ref[e], q_ref[...])
        dv = t_dot(p_ref[e], do)
        res.append((r[:, 0:128], dk, dv))
    first = lane < 64
    dq = (jnp.where(first, res[0][0], res[1][0]) * SCALE).astype(BF)
    dk = jnp.where(first, res[0][1], res[1][1]).astype(BF)
    dv = jnp.where(first, res[0][2], res[1][2]).astype(BF)

    @pl.when(g == 0)
    def _():
        wait(arriving)

    d_ref[:, 0:128] = dq
    d_ref[:, 128:256] = dk
    d_ref[:, 256:384] = dv
    qb_ref[0:1, :] = row_sum(dq.astype(F32))
    qb_ref[1:2, :] = row_sum(dv.astype(F32))
    w_ref[:, 0:128] = wq_ref[...]
    w_ref[:, 128:256] = wk_ref[...]
    w_ref[:, 256:384] = wv_ref[...]
    grad = dot(et_ref[...], d_ref[...]).astype(BF)
    gk_ref[...] = grad[: grad.shape[0] // 2]
    gs_ref[...] = grad[grad.shape[0] // 2 :]
    acc_ref[...] += dot_t(d_ref[...], w_ref[...])


def heads_back(first, count, probs, q, k, v, do, o, oh, oht, et, wq, wk, wv, acc, filled=()):
    heads = probs.shape[0]
    length, width = q.shape
    steps = count // 2
    base = first // 2
    sds = jax.ShapeDtypeStruct
    col = pl.BlockSpec((length, 128), lambda g: (0, g + base))
    wcol = pl.BlockSpec((width, 128), lambda g: (0, g + base))
    flops = 2 * length * width * 64 * count * 6 + count * 2 * length * length * (256 + 256 + 128 + 128)
    return pl.pallas_call(
        heads_kernel,
        out_shape=(sds((width // 2, 3 * width), BF), sds((width // 2, 3 * width), BF), sds((8, width), F32), sds((heads, 8, 256), F32), sds((length, width), F32)),
        grid=(steps,),
        in_specs=[pl.BlockSpec((2, length, length), lambda g: (g + base, 0, 0)), col, col, col, col, col, whole(oh.shape), whole(oht.shape),
                  pl.BlockSpec(memory_space=pl.ANY), wcol, wcol, wcol] + [pl.BlockSpec(memory_space=pl.ANY)] * (1 + len(filled)),
        out_specs=[pl.BlockSpec((width // 2, 384), lambda g: (0, g + base)), pl.BlockSpec((width // 2, 384), lambda g: (0, g + base)),
                   pl.BlockSpec((8, 128), lambda g: (0, g + base)), pl.BlockSpec((2, 8, 256), lambda g: (g + base, 0, 0)), whole_out((length, width))],
        input_output_aliases={13 + n: n for n in range(len(filled))},
        scratch_shapes=[pltpu.VMEM((length, 256), BF), pltpu.VMEM((length, 256), BF), pltpu.VMEM((2, length, length), BF),
                        pltpu.VMEM((2, length, length), F32), pltpu.VMEM((width, 384), BF), pltpu.VMEM((length, 384), BF),
                        pltpu.VMEM((width, length), BF), pltpu.SemaphoreType.DMA((2,))],
        cost_estimate=pl.CostEstimate(flops=20_000_000_000, bytes_accessed=8 << 20, transcendentals=0),
        name="heads_back",
    )(probs, q, k, v, do, o, oh, oht, et, wq, wk, wv, acc, *filled)


def encode_kernel(info_ref, *refs, n_seq):
    blocks = refs[:n_seq]
    in_ref, ct_ref, cp_ref, pm_ref, sm_ref, sm2_ref, be_ref, qb_ref = refs[n_seq : n_seq + 8]
    outs = refs[n_seq + 8 :]
    grads = outs[:n_seq]
    small_ref, acc_ref, gs_ref, ms_ref, gt_ref = outs[n_seq:]
    length, width = in_ref.shape
    place, count = info_ref[0], info_ref[1]
    acc_ref[...] = in_ref[...]
    small_ref[...] = jnp.zeros_like(small_ref)
    small_ref[0:3, :] = sm_ref[0:3, :]
    small_ref[3:6, :] = sm2_ref[0:3, :]
    small_ref[6:8, :] = qb_ref[0:2, :]
    tiles = be_ref.shape[1] // width
    for t in range(tiles):
        small_ref[8 + t : 9 + t, :] = be_ref[:, t * width : (t + 1) * width]
    taps, cells = 8 + tiles, 15 + tiles
    zero = jnp.zeros((EDGE, width), F32)
    gs_ref[0:EDGE, :] = zero
    gs_ref[EDGE + length :, :] = zero
    ms_ref[0:EDGE, :] = zero
    ms_ref[EDGE + length :, :] = zero
    gather_page(ms_ref, EDGE, place, n_seq, blocks[0], blocks[1:])
    for c in lanes(width):
        tok = ms_ref[EDGE + TEXT - 8 : EDGE + TEXT + CELLS + 8, c]
        own = acc_ref[TEXT : TEXT + CELLS, c]
        window = jnp.concatenate([acc_ref[TEXT - 8 : TEXT + CELLS, c], jnp.zeros((8, 128), F32)], 0)
        term = jnp.zeros((CELLS, 128), F32)
        for n in range(9):
            off = (n // 3 - 1) * GRID + n % 3 - 1
            term = term + shift_rows(window, -off, CELLS) * (cp_ref[n : n + 1, c] * pm_ref[:, 8 - n : 9 - n])
            small_ref[cells + n : cells + n + 1, c] = row_sum(own * shift_rows(tok, off, CELLS) * pm_ref[:, n : n + 1])
        gt_ref[:, c] = term

    def split_chunk(j, carry):
        r0 = pl.multiple_of(j * RT, RT)
        keep = (r0 + lax.broadcasted_iota(jnp.int32, (RT, 128), 0)) < count
        for c in lanes(width):
            dset = acc_ref[pl.ds(r0, RT), c]
            gs_ref[pl.ds(r0 + EDGE, RT), c] = jnp.where(keep, dset, 0.0)
            ms_ref[pl.ds(r0 + EDGE, RT), c] = jnp.where(keep, ms_ref[pl.ds(r0 + EDGE, RT), c], 0.0)
        return carry

    lax.fori_loop(0, length // RT, split_chunk, 0)
    for c in lanes(width):
        acc_ref[TEXT : TEXT + CELLS, c] = acc_ref[TEXT : TEXT + CELLS, c] + gt_ref[:, c]

    def conv_chunk(j, sums):
        r0 = pl.multiple_of(j * RT, RT)
        keep = (r0 + lax.broadcasted_iota(jnp.int32, (RT, 128), 0)) < count
        out = []
        for n, c in enumerate(lanes(width)):
            window = gs_ref[pl.ds(r0 + EDGE - 8, RT + 16), c]
            own = ms_ref[pl.ds(r0 + EDGE, RT), c]
            term = None
            for m, d in enumerate(TAPS):
                moved = shift_rows(window, -d, RT)
                part = moved * ct_ref[m : m + 1, c]
                term = part if term is None else term + part
                out.append(sums[n * len(TAPS) + m] + row_sum(moved * own))
            acc_ref[pl.ds(r0, RT), c] = acc_ref[pl.ds(r0, RT), c] + jnp.where(keep, term, 0.0)
        return tuple(out)

    zeros = (jnp.zeros((1, 128), F32),) * (len(TAPS) * (width // 128))
    sums = lax.fori_loop(0, length // RT, conv_chunk, zeros)
    for n, c in enumerate(lanes(width)):
        for m in range(len(TAPS)):
            small_ref[taps + m : taps + m + 1, c] = sums[n * len(TAPS) + m]
    stretch = length // n_seq
    for d in range(n_seq):
        dest = lax.rem(place + d, n_seq)
        grads[d][...] = acc_ref[pl.ds(pl.multiple_of(dest * stretch, 16), stretch), :].astype(BF)


def encode_back(info, blocks, d_settled, ct, cp, pm, sm, sm2, be, qb):
    n_seq = len(blocks)
    stretch, width = blocks[0].shape
    length = n_seq * stretch
    sds = jax.ShapeDtypeStruct
    rows = 24 + be.shape[1] // width
    rows += 8 - rows % 8
    return pl.pallas_call(
        functools.partial(encode_kernel, n_seq=n_seq),
        out_shape=(sds((stretch, width), BF),) * n_seq + (sds((rows, width), F32),),
        grid_spec=pltpu.PrefetchScalarGridSpec(
            num_scalar_prefetch=1, grid=(1,),
            in_specs=[whole((stretch, width))] * n_seq + [whole(d_settled.shape), whole(ct.shape), whole(cp.shape), whole(pm.shape), whole(sm.shape), whole(sm2.shape), whole(be.shape), whole(qb.shape)],
            out_specs=[whole_out((stretch, width))] * n_seq + [whole_out((rows, width))],
            scratch_shapes=[pltpu.VMEM((length, width), F32), pltpu.VMEM((length + 2 * EDGE, width), F32),
                            pltpu.VMEM((length + 2 * EDGE, width), F32), pltpu.VMEM((CELLS, width), F32)],
        ),
        cost_estimate=pl.CostEstimate(flops=10_000_000_000, bytes_accessed=8 << 20, transcendentals=0),
        name="encode_back",
    )(info, *blocks, d_settled, ct, cp, pm, sm, sm2, be, qb)


def turn_matrix(width, n, core):
    block, half = width // n, width // 2
    r = jnp.arange(width, dtype=jnp.int32)
    inner = jnp.where(r < half, r, r - half)
    parity = jnp.where(r < half, core, 1 - core)
    source = (2 * (inner // block) + parity) * block + inner % block
    return (source[:, None] == r[None]).astype(BF)


def restack_kernel(info_ref, *refs, n, layout):
    parts, outs = refs[:n], refs[n:]
    for d, part in enumerate(parts):
        source = lax.rem(info_ref[0] - d + n, n)
        for out, pieces in zip(outs, layout):
            at = 0
            for start, width in pieces:
                out[source, :, at : at + width] = part[:, start : start + width].astype(out.dtype)
                at += width


def restack(info, parts, dtype, layout=None):
    n = len(parts)
    rows, cols = parts[0].shape
    layout = layout or [[(0, cols)]]
    outs = pl.pallas_call(
        functools.partial(restack_kernel, n=n, layout=layout),
        out_shape=[jax.ShapeDtypeStruct((n, rows, sum(w for _, w in pieces)), dtype) for pieces in layout],
        in_specs=[pl.BlockSpec(memory_space=pltpu.SMEM)] + [pl.BlockSpec(memory_space=pltpu.VMEM)] * n,
        out_specs=[pl.BlockSpec(memory_space=pltpu.VMEM)] * len(layout),
        cost_estimate=pl.CostEstimate(flops=1000, bytes_accessed=1000, transcendentals=0),
        name="restack",
    )(info, *parts)
    return outs


def unpack_kernel(small_ref, *outs, heads, tiles):
    gct, gcp, qb, vb, ob, order, horiz, vert, ng, ns, be, rb, fg, fs = outs
    for row, out in ((0, fg), (1, fs), (2, rb), (3, ng), (4, ns), (5, ob), (6, qb), (7, vb)):
        out[...] = small_ref[row, :]
    width = small_ref.shape[1]
    for t in range(tiles):
        be[t * width : (t + 1) * width] = small_ref[8 + t, :]
    taps, cells, bias = 8 + tiles, 15 + tiles, 24 + tiles
    for s in range(3):
        for t in range(3):
            gct[s, t, :] = small_ref[taps + 3 + (t - 1) * (s + 1), :]
            gcp[s, t, :] = small_ref[cells + 3 * s + t, :]
    nb = order.shape[1]
    per = width // 128
    for h in range(heads):
        row, at = bias + h // per, 128 * (h % per)
        for n, out in enumerate((order, horiz, vert)):
            out[h, :] = small_ref[row, at + n * nb : at + (n + 1) * nb]


def unpack(small, heads, nb, ff):
    width = small.shape[1]
    sds = lambda *shape: jax.ShapeDtypeStruct(shape, F32)
    vec = sds(width)
    return pl.pallas_call(
        functools.partial(unpack_kernel, heads=heads, tiles=ff // width),
        out_shape=(sds(3, 3, width), sds(3, 3, width), vec, vec, vec, sds(heads, nb), sds(heads, nb), sds(heads, nb),
                   vec, vec, sds(ff), vec, vec, vec),
        cost_estimate=pl.CostEstimate(flops=1000, bytes_accessed=1000, transcendentals=0),
        name="unpack",
    )(small)


def one_hot_rows(ids, size):
    return (ids.reshape(1, -1) == jnp.arange(size, dtype=jnp.int32)[:, None]).astype(F32)


def tables(rel_order, rel_horiz, rel_vert):
    heads, nb = rel_order.shape
    high = lax.Precision.HIGHEST
    a = jnp.arange(BOX, dtype=jnp.int32)
    cell = one_hot_rows(jnp.clip(a[None, :] - a[:, None], -SPAN, SPAN) + SPAN, nb)

    def split(table):
        x = jnp.dot(table, cell, precision=high).reshape(heads, BOX, BOX)
        top = lax.reduce_precision(x, 8, 7)
        return top, x - top

    (hh, hl), (vh, vl) = split(rel_horiz), split(rel_vert)
    zero = jnp.zeros_like(hh)
    wt = jnp.concatenate([jnp.concatenate([hh, zero, hl, zero], 2), jnp.concatenate([zero, vh, zero, vl], 2)], 1).astype(BF)
    i = jnp.arange(RT, dtype=jnp.int32)[:, None]
    j = jnp.arange(128, dtype=jnp.int32)[None]
    band = jnp.stack([jnp.clip(d + j - i, -SPAN, SPAN) + SPAN for d in OFFSETS])
    od = jnp.dot(rel_order, one_hot_rows(band, nb), precision=high).reshape(heads, len(OFFSETS), RT, 128)
    edge = jnp.stack([rel_order[:, 0], rel_order[:, -1]], 1)
    return wt, od, edge


def bias_grads(diag, nb):
    heads = diag.shape[0]
    high = lax.Precision.HIGHEST
    at = jnp.arange(256, dtype=jnp.int32)
    step = at - (RT - 1)
    order_bins = jnp.stack([jnp.clip(d + step, -SPAN, SPAN) for d in OFFSETS] + [jnp.where(at < 128, -SPAN, SPAN)]) + SPAN
    order = jnp.dot(diag[:, :5].reshape(heads, -1), one_hot_rows(order_bins, nb).T, precision=high)
    flat = jnp.clip(step, -SPAN, SPAN) + SPAN
    horiz = jnp.dot(diag[:, 5], one_hot_rows(flat, nb).T, precision=high)
    low = jnp.clip(step - BOX, -SPAN, SPAN) + SPAN
    vert = jnp.dot(diag[:, 6], one_hot_rows(low, nb).T, precision=high)
    return order, horiz, vert


def patch_masks():
    g = jnp.arange(CELLS, dtype=jnp.int32)
    i, j = g // GRID, g % GRID
    cols = []
    for n in range(9):
        a, b = i + n // 3 - 1, j + n % 3 - 1
        cols.append((g < GRID * GRID) & (a >= 0) & (a < GRID) & (b >= 0) & (b < GRID))
    return jnp.pad(jnp.stack(cols, 1).astype(F32), ((0, 0), (0, 128 - 9)))


def text_taps(conv_text):
    rows = []
    for d in TAPS:
        if d == 0:
            rows.append(conv_text[0, 1] + conv_text[1, 1] + conv_text[2, 1])
        else:
            rows.append(conv_text[abs(d) - 1, 2 if d > 0 else 0])
    rows.append(jnp.zeros_like(rows[0]))
    return jnp.stack(rows)


def xor_pairs(n, bit):
    return [(i, i ^ bit) for i in range(n)]


def swap(value, axis, bit):
    return lax.ppermute(value, axis, xor_pairs(lax.axis_size(axis), bit))


def spread(blocks, after=None):
    n = lax.axis_size("seq")
    out = [blocks[0]]
    for d in range(1, n):
        out.append(lax.ppermute(blocks[d], "seq", [(i, (i + d) % n) for i in range(n)]))
    return out


def rotated(pages):
    n = lax.axis_size("seq")
    place = lax.axis_index("seq")
    return [lax.dynamic_index_in_dim(pages, lax.rem(place + d, n), 0, keepdims=False) for d in range(n)]


def total(terms):
    out = terms[0].astype(F32)
    for t in terms[1:]:
        out = out + t.astype(F32)
    return out.astype(BF)


class Reduction:
    def __init__(self, keep, send, line=False):
        self.line = line and lax.axis_size("seq") == 4
        n = lax.axis_size("pages")
        self.n = n
        self.page = lax.axis_index("pages")
        self.first = (self.page & 1) == 0
        self.bits = [1 << b for b in range(1, n.bit_length() - 1)]
        self.shape = (n // 2, keep.shape[0] * 2 // n, keep.shape[1])
        self.terms = [keep.reshape(self.shape)]
        self.send, self.at, self.name = send, 0, None

    def blocks(self, depth, other):
        up, down = self.bits[:depth], self.bits[::-1][:depth]
        out = []
        for k in range((self.n // 2) >> depth):
            pair = []
            for closed in (up, down):
                free = [b for b in self.bits if b not in closed]
                index = sum((((k >> i) & 1) * b) for i, b in enumerate(free))
                mine = sum(closed)
                flip = closed[-1] if other and closed else 0
                pair.append((index + ((self.page ^ flip) & mine)) // 2)
            out.append(jnp.where(self.first, *pair))
        return out

    def pick(self, depth, other):
        rows = []
        for k, block in enumerate(self.blocks(depth, other)):
            parts = []
            for t, term in enumerate(self.terms):
                have = max(t - 1, 0)
                if have == 0:
                    place = block
                else:
                    known = self.blocks(have, False)
                    place = sum(jnp.where(known[i] == block, i, 0) for i in range(len(known)))
                parts.append(lax.dynamic_index_in_dim(term, place, 0, keepdims=False))
            rows.append(total(parts))
        return jnp.stack(rows) if len(rows) > 1 else rows[0][None]

    def step(self):
        assert not self.over()
        at, last = self.at, len(self.bits)
        self.at += 1
        n = lax.axis_size("seq")
        ring = lambda d: [(i, (i + d) % n) for i in range(n)]
        place = lax.axis_index("seq")
        if at == 0:
            self.fresh = [swap(self.send, "pages", 1)]
        elif at <= last:
            self.terms.append(self.fresh[0].reshape((-1,) + self.shape[1:]))
            pairs = [(i, i ^ (self.bits[-at] if i & 1 else self.bits[at - 1])) for i in range(self.n)]
            self.fresh = [lax.ppermute(self.pick(at, True), "pages", pairs)]
        elif at == last + 1:
            self.terms.append(self.fresh[0].reshape((-1,) + self.shape[1:]))
            value = self.pick(last, False)[0]
            rows, cols = value.shape
            if self.line:
                self.own = value
                self.fresh = [lax.ppermute(value, "seq", [(0, 1), (3, 2)])]
                return
            quarters = value.reshape(n, rows // n, cols)
            piece = lambda d: lax.dynamic_index_in_dim(quarters, lax.rem(place + d, n), 0, keepdims=False)
            self.own = piece(0)
            self.fresh = [lax.ppermute(piece(d), "seq", ring(d)) for d in range(1, n)]
        else:
            self.own = total([self.own] + self.fresh)
            if self.line:
                self.fresh = [lax.ppermute(self.own, "seq", [(1, 2), (2, 1)] if at == last + 2 else [(1, 0), (2, 3)])]
                return
            self.fresh = [lax.ppermute(self.own, "seq", ring(d)) for d in range(1, n)]

    def over(self):
        return self.at == len(self.bits) + (4 if self.line else 3)

    def result(self, info, layout=None):
        if self.line:
            place = lax.axis_index("seq")
            return [jnp.where((place == 0) | (place == 3), self.fresh[0], self.own).astype(F32)]
        outs = restack(info, [self.own] + self.fresh, F32, layout)
        return [out.reshape(-1, out.shape[-1]) for out in outs]


def tie(value, *reductions):
    value, fresh, held = lax.optimization_barrier(
        (value, tuple(r.fresh for r in reductions), tuple(r.send for r in reductions)))
    for r, f, h in zip(reductions, fresh, held):
        r.fresh, r.send = f, h
    return value


def per_device(
    tokens, cotangent, conv_text, conv_patch, proj_query, bias_query, proj_key, proj_value, bias_value,
    proj_output, bias_output, rel_order, rel_horiz, rel_vert, norm_gain, norm_shift, expand_weight,
    expand_bias, reduce_weight, reduce_bias, final_gain, final_shift, text_count, box_left, box_top,
):
    pages_here, stretch, width = tokens.shape
    n_seq = lax.axis_size("seq")
    n_pages = lax.axis_size("pages")
    assert pages_here == n_seq and n_pages & (n_pages - 1) == 0
    place = lax.axis_index("seq")
    heads, nb = rel_order.shape
    ff = expand_weight.shape[1]
    pick = lambda a: lax.dynamic_index_in_dim(a, place, 0, keepdims=False)
    count, left, top = pick(text_count), pick(box_left), pick(box_top)
    blocks = spread(rotated(tokens))
    core = lax.axis_index("pages") & 1
    info = jnp.stack([place, count, core]).astype(jnp.int32)
    turn = turn_matrix(width, n_pages, core) if width // n_pages % 16 else jnp.zeros((8, 128), BF)
    cells = jnp.arange(BOX, dtype=jnp.int32)
    oh = jnp.concatenate([left[:, None] == cells[None], top[:, None] == cells[None]], 1).astype(BF)
    oht = jnp.concatenate([left[None] == cells[::-1, None], top[None] == cells[::-1, None]], 0).astype(BF)
    wt, od, edge = tables(rel_order, rel_horiz, rel_vert)
    pm, ct = patch_masks(), text_taps(conv_text)
    cp = jnp.pad(conv_patch.reshape(9, width), ((0, 7), (0, 0)))

    cot_out, blocks = lax.optimization_barrier((rotated(cotangent), blocks))
    cots = spread(cot_out)
    settled, et, q, k, v, probs, att = front(
        info, edge, blocks, ct, cp, pm, turn, proj_query, bias_query, proj_key, proj_value, bias_value, oh, wt, od, width // n_pages)
    *mixed, xh, rs, fl, gp, ds, dr, grk, grs, sm = middle(
        info, cots, att, settled, proj_output, bias_output, norm_gain, norm_shift, expand_weight,
        expand_bias, reduce_weight, reduce_bias, final_gain, final_shift, turn, ff // n_pages)
    c_reduce = Reduction(grk, grs)
    c_reduce.step()
    mixed = spread(mixed)
    done = back(info, width // n_pages, 0, 2, dr, ds, reduce_weight, gp, expand_weight, fl, turn)
    done = tie(done, c_reduce)
    c_reduce.step()
    done = back(info, width // n_pages, 2, ff // width - 2, dr, done[3], reduce_weight, gp, expand_weight, fl, turn, done[:3],
                (xh, rs, norm_gain, att, proj_output))
    done, mixed = tie((done, mixed), c_reduce)
    gek, ges, be, df, da, sm2 = done
    c_expand = Reduction(gek, ges)
    heads_of = lambda first, count, da, acc, filled=(): heads_back(
        first, count, probs, q, k, v, da, att, oh, oht, et, proj_query, proj_key, proj_value, acc, filled)
    cuts = (0, heads // 2, heads)
    c_reduce.step()
    c_expand.step()
    done = heads_of(0, cuts[1], da, df)
    done, da = tie((done, da), c_reduce, c_expand)
    for first, last in zip(cuts[1:-1], cuts[2:]):
        c_reduce.step()
        c_expand.step()
        done = heads_of(first, last - first, da, done[4], done[:4])
        done, da = tie((done, da), c_reduce, c_expand)
    gqk, gqs, qb, diag, acc = done
    c_qkv = Reduction(gqk, gqs)
    for r in (c_reduce, c_expand, c_qkv):
        if not r.over():
            r.step()
    *gts, small = encode_back(info, blocks, acc, ct, cp, pm, sm, sm2, be, qb)
    rounds = [("pages", 1 << b) for b in range(n_pages.bit_length() - 1)] + [("seq", 1 << b) for b in range(n_seq.bit_length() - 1)]
    hop = lambda d: lax.ppermute(gts[d], "seq", [(i, (i + d) % n_seq) for i in range(n_seq)])
    work = [c_reduce, c_expand, c_qkv]
    for r, name in zip(work, ("reduce", "expand", "qkv")):
        r.name = name
    bias = jnp.concatenate(bias_grads(diag, nb), 1)
    bias = jnp.pad(bias, ((0, 0), (0, 128 - 3 * nb))).reshape(-1, width)
    hops = {0: (2,), 1: (1,), 2: (3,)}
    turns = [rounds[1:3], rounds[:1] + rounds[3:4], rounds[4:]] if len(rounds) == 5 else [rounds]
    layouts = {
        "reduce": None,
        "expand": [[(0, ff)], [(ff, width)]],
        "qkv": [[(384 * p + 128 * n, 128) for p in range(heads // 2)] for n in range(3)],
    }
    ready = {}
    phase = 0
    while turns or not c_qkv.over():
        gts, small, bias, ready = tie((gts, small, bias, ready), *work)
        if phase == 0:
            small = lax.dynamic_update_slice(small, bias, (24 + ff // width, 0))
            ready["mixed"] = restack(info, mixed, BF)
        for r in work:
            if not r.over():
                r.step()
            elif r.own is not None and r is not c_qkv:
                ready[r.name] = r.result(info, layouts[r.name])
                r.own, r.fresh = None, []
        for d in hops.get(phase, ()):
            gts = [hop(d) if e == d else part for e, part in enumerate(gts)]
        for axis, bit in turns.pop(0) if turns else ():
            small = small + swap(small, axis, bit)
        phase += 1
    (mixed_out,) = ready["mixed"]
    (o_reduce,), (o_expand, o_output) = (
        ready[r.name] if r.name in ready else r.result(info, layouts[r.name]) for r in (c_reduce, c_expand))
    (grad_tokens,) = restack(info, gts, F32)
    smalls = unpack(small, heads, nb, ff)
    (grad_tokens, smalls, o_reduce, o_expand, o_output), c_qkv.fresh = lax.optimization_barrier(
        ((grad_tokens, smalls, o_reduce, o_expand, o_output), c_qkv.fresh))
    o_query, o_key, o_value = c_qkv.result(info, layouts["qkv"])

    (g_conv_text, g_conv_patch, g_qb, g_vb, g_ob, g_order, g_horiz, g_vert, g_ng, g_ns, g_be, g_rb, g_fg, g_fs) = smalls
    return (
        mixed_out, grad_tokens, g_conv_text, g_conv_patch, o_query, g_qb, o_key, o_value, g_vb,
        o_output, g_ob, g_order, g_horiz, g_vert, g_ng, g_ns, o_expand, g_be, o_reduce, g_rb, g_fg, g_fs,
    )


def solution(mesh):
    placed = (
        P("pages", "seq", None),
        P("pages", "seq", None),
        P(),
        P(),
        P(),
        P(),
        P(),
        P(),
        P(),
        P(),
        P(),
        P(),
        P(),
        P(),
        P(),
        P(),
        P(),
        P(),
        P(),
        P(),
        P(),
        P(),
        P("pages"),
        P("pages", None),
        P("pages", None),
    )
    return jax.shard_map(
        per_device,
        mesh=mesh,
        in_specs=placed,
        out_specs=(
            P("pages", "seq", None),
            P("pages", "seq", None),
            P(),
            P(),
            P("pages", None),
            P(),
            P("pages", None),
            P("pages", None),
            P(),
            P("pages", None),
            P(),
            P(),
            P(),
            P(),
            P(),
            P(),
            P("pages", None),
            P(),
            P("pages", None),
            P(),
            P(),
            P(),
        ),
        check_vma=False,
    )
```

```python
import functools
import jax
import jax.numpy as jnp
from jax import lax
from jax.experimental import pallas as pl
from jax.experimental.pallas import tpu as pltpu
from jax.sharding import PartitionSpec as P

BF = jnp.bfloat16
F32 = jnp.float32
TEXT = 512
GRID = 7
SPAN = 16
EPS = 1e-06
SCALE = 0.125
NEG = -1e30
BOX = 64
RT = 64
LR = 32
EDGE = 16
CELLS = 56
OFFSETS = (-128, -64, 0, 64)
TAPS = (-3, -2, -1, 0, 1, 2, 3)
ERF_P = 0.33
ERF_Q = (0.18635791540145874, 0.1829543262720108, 0.20123349130153656, 0.047190189361572266,
         0.4085558354854584, -0.35120898485183716, 0.4602709114551544, -0.1353536993265152)


def dot(a, b):
    return jnp.dot(a, b, preferred_element_type=F32)


def dot_t(a, b):
    return lax.dot_general(a, b, (((1,), (1,)), ((), ())), preferred_element_type=F32)


def t_dot(a, b):
    return lax.dot_general(a, b, (((0,), (0,)), ((), ())), preferred_element_type=F32)


def whole(shape, buffers=1):
    return pl.BlockSpec(shape, lambda *_: (0,) * len(shape), pipeline_mode=pl.Buffered(buffers))


def whole_out(shape):
    return pl.BlockSpec(shape, lambda *_: (0,) * len(shape))


def lanes(n):
    return [slice(128 * c, 128 * (c + 1)) for c in range(n // 128)]


def line(ref, part=slice(None)):
    return ref[part].reshape(1, -1)


def row_sum(x):
    return jnp.sum(x, axis=0, keepdims=True)


def fold(x):
    out = x[:8]
    for r in range(8, x.shape[0], 8):
        out = out + x[r : r + 8]
    return out


def shift_rows(window, offset, rows):
    if offset == 0:
        return window[8 : 8 + rows]
    return pltpu.roll(window, (-offset) % window.shape[0], 0)[8 : 8 + rows]


def gather_page(dest, row0, place, n_seq, own, others):
    stretch = own.shape[0]
    for d, block in enumerate((own,) + tuple(others)):
        source = lax.rem(place - d + n_seq, n_seq)
        dest[pl.ds(pl.multiple_of(row0 + source * stretch, 16), stretch), :] = block[...].astype(dest.dtype)


def turned_transpose(x_ref, turn_ref, core, block, dest, raw):
    rows = dest.shape[0]
    if block % 16:
        dest[...] = dot_t(turn_ref[...], x_ref[...]).astype(BF)
        return
    raw[...] = jnp.transpose(x_ref[...])
    half = rows // 2
    for k in range(half // block):
        for side in range(2):
            parity = core if side == 0 else 1 - core
            source = pl.multiple_of((2 * k + parity) * block, 16)
            dest[side * half + k * block : side * half + (k + 1) * block, :] = raw[pl.ds(source, block), :]


def moves(pairs, sems):
    return [pltpu.make_async_copy(source, dest, sems.at[n]) for n, (source, dest) in enumerate(pairs)]


def start(copies):
    for c in copies:
        c.start()


def wait(copies):
    for c in copies:
        c.wait()


def front_kernel(info_ref, edge_ref, *refs, n_seq, block):
    blocks = refs[:n_seq]
    (ct_ref, cp_ref, pm_ref, turn_ref, wq_any, bq_ref, wk_any, wv_any, bv_ref, oh_ref, wt_ref, ord_ref,
     set_any, et_any, q_any, k_any, v_any, p_ref, o_ref,
     entry_ref, xs_ref, ms_ref, ka_ref, qa_ref, s_ref, raw_ref,
     set_ref, et_ref, q_ref, k_ref, v_ref, wq_ref, wk_ref, wv_ref, in_sems, out_sems) = refs[n_seq:]
    g = pl.program_id(0)
    arriving = moves([(wq_any, wq_ref), (wk_any, wk_ref), (wv_any, wv_ref)], in_sems)
    leaving = moves([(set_ref, set_any), (et_ref, et_any), (q_ref, q_any), (k_ref, k_any), (v_ref, v_any)], out_sems)
    length, width = entry_ref.shape
    place, count = info_ref[0], info_ref[1]

    @pl.when(g == 0)
    def _():
        start(arriving)
        zero = jnp.zeros((EDGE, width), F32)
        xs_ref[0:EDGE, :] = zero
        xs_ref[EDGE + length :, :] = zero
        ms_ref[0:EDGE, :] = zero
        ms_ref[EDGE + length :, :] = zero
        gather_page(xs_ref, EDGE, place, n_seq, blocks[0], blocks[1:])

        def mask_chunk(i, carry):
            r0 = pl.multiple_of(i * RT, RT)
            keep = (r0 + lax.broadcasted_iota(jnp.int32, (RT, 128), 0)) < count
            for c in lanes(width):
                ms_ref[pl.ds(r0 + EDGE, RT), c] = jnp.where(keep, xs_ref[pl.ds(r0 + EDGE, RT), c], 0.0)
            return carry

        lax.fori_loop(0, length // RT, mask_chunk, 0)

        def conv_chunk(i, carry):
            r0 = pl.multiple_of(i * RT, RT)
            keep = (r0 + lax.broadcasted_iota(jnp.int32, (RT, 128), 0)) < count
            for c in lanes(width):
                window = ms_ref[pl.ds(r0 + EDGE - 8, RT + 16), c]
                term = None
                for n, d in enumerate(TAPS):
                    part = shift_rows(window, d, RT) * ct_ref[n : n + 1, c]
                    term = part if term is None else term + part
                set_ref[pl.ds(r0, RT), c] = xs_ref[pl.ds(r0 + EDGE, RT), c] + jnp.where(keep, term, 0.0)
            return carry

        lax.fori_loop(0, length // RT, conv_chunk, 0)
        for c in lanes(width):
            window = xs_ref[EDGE + TEXT - 8 : EDGE + TEXT + CELLS + 8, c]
            term = jnp.zeros((CELLS, 128), F32)
            for n in range(9):
                off = (n // 3 - 1) * GRID + n % 3 - 1
                term = term + shift_rows(window, off, CELLS) * (cp_ref[n : n + 1, c] * pm_ref[:, n : n + 1])
            set_ref[TEXT : TEXT + CELLS, c] = set_ref[TEXT : TEXT + CELLS, c] + term
        entry_ref[...] = set_ref[...].astype(BF)
        turned_transpose(entry_ref, turn_ref, info_ref[2], block, et_ref, raw_ref)
        wait(arriving)
        for c in range(width // 256):
            s = slice(256 * c, 256 * (c + 1))
            q_ref[:, s] = (dot(entry_ref[...], wq_ref[:, s]) + line(bq_ref, s)).astype(BF) * jnp.asarray(SCALE, BF)
            k_ref[:, s] = dot(entry_ref[...], wk_ref[:, s]).astype(BF)
            v_ref[:, s] = (dot(entry_ref[...], wv_ref[:, s]) + line(bv_ref, s)).astype(BF)
        ka_ref[:, 128:256] = oh_ref[...]
        ka_ref[:, 256:384] = oh_ref[...]
        start(leaving)

    @pl.when(g == pl.num_programs(0) - 1)
    def _():
        wait(leaving)

    pair = pl.ds(pl.multiple_of(g * 128, 128), 128)
    ka_ref[:, 0:128] = k_ref[:, pair]
    lane = lax.broadcasted_iota(jnp.int32, (length, 128), 1)
    for e in range(2):
        mine = (lane < 64) if e == 0 else (lane >= 64)
        qa_ref[e, :, 0:128] = jnp.where(mine, q_ref[:, pair], jnp.zeros((), BF))
        qa_ref[e, :, 128:384] = dot(oh_ref[...], wt_ref[e]).astype(BF)
        s_ref[e] = dot_t(qa_ref[e], ka_ref[...])
    cols = (length + 127) // 128
    at = lax.broadcasted_iota(jnp.int32, (1, length), 1)
    ok = (at < count) | ((at >= TEXT) & (at < TEXT + GRID * GRID))
    bar = jnp.where(ok, 0.0, NEG)
    outs = []
    for e in range(2):
        left, right = edge_ref[2 * g + e, 0], edge_ref[2 * g + e, 1]
        for a in range(length // RT):
            r0 = a * RT
            parts = []
            for b in range(cols):
                w = min(128, length - 128 * b)
                d = 128 * b - r0
                t = s_ref[e, r0 : r0 + RT, 128 * b : 128 * b + w]
                m = bar[:, 128 * b : 128 * b + w]
                if d in OFFSETS:
                    t = t + ord_ref[e, OFFSETS.index(d)][:, :w] + m
                else:
                    t = t + (m + (left if d < 0 else right))
                parts.append(t)
            t = jnp.concatenate(parts, 1)
            top = jnp.max(t, axis=1, keepdims=True)
            ex = jnp.exp(t - top)
            total = jnp.sum(ex, axis=1, keepdims=True)
            p_ref[e, r0 : r0 + RT, :] = (ex * (1.0 / total)).astype(BF)
        outs.append(dot(p_ref[e], v_ref[:, pair]))
    o_ref[...] = jnp.where(lane < 64, outs[0], outs[1]).astype(BF)


def front(info, edge, blocks, ct, cp, pm, turn, wq, bq, wk, wv, bv, oh, wt, od, block):
    n_seq = len(blocks)
    stretch, width = blocks[0].shape
    length = n_seq * stretch
    heads = wt.shape[0]
    sds = jax.ShapeDtypeStruct
    flops = 2 * length * width * width * 3 + heads * 2 * length * length * (384 + 128)
    return pl.pallas_call(
        functools.partial(front_kernel, n_seq=n_seq, block=block),
        out_shape=(sds((length, width), F32), sds((width, length), BF)) + (sds((length, width), BF),) * 3
        + (sds((heads, length, length), BF), sds((length, width), BF)),
        grid_spec=pltpu.PrefetchScalarGridSpec(
            num_scalar_prefetch=2, grid=(heads // 2,),
            in_specs=[whole((stretch, width))] * n_seq
            + [whole(ct.shape), whole(cp.shape), whole(pm.shape), whole(turn.shape), pl.BlockSpec(memory_space=pl.ANY), whole(bq.shape), pl.BlockSpec(memory_space=pl.ANY),
               pl.BlockSpec(memory_space=pl.ANY), whole(bv.shape), whole(oh.shape),
               pl.BlockSpec((2, 128, 256), lambda g, *_: (g, 0, 0)),
               pl.BlockSpec((2, len(OFFSETS), RT, 128), lambda g, *_: (g, 0, 0, 0))],
            out_specs=[pl.BlockSpec(memory_space=pl.ANY)] * 5
            + [pl.BlockSpec((2, length, length), lambda g, *_: (g, 0, 0)), pl.BlockSpec((length, 128), lambda g, *_: (0, g))],
            scratch_shapes=[pltpu.VMEM((length, width), BF), pltpu.VMEM((length + 2 * EDGE, width), F32), pltpu.VMEM((length + 2 * EDGE, width), F32),
                            pltpu.VMEM((length, 384), BF), pltpu.VMEM((2, length, 384), BF), pltpu.VMEM((2, length, length), F32), pltpu.VMEM((width, length), BF),
                            pltpu.VMEM((length, width), F32), pltpu.VMEM((width, length), BF)]
            + [pltpu.VMEM((length, width), BF)] * 3 + [pltpu.VMEM((width, width), BF)] * 3
            + [pltpu.SemaphoreType.DMA((3,)), pltpu.SemaphoreType.DMA((5,))],
        ),
        cost_estimate=pl.CostEstimate(flops=25_000_000_000, bytes_accessed=8 << 20, transcendentals=0),
        name="front",
    )(info, edge, *blocks, ct, cp, pm, turn, wq, bq, wk, wv, bv, oh, wt, od)


def norm_stats(u):
    mean = jnp.mean(u, axis=1, keepdims=True)
    c = u - mean
    rs = lax.rsqrt(jnp.mean(c * c, axis=1, keepdims=True) + EPS)
    return c * rs, rs


def norm_back(u, xhat, rs):
    return rs * (u - jnp.mean(u, axis=1, keepdims=True) - xhat * jnp.mean(u * xhat, axis=1, keepdims=True))


def gelu_pair(x):
    t = 1.0 / (1.0 + jnp.abs(x) * (ERF_P * 0.7071067811865476))
    bell = jnp.exp2(x * x * -0.7213475204444817)
    q = jnp.full_like(t, 0.5 * ERF_Q[7])
    for k in range(6, -1, -1):
        q = q * t + 0.5 * ERF_Q[k]
    tail = q * t * bell
    cdf = jnp.where(x < 0, tail, 1.0 - tail)
    return x * cdf, cdf + x * bell * 0.3989422804014327


def middle_kernel(info_ref, *refs, n_seq, tiles, tile, block):
    cots = refs[:n_seq]
    (att_ref, set_ref, wo_ref, bo_ref, ng_ref, ns_ref, w1_ref, b1_ref, w2_ref, b2_ref, fg_ref, fs_ref, turn_ref) = refs[n_seq : n_seq + 13]
    outs = refs[n_seq + 13 :]
    mixed = outs[:n_seq]
    (xh_any, rs_any, fl_any, gp_ref, ds_any, dr_any, gk_ref, gs_ref, sm_ref, act_ref, fn_ref, acc_ref, cot_ref, mix_ref, e_ref, g_ref, b1_rows,
     xh_ref, rs_ref, fl_ref, ds_ref, dr_ref, cot_sems, norm_sems, out_sems) = outs[n_seq:]
    i = pl.program_id(0)
    length, width = fl_ref.shape
    place = info_ref[0]
    stretch = length // n_seq
    block_of = lambda ref, d: ref.at[pl.ds(pl.multiple_of(lax.rem(place + d, n_seq) * stretch, 16), stretch), :]
    arriving = moves([(cots[d], block_of(cot_ref, n_seq - d)) for d in range(n_seq)], cot_sems)
    normed = moves([(xh_ref, xh_any), (rs_ref, rs_any), (fl_ref, fl_any)], norm_sems)
    leaving = moves([(ds_ref, ds_any), (dr_ref, dr_any)] + [(block_of(mix_ref, d), mixed[d]) for d in range(n_seq)], out_sems)

    @pl.when(i == 0)
    def _():
        start(arriving)
        for c in range(width // 256):
            s = slice(256 * c, 256 * (c + 1))
            acc_ref[:, s] = dot(att_ref[...], wo_ref[:, s])

        def chunk(j, carry):
            r = pl.ds(pl.multiple_of(j * LR, LR), LR)
            u = set_ref[r, :] + (acc_ref[r, :] + line(bo_ref))
            xhat, rs = norm_stats(u)
            xh_ref[r, :] = xhat
            rs_ref[r, :] = jnp.broadcast_to(rs, (LR, 128))
            fn = xhat * line(ng_ref) + line(ns_ref)
            fn_ref[r, :] = fn
            fl_ref[r, :] = fn.astype(BF)
            acc_ref[r, :] = jnp.broadcast_to(line(b2_ref), (LR, width))
            return carry

        lax.fori_loop(0, length // LR, chunk, 0, unroll=6)
        start(normed)
        for t in range(tiles):
            b1_rows[t] = line(b1_ref, slice(t * tile, (t + 1) * tile))

    @pl.when(i < tiles)
    def _():
        half = tile // 3
        for n in range(3):
            e_ref[n] = dot(fl_ref[...], w1_ref[:, n * half : (n + 1) * half])
        for n in range(3):
            s = slice(n * half, (n + 1) * half)
            act, gp = gelu_pair(e_ref[n] + b1_rows[i, :, s])
            act_ref[i, :, s] = act.astype(BF)
            gp_ref[:, s] = gp.astype(gp_ref.dtype)
        for c in range(width // 256):
            s = slice(256 * c, 256 * (c + 1))
            acc_ref[:, s] += dot(act_ref[i], w2_ref[:, s])

    @pl.when(i == tiles - 1)
    def _():
        wait(arriving)

        def chunk(j, sums):
            r0 = pl.multiple_of(j * LR, LR)
            r = pl.ds(r0, LR)
            second = fn_ref[r, :] + acc_ref[r, :]
            xhat, rs = norm_stats(second)
            mix_ref[r, :] = (xhat * line(fg_ref) + line(fs_ref)).astype(BF)
            cot = cot_ref[r, :].astype(F32)
            back = norm_back(cot * line(fg_ref), xhat, rs)
            ds_ref[r, :] = back
            low = back.astype(BF)
            dr_ref[r, :] = low
            return (sums[0] + fold(cot * xhat), sums[1] + fold(cot), sums[2] + fold(low.astype(F32)))

        sums = lax.fori_loop(0, length // LR, chunk, (jnp.zeros((8, width), F32),) * 3, unroll=6)
        for n in range(3):
            sm_ref[n : n + 1, :] = row_sum(sums[n])
        start(leaving)

    @pl.when(i == pl.num_programs(0) - 1)
    def _():
        wait(normed)
        wait(leaving)

    @pl.when(i >= tiles)
    def _():
        grad = t_dot(act_ref[i - tiles], dr_ref[...]).astype(BF)
        if 2 * block == tile:
            g_ref[...] = grad
            core = info_ref[2]
            gk_ref[...] = g_ref[pl.ds(pl.multiple_of(core * block, block), block), :]
            gs_ref[...] = g_ref[pl.ds(pl.multiple_of((1 - core) * block, block), block), :]
        else:
            turned = dot(turn_ref[...], grad).astype(BF)
            gk_ref[...] = turned[: tile // 2]
            gs_ref[...] = turned[tile // 2 :]


def middle(info, cots, att, settled, wo, bo, ng, ns, w1, b1, w2, b2, fg, fs, turn, block):
    tile = w1.shape[0]
    n_seq = len(cots)
    stretch, width = cots[0].shape
    length = n_seq * stretch
    ff = w1.shape[1]
    tiles = ff // tile
    sds = jax.ShapeDtypeStruct
    early = lambda i: jnp.minimum(i, tiles - 1)
    late = lambda i: jnp.maximum(i - tiles, 0)
    return pl.pallas_call(
        functools.partial(middle_kernel, n_seq=n_seq, tiles=tiles, tile=tile, block=block),
        out_shape=(sds((stretch, width), BF),) * n_seq
        + (sds((length, width), F32), sds((length, 128), F32), sds((length, width), BF), sds((length, ff), BF),
           sds((length, width), F32), sds((length, width), BF), sds((ff // 2, width), BF), sds((ff // 2, width), BF), sds((8, width), F32)),
        grid_spec=pltpu.PrefetchScalarGridSpec(
            num_scalar_prefetch=1, grid=(2 * tiles,),
            in_specs=[pl.BlockSpec(memory_space=pl.ANY)] * n_seq
            + [whole(att.shape), whole(settled.shape), whole(wo.shape), whole(bo.shape), whole(ng.shape), whole(ns.shape),
               pl.BlockSpec((width, tile), lambda i, *_: (0, early(i))), whole(b1.shape),
               pl.BlockSpec((tile, width), lambda i, *_: (early(i), 0)), whole(b2.shape), whole(fg.shape), whole(fs.shape), whole(turn.shape)],
            out_specs=[pl.BlockSpec(memory_space=pl.ANY)] * (n_seq + 3)
            + [pl.BlockSpec((length, tile), lambda i, *_: (0, early(i))), pl.BlockSpec(memory_space=pl.ANY), pl.BlockSpec(memory_space=pl.ANY),
               pl.BlockSpec((tile // 2, width), lambda i, *_: (late(i), 0)), pl.BlockSpec((tile // 2, width), lambda i, *_: (late(i), 0)),
               whole_out((8, width))],
            scratch_shapes=[pltpu.VMEM((tiles, length, tile), BF), pltpu.VMEM((length, width), F32), pltpu.VMEM((length, width), F32),
                            pltpu.VMEM((length, width), BF), pltpu.VMEM((length, width), BF), pltpu.VMEM((3, length, tile // 3), F32),
                            pltpu.VMEM((tile, width), BF), pltpu.VMEM((tiles, 1, tile), F32),
                            pltpu.VMEM((length, width), F32), pltpu.VMEM((length, 128), F32), pltpu.VMEM((length, width), BF),
                            pltpu.VMEM((length, width), F32), pltpu.VMEM((length, width), BF),
                            pltpu.SemaphoreType.DMA((n_seq,)), pltpu.SemaphoreType.DMA((3,)), pltpu.SemaphoreType.DMA((2 + n_seq,))],
        ),
        cost_estimate=pl.CostEstimate(flops=35_000_000_000, bytes_accessed=8 << 20, transcendentals=0),
        name="middle",
    )(info, *cots, att, settled, wo, bo, ng, ns, w1, b1, w2, b2, fg, fs, turn)


def back_kernel(info_ref, *refs, tiles, last, block):
    core = info_ref[2]
    if last:
        (dr_ref, in_ref, w2_ref, gp_ref, w1_ref, fl_ref, turn_ref, xh_any, rs_any, ng_ref, att_any, wo_any) = refs[:12]
        (gk_ref, gs_ref, be_ref, df_ref, da_ref, sm_ref, flt_ref, raw_ref, acc_ref, db_ref,
         xh_ref, rs_ref, att_ref, wo_ref, sems) = refs[-15:]
        arriving = moves([(xh_any, xh_ref), (rs_any, rs_ref), (att_any, att_ref), (wo_any, wo_ref)], sems)
    else:
        (dr_ref, in_ref, w2_ref, gp_ref, w1_ref, fl_ref, turn_ref) = refs[:7]
        (gk_ref, gs_ref, be_ref, acc_ref, flt_ref, raw_ref) = refs[-6:]
    i = pl.program_id(0)
    length, width = dr_ref.shape

    @pl.when(i == 0)
    def _():
        if last:
            start(arriving)
        turned_transpose(fl_ref, turn_ref, core, block, flt_ref, raw_ref)
        acc_ref[...] = in_ref[...]

    @pl.when(i < tiles)
    def _():
        de = dot_t(dr_ref[...], w2_ref[...]) * gp_ref[...].astype(F32)
        de = de.astype(BF)
        be_ref[...] = row_sum(de.astype(F32))
        grad = dot(flt_ref[...], de).astype(BF)
        gk_ref[...] = grad[: width // 2]
        gs_ref[...] = grad[width // 2 :]
        acc_ref[...] += dot_t(de, w1_ref[...])

    if not last:
        return

    @pl.when(i == tiles)
    def _():
        wait(arriving)

        def chunk(j, sums):
            r = pl.ds(pl.multiple_of(j * LR, LR), LR)
            first = acc_ref[r, :]
            xhat = xh_ref[r, :]
            back = norm_back(first * line(ng_ref), xhat, rs_ref[r, 0:1])
            df_ref[r, :] = back
            low = back.astype(BF)
            db_ref[r, :] = low
            return (sums[0] + fold(first * xhat), sums[1] + fold(first), sums[2] + fold(low.astype(F32)))

        sums = lax.fori_loop(0, length // LR, chunk, (jnp.zeros((8, width), F32),) * 3, unroll=6)
        for n in range(3):
            sm_ref[n : n + 1, :] = row_sum(sums[n])
        da_ref[...] = dot_t(db_ref[...], wo_ref[...]).astype(BF)
        turned_transpose(att_ref, turn_ref, core, block, flt_ref, raw_ref)
        grad = dot(flt_ref[...], db_ref[...]).astype(BF)
        gk_ref[...] = grad[: width // 2]
        gs_ref[...] = grad[width // 2 :]


def back(info, block, first, tiles, dr, acc, w2, gp, w1, fl, turn, filled=(), norm=None):
    length, width = dr.shape
    ff = w1.shape[1]
    last = norm is not None
    sds = jax.ShapeDtypeStruct
    at = lambda i: jnp.minimum(i, tiles - 1) + first
    grad = pl.BlockSpec((width // 2, width), lambda i, *_: (0, i + first))
    args = [dr, acc, w2, gp, w1, fl, turn] + list(norm or ())
    out_shape = [sds((width // 2, ff + width), BF), sds((width // 2, ff + width), BF), sds((1, ff), F32), sds((length, width), F32)]
    out_specs = [grad, grad, pl.BlockSpec((1, width), lambda i, *_: (0, at(i))), whole_out((length, width))]
    scratch = [pltpu.VMEM((width, length), BF), pltpu.VMEM((width, length), BF)]
    if last:
        out_shape += [sds((length, width), BF), sds((8, width), F32)]
        out_specs += [whole_out((length, width)), whole_out((8, width))]
        scratch += [pltpu.VMEM((length, width), F32), pltpu.VMEM((length, width), BF), pltpu.VMEM((length, width), F32),
                    pltpu.VMEM((length, 128), F32), pltpu.VMEM((length, width), BF), pltpu.VMEM((width, width), BF),
                    pltpu.SemaphoreType.DMA((4,))]
    return pl.pallas_call(
        functools.partial(back_kernel, tiles=tiles, last=last, block=block),
        out_shape=tuple(out_shape),
        grid_spec=pltpu.PrefetchScalarGridSpec(
            num_scalar_prefetch=1, grid=(tiles + last,),
            in_specs=[whole(dr.shape), whole(acc.shape), pl.BlockSpec((width, width), lambda i, *_: (at(i), 0)),
                      pl.BlockSpec((length, width), lambda i, *_: (0, at(i))), pl.BlockSpec((width, width), lambda i, *_: (0, at(i)))]
            + [pl.BlockSpec(memory_space=pl.ANY) if n in (7, 8, 10, 11) else whole(x.shape) for n, x in enumerate(args) if n >= 5]
            + [pl.BlockSpec(memory_space=pl.ANY)] * len(filled),
            out_specs=out_specs,
            scratch_shapes=scratch,
        ),
        input_output_aliases={1 + len(args) + n: n for n in range(len(filled))},
        cost_estimate=pl.CostEstimate(flops=12_000_000_000, bytes_accessed=8 << 20, transcendentals=0),
        name="back",
    )(info, *args, *filled)


def diagonals(x):
    wide = jnp.concatenate([x, jnp.zeros_like(x)], 1)
    return row_sum(pltpu.roll(wide, 0, 1, stride=1, stride_axis=0))


def hi_lo(x):
    hi = x.astype(BF)
    return jnp.concatenate([hi, (x - hi.astype(F32)).astype(BF)], 1)


def heads_kernel(*refs):
    (p_ref, q_ref, k_ref, v_ref, do_ref, o_ref, oh_ref, oht_ref, et_any, wq_ref, wk_ref, wv_ref, in_any) = refs[:13]
    (gk_ref, gs_ref, qb_ref, diag_ref, acc_ref, va_ref, rhs_ref, dsc_ref, dp_ref, w_ref, d_ref, et_ref, sems) = refs[-13:]
    arriving = moves([(et_any, et_ref), (in_any, acc_ref)], sems)
    g = pl.program_id(0)
    length = q_ref.shape[0]
    lane = lax.broadcasted_iota(jnp.int32, (length, 128), 1)

    @pl.when(g == 0)
    def _():
        va_ref[:, 128:256] = jnp.where(lane < 2, 1.0, 0.0).astype(BF)
        rhs_ref[:, 128:256] = oh_ref[...]
        start(arriving)

    va_ref[:, 0:128] = v_ref[...]
    rhs_ref[:, 0:128] = k_ref[...]
    cols = (length + 127) // 128
    flip = (lax.broadcasted_iota(jnp.int32, (RT, RT), 0) + lax.broadcasted_iota(jnp.int32, (RT, RT), 1) == RT - 1).astype(F32).astype(BF)
    do = do_ref[...]
    prod = do.astype(F32) * o_ref[...].astype(F32)
    res = []
    for e in range(2):
        mine = (lane < 64) if e == 0 else (lane >= 64)
        inner = -jnp.sum(jnp.where(mine, prod, 0.0), axis=1, keepdims=True)
        hi = inner.astype(BF)
        lo = inner - hi.astype(F32)
        ext = jnp.where(lane == 0, hi.astype(F32), jnp.where(lane == 1, lo, 0.0)).astype(BF)
        da = jnp.concatenate([jnp.where(mine, do, jnp.zeros((), BF)), ext], 1)
        dp_ref[e] = dot_t(da, va_ref[...])
    for e in range(2):
        sums = {}
        for a in range(length // RT):
            r0 = a * RT
            ds = p_ref[e, r0 : r0 + RT, :].astype(F32) * dp_ref[e, r0 : r0 + RT, :]
            dsc_ref[e, r0 : r0 + RT, :] = ds.astype(BF)
            for b in range(cols):
                w = min(128, length - 128 * b)
                d = 128 * b - r0
                t = ds[:, 128 * b : 128 * b + w]
                if w < 128:
                    t = jnp.concatenate([t, jnp.zeros((RT, 128 - w), F32)], 1)
                key = OFFSETS.index(d) if d in OFFSETS else (4 if d < 0 else 5)
                sums[key] = sums[key] + t if key in sums else t
        for n in range(4):
            turned = dot(flip, hi_lo(sums[n]))
            diag_ref[e, n : n + 1, :] = diagonals(turned[:, 0:128] + turned[:, 128:256])
        diag_ref[e, 4:5, 0:128] = row_sum(sums[4])
        diag_ref[e, 4:5, 128:256] = row_sum(sums[5])
        r = dot(dsc_ref[e], rhs_ref[...])
        hh = dot(oht_ref[...], hi_lo(r[:, 128:256]))
        hist = hh[:, 0:128] + hh[:, 128:256]
        half = lane[:BOX] < BOX
        diag_ref[e, 5:6, :] = diagonals(jnp.where(half, hist[:BOX], 0.0))
        diag_ref[e, 6:7, :] = diagonals(jnp.where(half, 0.0, hist[BOX:]))
        diag_ref[e, 7:8, :] = jnp.zeros((1, 256), F32)
        dk = t_dot(dsc_ref[e], q_ref[...])
        dv = t_dot(p_ref[e], do)
        res.append((r[:, 0:128], dk, dv))
    first = lane < 64
    dq = (jnp.where(first, res[0][0], res[1][0]) * SCALE).astype(BF)
    dk = jnp.where(first, res[0][1], res[1][1]).astype(BF)
    dv = jnp.where(first, res[0][2], res[1][2]).astype(BF)

    @pl.when(g == 0)
    def _():
        wait(arriving)

    d_ref[:, 0:128] = dq
    d_ref[:, 128:256] = dk
    d_ref[:, 256:384] = dv
    qb_ref[0:1, :] = row_sum(dq.astype(F32))
    qb_ref[1:2, :] = row_sum(dv.astype(F32))
    w_ref[:, 0:128] = wq_ref[...]
    w_ref[:, 128:256] = wk_ref[...]
    w_ref[:, 256:384] = wv_ref[...]
    grad = dot(et_ref[...], d_ref[...]).astype(BF)
    gk_ref[...] = grad[: grad.shape[0] // 2]
    gs_ref[...] = grad[grad.shape[0] // 2 :]
    acc_ref[...] += dot_t(d_ref[...], w_ref[...])


def heads_back(first, count, probs, q, k, v, do, o, oh, oht, et, wq, wk, wv, acc, filled=()):
    heads = probs.shape[0]
    length, width = q.shape
    steps = count // 2
    base = first // 2
    sds = jax.ShapeDtypeStruct
    col = pl.BlockSpec((length, 128), lambda g: (0, g + base))
    wcol = pl.BlockSpec((width, 128), lambda g: (0, g + base))
    flops = 2 * length * width * 64 * count * 6 + count * 2 * length * length * (256 + 256 + 128 + 128)
    return pl.pallas_call(
        heads_kernel,
        out_shape=(sds((width // 2, 3 * width), BF), sds((width // 2, 3 * width), BF), sds((8, width), F32), sds((heads, 8, 256), F32), sds((length, width), F32)),
        grid=(steps,),
        in_specs=[pl.BlockSpec((2, length, length), lambda g: (g + base, 0, 0)), col, col, col, col, col, whole(oh.shape), whole(oht.shape),
                  pl.BlockSpec(memory_space=pl.ANY), wcol, wcol, wcol] + [pl.BlockSpec(memory_space=pl.ANY)] * (1 + len(filled)),
        out_specs=[pl.BlockSpec((width // 2, 384), lambda g: (0, g + base)), pl.BlockSpec((width // 2, 384), lambda g: (0, g + base)),
                   pl.BlockSpec((8, 128), lambda g: (0, g + base)), pl.BlockSpec((2, 8, 256), lambda g: (g + base, 0, 0)), whole_out((length, width))],
        input_output_aliases={13 + n: n for n in range(len(filled))},
        scratch_shapes=[pltpu.VMEM((length, 256), BF), pltpu.VMEM((length, 256), BF), pltpu.VMEM((2, length, length), BF),
                        pltpu.VMEM((2, length, length), F32), pltpu.VMEM((width, 384), BF), pltpu.VMEM((length, 384), BF),
                        pltpu.VMEM((width, length), BF), pltpu.SemaphoreType.DMA((2,))],
        cost_estimate=pl.CostEstimate(flops=20_000_000_000, bytes_accessed=8 << 20, transcendentals=0),
        name="heads_back",
    )(probs, q, k, v, do, o, oh, oht, et, wq, wk, wv, acc, *filled)


def encode_kernel(info_ref, *refs, n_seq):
    blocks = refs[:n_seq]
    in_ref, ct_ref, cp_ref, pm_ref, sm_ref, sm2_ref, be_ref, qb_ref = refs[n_seq : n_seq + 8]
    outs = refs[n_seq + 8 :]
    grads = outs[:n_seq]
    small_ref, acc_ref, gs_ref, ms_ref, gt_ref = outs[n_seq:]
    length, width = in_ref.shape
    place, count = info_ref[0], info_ref[1]
    acc_ref[...] = in_ref[...]
    small_ref[...] = jnp.zeros_like(small_ref)
    small_ref[0:3, :] = sm_ref[0:3, :]
    small_ref[3:6, :] = sm2_ref[0:3, :]
    small_ref[6:8, :] = qb_ref[0:2, :]
    tiles = be_ref.shape[1] // width
    for t in range(tiles):
        small_ref[8 + t : 9 + t, :] = be_ref[:, t * width : (t + 1) * width]
    taps, cells = 8 + tiles, 15 + tiles
    zero = jnp.zeros((EDGE, width), F32)
    gs_ref[0:EDGE, :] = zero
    gs_ref[EDGE + length :, :] = zero
    ms_ref[0:EDGE, :] = zero
    ms_ref[EDGE + length :, :] = zero
    gather_page(ms_ref, EDGE, place, n_seq, blocks[0], blocks[1:])
    for c in lanes(width):
        tok = ms_ref[EDGE + TEXT - 8 : EDGE + TEXT + CELLS + 8, c]
        own = acc_ref[TEXT : TEXT + CELLS, c]
        window = jnp.concatenate([acc_ref[TEXT - 8 : TEXT + CELLS, c], jnp.zeros((8, 128), F32)], 0)
        term = jnp.zeros((CELLS, 128), F32)
        for n in range(9):
            off = (n // 3 - 1) * GRID + n % 3 - 1
            term = term + shift_rows(window, -off, CELLS) * (cp_ref[n : n + 1, c] * pm_ref[:, 8 - n : 9 - n])
            small_ref[cells + n : cells + n + 1, c] = row_sum(own * shift_rows(tok, off, CELLS) * pm_ref[:, n : n + 1])
        gt_ref[:, c] = term

    def split_chunk(j, carry):
        r0 = pl.multiple_of(j * RT, RT)
        keep = (r0 + lax.broadcasted_iota(jnp.int32, (RT, 128), 0)) < count
        for c in lanes(width):
            dset = acc_ref[pl.ds(r0, RT), c]
            gs_ref[pl.ds(r0 + EDGE, RT), c] = jnp.where(keep, dset, 0.0)
            ms_ref[pl.ds(r0 + EDGE, RT), c] = jnp.where(keep, ms_ref[pl.ds(r0 + EDGE, RT), c], 0.0)
        return carry

    lax.fori_loop(0, length // RT, split_chunk, 0)
    for c in lanes(width):
        acc_ref[TEXT : TEXT + CELLS, c] = acc_ref[TEXT : TEXT + CELLS, c] + gt_ref[:, c]

    def conv_chunk(j, sums):
        r0 = pl.multiple_of(j * RT, RT)
        keep = (r0 + lax.broadcasted_iota(jnp.int32, (RT, 128), 0)) < count
        out = []
        for n, c in enumerate(lanes(width)):
            window = gs_ref[pl.ds(r0 + EDGE - 8, RT + 16), c]
            own = ms_ref[pl.ds(r0 + EDGE, RT), c]
            term = None
            for m, d in enumerate(TAPS):
                moved = shift_rows(window, -d, RT)
                part = moved * ct_ref[m : m + 1, c]
                term = part if term is None else term + part
                out.append(sums[n * len(TAPS) + m] + row_sum(moved * own))
            acc_ref[pl.ds(r0, RT), c] = acc_ref[pl.ds(r0, RT), c] + jnp.where(keep, term, 0.0)
        return tuple(out)

    zeros = (jnp.zeros((1, 128), F32),) * (len(TAPS) * (width // 128))
    sums = lax.fori_loop(0, length // RT, conv_chunk, zeros)
    for n, c in enumerate(lanes(width)):
        for m in range(len(TAPS)):
            small_ref[taps + m : taps + m + 1, c] = sums[n * len(TAPS) + m]
    stretch = length // n_seq
    for d in range(n_seq):
        dest = lax.rem(place + d, n_seq)
        grads[d][...] = acc_ref[pl.ds(pl.multiple_of(dest * stretch, 16), stretch), :].astype(BF)


def encode_back(info, blocks, d_settled, ct, cp, pm, sm, sm2, be, qb):
    n_seq = len(blocks)
    stretch, width = blocks[0].shape
    length = n_seq * stretch
    sds = jax.ShapeDtypeStruct
    rows = 24 + be.shape[1] // width
    rows += 8 - rows % 8
    return pl.pallas_call(
        functools.partial(encode_kernel, n_seq=n_seq),
        out_shape=(sds((stretch, width), BF),) * n_seq + (sds((rows, width), F32),),
        grid_spec=pltpu.PrefetchScalarGridSpec(
            num_scalar_prefetch=1, grid=(1,),
            in_specs=[whole((stretch, width))] * n_seq + [whole(d_settled.shape), whole(ct.shape), whole(cp.shape), whole(pm.shape), whole(sm.shape), whole(sm2.shape), whole(be.shape), whole(qb.shape)],
            out_specs=[whole_out((stretch, width))] * n_seq + [whole_out((rows, width))],
            scratch_shapes=[pltpu.VMEM((length, width), F32), pltpu.VMEM((length + 2 * EDGE, width), F32),
                            pltpu.VMEM((length + 2 * EDGE, width), F32), pltpu.VMEM((CELLS, width), F32)],
        ),
        cost_estimate=pl.CostEstimate(flops=10_000_000_000, bytes_accessed=8 << 20, transcendentals=0),
        name="encode_back",
    )(info, *blocks, d_settled, ct, cp, pm, sm, sm2, be, qb)


def turn_matrix(width, n, core):
    block, half = width // n, width // 2
    r = jnp.arange(width, dtype=jnp.int32)
    inner = jnp.where(r < half, r, r - half)
    parity = jnp.where(r < half, core, 1 - core)
    source = (2 * (inner // block) + parity) * block + inner % block
    return (source[:, None] == r[None]).astype(BF)


def restack_kernel(info_ref, *refs, n, layout):
    parts, outs = refs[:n], refs[n:]
    for d, part in enumerate(parts):
        source = lax.rem(info_ref[0] - d + n, n)
        for out, pieces in zip(outs, layout):
            at = 0
            for start, width in pieces:
                out[source, :, at : at + width] = part[:, start : start + width].astype(out.dtype)
                at += width


def restack(info, parts, dtype, layout=None):
    n = len(parts)
    rows, cols = parts[0].shape
    layout = layout or [[(0, cols)]]
    outs = pl.pallas_call(
        functools.partial(restack_kernel, n=n, layout=layout),
        out_shape=[jax.ShapeDtypeStruct((n, rows, sum(w for _, w in pieces)), dtype) for pieces in layout],
        in_specs=[pl.BlockSpec(memory_space=pltpu.SMEM)] + [pl.BlockSpec(memory_space=pltpu.VMEM)] * n,
        out_specs=[pl.BlockSpec(memory_space=pltpu.VMEM)] * len(layout),
        cost_estimate=pl.CostEstimate(flops=1000, bytes_accessed=1000, transcendentals=0),
        name="restack",
    )(info, *parts)
    return outs


def unpack_kernel(small_ref, *outs, heads, tiles):
    gct, gcp, qb, vb, ob, order, horiz, vert, ng, ns, be, rb, fg, fs = outs
    for row, out in ((0, fg), (1, fs), (2, rb), (3, ng), (4, ns), (5, ob), (6, qb), (7, vb)):
        out[...] = small_ref[row, :]
    width = small_ref.shape[1]
    for t in range(tiles):
        be[t * width : (t + 1) * width] = small_ref[8 + t, :]
    taps, cells, bias = 8 + tiles, 15 + tiles, 24 + tiles
    for s in range(3):
        for t in range(3):
            gct[s, t, :] = small_ref[taps + 3 + (t - 1) * (s + 1), :]
            gcp[s, t, :] = small_ref[cells + 3 * s + t, :]
    nb = order.shape[1]
    per = width // 128
    for h in range(heads):
        row, at = bias + h // per, 128 * (h % per)
        for n, out in enumerate((order, horiz, vert)):
            out[h, :] = small_ref[row, at + n * nb : at + (n + 1) * nb]


def unpack(small, heads, nb, ff):
    width = small.shape[1]
    sds = lambda *shape: jax.ShapeDtypeStruct(shape, F32)
    vec = sds(width)
    return pl.pallas_call(
        functools.partial(unpack_kernel, heads=heads, tiles=ff // width),
        out_shape=(sds(3, 3, width), sds(3, 3, width), vec, vec, vec, sds(heads, nb), sds(heads, nb), sds(heads, nb),
                   vec, vec, sds(ff), vec, vec, vec),
        cost_estimate=pl.CostEstimate(flops=1000, bytes_accessed=1000, transcendentals=0),
        name="unpack",
    )(small)


def one_hot_rows(ids, size):
    return (ids.reshape(1, -1) == jnp.arange(size, dtype=jnp.int32)[:, None]).astype(F32)


def tables(rel_order, rel_horiz, rel_vert):
    heads, nb = rel_order.shape
    high = lax.Precision.HIGHEST
    a = jnp.arange(BOX, dtype=jnp.int32)
    cell = one_hot_rows(jnp.clip(a[None, :] - a[:, None], -SPAN, SPAN) + SPAN, nb)

    def split(table):
        x = jnp.dot(table, cell, precision=high).reshape(heads, BOX, BOX)
        top = lax.reduce_precision(x, 8, 7)
        return top, x - top

    (hh, hl), (vh, vl) = split(rel_horiz), split(rel_vert)
    zero = jnp.zeros_like(hh)
    wt = jnp.concatenate([jnp.concatenate([hh, zero, hl, zero], 2), jnp.concatenate([zero, vh, zero, vl], 2)], 1).astype(BF)
    i = jnp.arange(RT, dtype=jnp.int32)[:, None]
    j = jnp.arange(128, dtype=jnp.int32)[None]
    band = jnp.stack([jnp.clip(d + j - i, -SPAN, SPAN) + SPAN for d in OFFSETS])
    od = jnp.dot(rel_order, one_hot_rows(band, nb), precision=high).reshape(heads, len(OFFSETS), RT, 128)
    edge = jnp.stack([rel_order[:, 0], rel_order[:, -1]], 1)
    return wt, od, edge


def bias_grads(diag, nb):
    heads = diag.shape[0]
    high = lax.Precision.HIGHEST
    at = jnp.arange(256, dtype=jnp.int32)
    step = at - (RT - 1)
    order_bins = jnp.stack([jnp.clip(d + step, -SPAN, SPAN) for d in OFFSETS] + [jnp.where(at < 128, -SPAN, SPAN)]) + SPAN
    order = jnp.dot(diag[:, :5].reshape(heads, -1), one_hot_rows(order_bins, nb).T, precision=high)
    flat = jnp.clip(step, -SPAN, SPAN) + SPAN
    horiz = jnp.dot(diag[:, 5], one_hot_rows(flat, nb).T, precision=high)
    low = jnp.clip(step - BOX, -SPAN, SPAN) + SPAN
    vert = jnp.dot(diag[:, 6], one_hot_rows(low, nb).T, precision=high)
    return order, horiz, vert


def patch_masks():
    g = jnp.arange(CELLS, dtype=jnp.int32)
    i, j = g // GRID, g % GRID
    cols = []
    for n in range(9):
        a, b = i + n // 3 - 1, j + n % 3 - 1
        cols.append((g < GRID * GRID) & (a >= 0) & (a < GRID) & (b >= 0) & (b < GRID))
    return jnp.pad(jnp.stack(cols, 1).astype(F32), ((0, 0), (0, 128 - 9)))


def text_taps(conv_text):
    rows = []
    for d in TAPS:
        if d == 0:
            rows.append(conv_text[0, 1] + conv_text[1, 1] + conv_text[2, 1])
        else:
            rows.append(conv_text[abs(d) - 1, 2 if d > 0 else 0])
    rows.append(jnp.zeros_like(rows[0]))
    return jnp.stack(rows)


def xor_pairs(n, bit):
    return [(i, i ^ bit) for i in range(n)]


def swap(value, axis, bit):
    return lax.ppermute(value, axis, xor_pairs(lax.axis_size(axis), bit))


def spread(blocks, after=None):
    n = lax.axis_size("seq")
    out = [blocks[0]]
    for d in range(1, n):
        out.append(lax.ppermute(blocks[d], "seq", [(i, (i + d) % n) for i in range(n)]))
    return out


def rotated(pages):
    n = lax.axis_size("seq")
    place = lax.axis_index("seq")
    return [lax.dynamic_index_in_dim(pages, lax.rem(place + d, n), 0, keepdims=False) for d in range(n)]


def total(terms):
    out = terms[0].astype(F32)
    for t in terms[1:]:
        out = out + t.astype(F32)
    return out.astype(BF)


class Reduction:
    def __init__(self, keep, send, line=False):
        self.line = line and lax.axis_size("seq") == 4
        n = lax.axis_size("pages")
        self.n = n
        self.page = lax.axis_index("pages")
        self.first = (self.page & 1) == 0
        self.bits = [1 << b for b in range(1, n.bit_length() - 1)]
        self.shape = (n // 2, keep.shape[0] * 2 // n, keep.shape[1])
        self.terms = [keep.reshape(self.shape)]
        self.send, self.at, self.name = send, 0, None

    def blocks(self, depth, other):
        up, down = self.bits[:depth], self.bits[::-1][:depth]
        out = []
        for k in range((self.n // 2) >> depth):
            pair = []
            for closed in (up, down):
                free = [b for b in self.bits if b not in closed]
                index = sum((((k >> i) & 1) * b) for i, b in enumerate(free))
                mine = sum(closed)
                flip = closed[-1] if other and closed else 0
                pair.append((index + ((self.page ^ flip) & mine)) // 2)
            out.append(jnp.where(self.first, *pair))
        return out

    def pick(self, depth, other):
        rows = []
        for k, block in enumerate(self.blocks(depth, other)):
            parts = []
            for t, term in enumerate(self.terms):
                have = max(t - 1, 0)
                if have == 0:
                    place = block
                else:
                    known = self.blocks(have, False)
                    place = sum(jnp.where(known[i] == block, i, 0) for i in range(len(known)))
                parts.append(lax.dynamic_index_in_dim(term, place, 0, keepdims=False))
            rows.append(total(parts))
        return jnp.stack(rows) if len(rows) > 1 else rows[0][None]

    def step(self):
        assert not self.over()
        at, last = self.at, len(self.bits)
        self.at += 1
        n = lax.axis_size("seq")
        ring = lambda d: [(i, (i + d) % n) for i in range(n)]
        place = lax.axis_index("seq")
        if at == 0:
            self.fresh = [swap(self.send, "pages", 1)]
        elif at <= last:
            self.terms.append(self.fresh[0].reshape((-1,) + self.shape[1:]))
            pairs = [(i, i ^ (self.bits[-at] if i & 1 else self.bits[at - 1])) for i in range(self.n)]
            self.fresh = [lax.ppermute(self.pick(at, True), "pages", pairs)]
        elif at == last + 1:
            self.terms.append(self.fresh[0].reshape((-1,) + self.shape[1:]))
            value = self.pick(last, False)[0]
            rows, cols = value.shape
            if self.line:
                self.own = value
                self.fresh = [lax.ppermute(value, "seq", [(0, 1), (3, 2)])]
                return
            quarters = value.reshape(n, rows // n, cols)
            piece = lambda d: lax.dynamic_index_in_dim(quarters, lax.rem(place + d, n), 0, keepdims=False)
            self.own = piece(0)
            self.fresh = [lax.ppermute(piece(d), "seq", ring(d)) for d in range(1, n)]
        else:
            self.own = total([self.own] + self.fresh)
            if self.line:
                self.fresh = [lax.ppermute(self.own, "seq", [(1, 2), (2, 1)] if at == last + 2 else [(1, 0), (2, 3)])]
                return
            self.fresh = [lax.ppermute(self.own, "seq", ring(d)) for d in range(1, n)]

    def over(self):
        return self.at == len(self.bits) + (4 if self.line else 3)

    def result(self, info, layout=None):
        if self.line:
            place = lax.axis_index("seq")
            return [jnp.where((place == 0) | (place == 3), self.fresh[0], self.own).astype(F32)]
        outs = restack(info, [self.own] + self.fresh, F32, layout)
        return [out.reshape(-1, out.shape[-1]) for out in outs]


def tie(value, *reductions):
    value, fresh, held = lax.optimization_barrier(
        (value, tuple(r.fresh for r in reductions), tuple(r.send for r in reductions)))
    for r, f, h in zip(reductions, fresh, held):
        r.fresh, r.send = f, h
    return value


def per_device(
    tokens, cotangent, conv_text, conv_patch, proj_query, bias_query, proj_key, proj_value, bias_value,
    proj_output, bias_output, rel_order, rel_horiz, rel_vert, norm_gain, norm_shift, expand_weight,
    expand_bias, reduce_weight, reduce_bias, final_gain, final_shift, text_count, box_left, box_top,
):
    pages_here, stretch, width = tokens.shape
    n_seq = lax.axis_size("seq")
    n_pages = lax.axis_size("pages")
    assert pages_here == n_seq and n_pages & (n_pages - 1) == 0
    place = lax.axis_index("seq")
    heads, nb = rel_order.shape
    ff = expand_weight.shape[1]
    pick = lambda a: lax.dynamic_index_in_dim(a, place, 0, keepdims=False)
    count, left, top = pick(text_count), pick(box_left), pick(box_top)
    blocks = spread(rotated(tokens))
    core = lax.axis_index("pages") & 1
    info = jnp.stack([place, count, core]).astype(jnp.int32)
    turn = turn_matrix(width, n_pages, core) if width // n_pages % 16 else jnp.zeros((8, 128), BF)
    cells = jnp.arange(BOX, dtype=jnp.int32)
    oh = jnp.concatenate([left[:, None] == cells[None], top[:, None] == cells[None]], 1).astype(BF)
    oht = jnp.concatenate([left[None] == cells[::-1, None], top[None] == cells[::-1, None]], 0).astype(BF)
    wt, od, edge = tables(rel_order, rel_horiz, rel_vert)
    pm, ct = patch_masks(), text_taps(conv_text)
    cp = jnp.pad(conv_patch.reshape(9, width), ((0, 7), (0, 0)))

    cot_out, blocks = lax.optimization_barrier((rotated(cotangent), blocks))
    cots = spread(cot_out)
    settled, et, q, k, v, probs, att = front(
        info, edge, blocks, ct, cp, pm, turn, proj_query, bias_query, proj_key, proj_value, bias_value, oh, wt, od, width // n_pages)
    *mixed, xh, rs, fl, gp, ds, dr, grk, grs, sm = middle(
        info, cots, att, settled, proj_output, bias_output, norm_gain, norm_shift, expand_weight,
        expand_bias, reduce_weight, reduce_bias, final_gain, final_shift, turn, ff // n_pages)
    c_reduce = Reduction(grk, grs)
    c_reduce.step()
    mixed = spread(mixed)
    done = back(info, width // n_pages, 0, 2, dr, ds, reduce_weight, gp, expand_weight, fl, turn)
    done = tie(done, c_reduce)
    c_reduce.step()
    done = back(info, width // n_pages, 2, ff // width - 2, dr, done[3], reduce_weight, gp, expand_weight, fl, turn, done[:3],
                (xh, rs, norm_gain, att, proj_output))
    done, mixed = tie((done, mixed), c_reduce)
    gek, ges, be, df, da, sm2 = done
    c_expand = Reduction(gek, ges)
    heads_of = lambda first, count, da, acc, filled=(): heads_back(
        first, count, probs, q, k, v, da, att, oh, oht, et, proj_query, proj_key, proj_value, acc, filled)
    cuts = (0, heads // 2, heads)
    c_reduce.step()
    c_expand.step()
    done = heads_of(0, cuts[1], da, df)
    done, da = tie((done, da), c_reduce, c_expand)
    for first, last in zip(cuts[1:-1], cuts[2:]):
        c_reduce.step()
        c_expand.step()
        done = heads_of(first, last - first, da, done[4], done[:4])
        done, da = tie((done, da), c_reduce, c_expand)
    gqk, gqs, qb, diag, acc = done
    c_qkv = Reduction(gqk, gqs)
    for r in (c_reduce, c_expand, c_qkv):
        if not r.over():
            r.step()
    *gts, small = encode_back(info, blocks, acc, ct, cp, pm, sm, sm2, be, qb)
    rounds = [("pages", 1 << b) for b in range(n_pages.bit_length() - 1)] + [("seq", 1 << b) for b in range(n_seq.bit_length() - 1)]
    hop = lambda d: lax.ppermute(gts[d], "seq", [(i, (i + d) % n_seq) for i in range(n_seq)])
    work = [c_reduce, c_expand, c_qkv]
    for r, name in zip(work, ("reduce", "expand", "qkv")):
        r.name = name
    bias = jnp.concatenate(bias_grads(diag, nb), 1)
    bias = jnp.pad(bias, ((0, 0), (0, 128 - 3 * nb))).reshape(-1, width)
    hops = {0: (2,), 1: (3,), 2: (1,)}
    turns = [rounds[1:3], rounds[:1] + rounds[3:4], rounds[4:]] if len(rounds) == 5 else [rounds]
    layouts = {
        "reduce": None,
        "expand": [[(0, ff)], [(ff, width)]],
        "qkv": [[(384 * p + 128 * n, 128) for p in range(heads // 2)] for n in range(3)],
    }
    ready = {}
    phase = 0
    while turns or not c_qkv.over():
        gts, small, bias, ready = tie((gts, small, bias, ready), *work)
        if phase == 0:
            small = lax.dynamic_update_slice(small, bias, (24 + ff // width, 0))
            ready["mixed"] = restack(info, mixed, BF)
        for r in work:
            if not r.over():
                r.step()
            elif r.own is not None and r is not c_qkv:
                ready[r.name] = r.result(info, layouts[r.name])
                r.own, r.fresh = None, []
        for d in hops.get(phase, ()):
            gts = [hop(d) if e == d else part for e, part in enumerate(gts)]
        for axis, bit in turns.pop(0) if turns else ():
            small = small + swap(small, axis, bit)
        phase += 1
    (mixed_out,) = ready["mixed"]
    (o_reduce,), (o_expand, o_output) = (
        ready[r.name] if r.name in ready else r.result(info, layouts[r.name]) for r in (c_reduce, c_expand))
    (grad_tokens,) = restack(info, gts, F32)
    smalls = unpack(small, heads, nb, ff)
    (grad_tokens, smalls, o_reduce, o_expand, o_output), c_qkv.fresh = lax.optimization_barrier(
        ((grad_tokens, smalls, o_reduce, o_expand, o_output), c_qkv.fresh))
    o_query, o_key, o_value = c_qkv.result(info, layouts["qkv"])

    (g_conv_text, g_conv_patch, g_qb, g_vb, g_ob, g_order, g_horiz, g_vert, g_ng, g_ns, g_be, g_rb, g_fg, g_fs) = smalls
    return (
        mixed_out, grad_tokens, g_conv_text, g_conv_patch, o_query, g_qb, o_key, o_value, g_vb,
        o_output, g_ob, g_order, g_horiz, g_vert, g_ng, g_ns, o_expand, g_be, o_reduce, g_rb, g_fg, g_fs,
    )


def solution(mesh):
    placed = (
        P("pages", "seq", None),
        P("pages", "seq", None),
        P(),
        P(),
        P(),
        P(),
        P(),
        P(),
        P(),
        P(),
        P(),
        P(),
        P(),
        P(),
        P(),
        P(),
        P(),
        P(),
        P(),
        P(),
        P(),
        P(),
        P("pages"),
        P("pages", None),
        P("pages", None),
    )
    return jax.shard_map(
        per_device,
        mesh=mesh,
        in_specs=placed,
        out_specs=(
            P("pages", "seq", None),
            P("pages", "seq", None),
            P(),
            P(),
            P("pages", None),
            P(),
            P("pages", None),
            P("pages", None),
            P(),
            P("pages", None),
            P(),
            P(),
            P(),
            P(),
            P(),
            P(),
            P("pages", None),
            P(),
            P("pages", None),
            P(),
            P(),
            P(),
        ),
        check_vma=False,
    )
```
